256 devices in a mesh: section: 4 (over x), seq: 16 (over z, y_lo), dp: 4 (over y_hi, core).
Axes of the slice: x: 4, y: 4 (y_hi: 2, y_lo: 2; y = y_hi * 2 + y_lo), z: 8, core: 2. Of those that a mesh axis runs over, the one named last changes fastest.
Arguments:
- main_hidden: bfloat16 [4, 4, 2048, 7168], P('section', 'dp', 'seq'), may hold values from -6 to 6
- embedded: bfloat16 [4, 4, 2048, 7168], P('section', 'dp', 'seq'), may hold values from -6 to 6
- cotangent: bfloat16 [4, 4, 2048, 7168], P('section', 'dp', 'seq'), may hold values from -6 to 6
- slot_token: int32 [4, 4, 2, 96], P('section', 'dp', None, 'seq'), may hold values from 0 to 127, as said below
- slot_count: int32 [4, 4, 2, 16], P('section', 'dp', None, 'seq'), may hold values from 1 to 6, as said below
- route_gate: float32 [4, 4, 2, 96], P('section', 'dp', None, 'seq'), may hold values from 0.2 to 2
- norm_gain: float32 [2, 2, 7168], replicated, may hold values from 0.5 to 1.5
- expert_weight: bfloat16 [2, 3, 7168, 2048], P(None, None, 'seq', 'dp'), may hold values from -0.0625 to 0.0625
Outputs:
- hidden_grad: bfloat16 [4, 4, 2048, 7168], P('section', 'dp', 'seq')
- expert_grad: bfloat16 [4, 2, 3, 7168, 2048], P('section', None, None, 'seq', 'dp')
- gain_grad: float32 [4, 2, 2, 7168], P('section', None, None, ('seq', 'dp'))
The draws below stay inside these ranges and needn't reach their ends.
Inputs may be any that keep to these rules, and one draw needn't show every extreme that they name: `slot_token`: the slots of one device and depth name distinct positions of that device's block. `slot_count`: in every micro-batch, sequence and depth some device has all 6 slots live.
All inputs are finite; a program needn't handle non-finite values.
Results may differ from the reference program's by a relative error of at most 0.0077.
Values may be sent and summed in bfloat16 or wider, within the bound.
A program may use at most 128 MiB of HBM per device.

```python
import math
import jax
import jax.numpy as jnp
from jax import lax

D = 7168
H = 2048
TOK_DEV = 128
CAP = 6
DEPTHS = 2
SECTIONS = 4
BATCH = 4
SEQ_SHARDS = 16
LENGTH = 2048
SLOTS = 96


def draw_slot_token(key, part):
    blocks = SECTIONS * BATCH * DEPTHS * SEQ_SHARDS
    keys = jax.random.split(jax.random.fold_in(key, 11), blocks)
    chosen = jax.vmap(lambda single: jax.random.permutation(single, TOK_DEV))(keys)[:, :CAP]
    return chosen.reshape(SECTIONS, BATCH, DEPTHS, SLOTS).astype(jnp.int32)


def draw_slot_count(key, part):
    first, second = jax.random.split(jax.random.fold_in(key, 23))
    counts = jax.random.randint(first, (SECTIONS, BATCH, DEPTHS, SEQ_SHARDS), 1, CAP + 1)
    full = jax.random.randint(second, (SECTIONS, BATCH, DEPTHS, 1), 0, SEQ_SHARDS)
    places = jnp.arange(SEQ_SHARDS, dtype=jnp.int32)
    return jnp.where(places == full, CAP, counts).astype(jnp.int32)


def steps_of(rng, dims, cuts, smallest, top_value):
    def one(axis_at, parts):
        draws = jax.random.uniform(jax.random.fold_in(jax.random.fold_in(rng, 6), axis_at), (parts,), jnp.float32, smallest / len(cuts), top_value / len(cuts))
        return jnp.repeat(jnp.exp(draws), dims[axis_at] // parts).reshape((-1,) + (1,) * (len(dims) - axis_at - 1))

    level = one(*cuts[0])
    for cut in cuts[1:]:
        level = level * one(*cut)
    return level


def bell_draw(stream_key, extent, deviation, most, shards=(), held_as=jnp.bfloat16):
    entries = deviation * jax.random.normal(stream_key, extent, jnp.float32)
    if shards:
        entries = entries * steps_of(stream_key, extent, shards, -0.22, 0.18)
    return jnp.clip(entries, -most, most).astype(held_as)


def setup_inputs(seed: int = 0) -> dict:
    streams_of = jax.random.split(jax.random.key(seed), 9)
    main_hidden = bell_draw(streams_of[0], (SECTIONS, BATCH, LENGTH, D), 1.0, 6.0, ((0, 4), (1, 4), (2, 16)))
    embedded = bell_draw(streams_of[1], (SECTIONS, BATCH, LENGTH, D), 1.0, 6.0, ((0, 4), (1, 4), (2, 16)))
    cotangent = bell_draw(streams_of[2], (SECTIONS, BATCH, LENGTH, D), 1.0, 6.0, ((0, 4), (1, 4), (2, 16)))
    slot_token = draw_slot_token(jax.random.fold_in(streams_of[8], 71), 0)
    slot_count = draw_slot_count(jax.random.fold_in(streams_of[8], 71), 0)
    route_gate = jnp.clip(jnp.exp(math.log(2.0) - 2.3025851 * jax.random.uniform(streams_of[5], (SECTIONS, BATCH, DEPTHS, SLOTS), jnp.float32) ** steps_of(streams_of[5], (SECTIONS, BATCH, DEPTHS, SLOTS), ((0, 4), (1, 4), (3, 16)), -0.2, 0.2)), 0.2, 2.0)
    norm_gain = jnp.clip(1.0 + 0.1 * jax.random.normal(streams_of[6], (DEPTHS, 2, D), jnp.float32), 0.5, 1.5)
    expert_weight = bell_draw(streams_of[7], (DEPTHS, 3, D, H), D ** -0.5, 0.0625, ((2, 16), (3, 4)))
    return dict(main_hidden=main_hidden, embedded=embedded, cotangent=cotangent, slot_token=slot_token, slot_count=slot_count, route_gate=route_gate, norm_gain=norm_gain, expert_weight=expert_weight)


eps_norm = 1e-06

def normed(value):
    wide = value.astype(jnp.float32)
    scale = lax.rsqrt(lax.optimization_barrier(jnp.mean(wide * wide, axis=-1, keepdims=True)) + eps_norm)
    return (wide * scale, scale)

def norm_back(grad, unit, scale):
    inner = lax.optimization_barrier(jnp.mean(grad * unit, axis=-1, keepdims=True))
    return (grad - unit * inner) * scale

def contract_rows(left, right):
    return lax.dot_general(left, right, (((0,), (0,)), ((), ())), preferred_element_type=jnp.float32)

def contract_last(left, right):
    return lax.dot_general(left, right, (((1,), (1,)), ((), ())), preferred_element_type=jnp.float32)

def one_sequence(hidden, embedded, cotangent, slots, counts, gates, norm_gain, expert_weight):
    order = jnp.arange(SLOTS, dtype=jnp.int32)
    padded = jnp.concatenate([embedded, jnp.zeros((DEPTHS, D), jnp.bfloat16)], 0)
    current = hidden
    saved = []
    for depth in range(DEPTHS):
        shifted = padded[depth + 1:depth + 1 + LENGTH]
        unit_h, scale_h = normed(current)
        unit_e, scale_e = normed(shifted)
        mixed = (unit_h * norm_gain[depth, 0] + unit_e * norm_gain[depth, 1]).astype(jnp.bfloat16)
        tokens = (order // CAP * TOK_DEV + slots[depth]).astype(jnp.int32)
        live = order % CAP < counts[depth][order // CAP]
        weight = gates[depth] * live.astype(jnp.float32)
        rows = mixed[tokens] * live[:, None].astype(jnp.bfloat16)
        gate_in = jnp.dot(rows, expert_weight[depth, 0], preferred_element_type=jnp.float32)
        up_in = jnp.dot(rows, expert_weight[depth, 1], preferred_element_type=jnp.float32)
        act = (jax.nn.silu(gate_in) * up_in).astype(jnp.bfloat16)
        result = contract_last(act, expert_weight[depth, 2])
        current = mixed.astype(jnp.float32).at[tokens].add(result * weight[:, None]).astype(jnp.bfloat16)
        saved.append((unit_h, scale_h, unit_e, tokens, live, weight, rows, gate_in, up_in, act))
    grad = cotangent.astype(jnp.float32)
    weight_grads = [None] * DEPTHS
    gain_terms = [None] * DEPTHS
    for depth in reversed(range(DEPTHS)):
        unit_h, scale_h, unit_e, tokens, live, weight, rows, gate_in, up_in, act = saved[depth]
        dout = (grad[tokens] * weight[:, None]).astype(jnp.bfloat16)
        d_act = jnp.dot(dout, expert_weight[depth, 2], preferred_element_type=jnp.float32)
        down_grad = contract_rows(dout, act)
        sig = jax.nn.sigmoid(gate_in)
        d_gate = (d_act * up_in * sig * (1.0 + gate_in * (1.0 - sig))).astype(jnp.bfloat16)
        d_up = (d_act * jax.nn.silu(gate_in)).astype(jnp.bfloat16)
        gate_grad = contract_rows(rows, d_gate)
        up_grad = contract_rows(rows, d_up)
        d_rows = contract_last(d_gate, expert_weight[depth, 0]) + contract_last(d_up, expert_weight[depth, 1])
        d_mixed = grad.at[tokens].add(d_rows * live[:, None].astype(jnp.float32))
        gain_terms[depth] = jnp.stack([lax.optimization_barrier(jnp.sum(d_mixed * unit_h, 0)), lax.optimization_barrier(jnp.sum(d_mixed * unit_e, 0))])
        weight_grads[depth] = jnp.stack([gate_grad, up_grad, down_grad])
        grad = norm_back(d_mixed * norm_gain[depth, 0], unit_h, scale_h)
    return (grad.astype(jnp.bfloat16), jnp.stack(weight_grads), jnp.stack(gain_terms))

def one_section(items, norm_gain, expert_weight):
    hidden, embedded, cotangent, slots, counts, gates = items
    grads = []
    weight_total = jnp.zeros((DEPTHS, 3, D, H), jnp.float32)
    gain_total = jnp.zeros((DEPTHS, 2, D), jnp.float32)
    for batch in range(BATCH):
        grad, weight_grad, gain_grad = one_sequence(hidden[batch], embedded[batch], cotangent[batch], slots[batch], counts[batch], gates[batch], norm_gain, expert_weight)
        grads.append(grad)
        weight_total = weight_total + weight_grad
        gain_total = gain_total + gain_grad
    return (jnp.stack(grads), weight_total.astype(jnp.bfloat16), gain_total)

def reference(main_hidden, embedded, cotangent, slot_token, slot_count, route_gate, norm_gain, expert_weight):
    started = jnp.roll(main_hidden, 1, axis=0)
    grads, expert_grad, gain_grad = lax.map(lambda items: one_section(items, norm_gain, expert_weight), (started, embedded, cotangent, slot_token, slot_count, route_gate))
    hidden_grad = jnp.roll(grads, -1, axis=0)
    return (hidden_grad, expert_grad, gain_grad)
```

```python
import functools

import jax
import jax.numpy as jnp
from jax import lax
from jax.experimental import pallas as pl
from jax.experimental.pallas import tpu as pltpu
from jax.sharding import PartitionSpec as P

eps_norm = 1e-06
MESH = pl.DeviceIdType.MESH
F32 = jnp.float32
BF16 = jnp.bfloat16
PK = 16


def from_behind(value, axis, steps):
    count = lax.axis_size(axis)
    pairs = [(source, (source + steps) % count) for source in range(count)]
    return lax.ppermute(value, axis, pairs)


def from_ahead(array, axis, by):
    size = lax.axis_size(axis)
    pairs = [(i, i - by) for i in range(size) if 0 <= i - by < size]
    return lax.ppermute(array, axis, pairs)


def normed(value):
    wide = value.astype(F32)
    scale = lax.rsqrt(jnp.mean(wide * wide, axis=-1, keepdims=True) + eps_norm)
    return (wide * scale, scale)


def norm_back(grad, unit, scale):
    inner = jnp.mean(grad * unit, axis=-1, keepdims=True)
    return (grad - unit * inner) * scale


def dot_nn(a, b):
    return lax.dot_general(a, b, (((1,), (0,)), ((), ())), preferred_element_type=F32)


def dot_nt(a, b):
    return lax.dot_general(a, b, (((1,), (1,)), ((), ())), preferred_element_type=F32)


def dot_tn(a, b):
    return lax.dot_general(a, b, (((0,), (0,)), ((), ())), preferred_element_type=F32)


class Wires:
    def __init__(self, send, recv):
        self.send, self.recv = send, recv
        self.phases = 0
        self.open = []

    def copy(self, src, dst, ph, slot_s, slot_r, axis, to):
        return pltpu.make_async_remote_copy(
            src_ref=src,
            dst_ref=dst,
            send_sem=self.send.at[ph, slot_s],
            recv_sem=self.recv.at[ph, slot_r],
            device_id={axis: to},
            device_id_type=MESH,
        )

    def start(self, axis, size, me, src_of, dst):
        ph = self.phases
        self.phases += 1

        def body(o, c):
            to = lax.rem(me + o, size)
            self.copy(src_of(to), dst, ph, o, me, axis, to).start()
            return c

        lax.fori_loop(1, size, body, 0)
        self.open.append((ph, axis, size, me, src_of))
        return ph

    def wait(self, ph, axis, size, me, dst_of):
        def body(o, c):
            frm = lax.rem(me + o, size)
            self.copy(dst_of(frm), dst_of(frm), ph, o, frm, axis, frm).wait_recv()
            return c

        lax.fori_loop(1, size, body, 0)

    def drain(self):
        for ph, axis, size, me, src_of in self.open:

            def body(o, c):
                to = lax.rem(me + o, size)
                self.copy(src_of(to), src_of(to), ph, o, me, axis, to).wait_send()
                return c

            lax.fori_loop(1, size, body, 0)


def greet(axes):
    barrier = pltpu.get_barrier_semaphore()
    total = 0
    for axis, size, me in axes:

        def body(o, c):
            to = lax.rem(me + o, size)
            pl.semaphore_signal(barrier, inc=1, device_id={axis: to}, device_id_type=MESH)
            return c

        lax.fori_loop(1, size, body, 0)
        total += size - 1
    pl.semaphore_wait(barrier, total)


def chain_kernel(S, Q, C, D, pk, meta, g2, w, eg, ret, land, mland, rows, xr, do, gu, lg, da, ld,
                 act, dg, op, lo, pv, ss, ssl, od, rb, gsv, send, recv):
    me = lax.axis_index("seq")
    d = lax.axis_index("dp")
    DS, HS = w.shape[2], w.shape[3]
    RW = C * S
    CG = S // Q
    PC = HS // CG
    rg, cg = me // CG, lax.rem(me, CG)
    wires = Wires(send, recv)

    def rowslice(g):
        return pl.ds(pl.multiple_of(g * RW, 32 if RW % 32 == 0 else 8), RW)

    def piece_of(ref):
        def src(to):
            return ref.at[to % CG, :, rowslice(to // CG), :]
        return src

    def seq_start(src_of, dst):
        return wires.start("seq", S, me, src_of, dst)

    def seq_wait(ph, dst_of):
        wires.wait(ph, "seq", S, me, dst_of)

    def dp_start(src_of, dst):
        return wires.start("dp", Q, d, src_of, dst)

    def dp_wait(ph, dst_of):
        wires.wait(ph, "dp", Q, d, dst_of)

    greet((("seq", S, me), ("dp", Q, d)))

    def blk(b):
        return pl.ds(pl.multiple_of(b * PK, PK), PK)

    ph_b = seq_start(lambda to: pk.at[0, to], land.at[0, blk(me), :])
    ph_m = seq_start(lambda to: meta, mland.at[me])
    ph_a = seq_start(lambda to: pk.at[1, to], land.at[1, blk(me), :])
    land[0, blk(me), :] = pk[0, me]
    land[1, blk(me), :] = pk[1, me]
    mland[me] = meta[...]

    def unpack(k):
        r = lax.broadcasted_iota(jnp.int32, (S * PK, S * PK), 0)
        c = lax.broadcasted_iota(jnp.int32, (S * PK, S * PK), 1)
        perm = jnp.where(c == (r % S) * PK + r // S, 1.0, 0.0).astype(BF16)
        rows[k] = dot_nn(perm, land[k])

    def rows_at(k, slot):
        return rows[k, slot * S:(slot + 1) * S, :]

    def gather_dp(k, dst):
        return dp_start(lambda to: dst.at[k, rowslice(d), :], dst.at[k, rowslice(d), :])

    def gather_dp_wait(ph, k, dst):
        dp_wait(ph, lambda frm: dst.at[k, rowslice(frm), :])

    def gate_up(k):
        for half in range(2):
            full = dot_nn(xr[k], w[k, half]).astype(BF16)
            for q in range(CG):
                gu[k, q, half] = full[:, q * PC:(q + 1) * PC]
        ph = seq_start(piece_of(gu.at[k]), lg.at[k, me])
        lg[k, me] = gu[k, cg, :, rowslice(rg), :]
        return ph

    def gate_up_wait(ph, k):
        seq_wait(ph, lambda frm: lg.at[k, frm])
        return add_up(lg.at[k])

    def add_up(ref):
        total = ref[0].astype(F32)
        for b in range(1, ref.shape[0]):
            total = total + ref[b].astype(F32)
        return total

    def dact(k):
        full = dot_nn(do[k], w[k, 2]).astype(BF16)
        for q in range(CG):
            da[k, q, 0] = full[:, q * PC:(q + 1) * PC]
        ph = seq_start(piece_of(da.at[k]), ld.at[k, me])
        ld[k, me] = da[k, cg, :, rowslice(rg), :]
        return ph

    def dact_wait(ph, k):
        seq_wait(ph, lambda frm: ld.at[k, frm])
        return add_up(ld.at[k])[0]

    def spread_piece(ref):
        mine = ref.at[cg, :, rowslice(rg), :]
        return seq_start(lambda to: mine, mine)

    def spread_wait(ph, ref):
        seq_wait(ph, lambda frm: ref.at[lax.rem(frm, CG), :, rowslice(frm // CG), :])

    def reduce_dp(n, full):
        op[n] = full.astype(BF16)
        ph = dp_start(lambda to: op.at[n, rowslice(to), :], lo.at[n, d])
        lo[n, d] = op[n, rowslice(d), :]
        return ph

    def reduce_dp_wait(ph, n):
        dp_wait(ph, lambda frm: lo.at[n, frm])
        return add_up(lo.at[n])

    def drows(k):
        total = None
        for q in range(CG):
            cols = slice(q * PC, (q + 1) * PC)
            part = dot_nt(dg[k, q, 0], w[k, 0, :, cols]) + dot_nt(dg[k, q, 1], w[k, 1, :, cols])
            total = part if total is None else total + part
        return total

    def sums_start(n, cols):
        lane = lax.broadcasted_iota(jnp.int32, (S, 128), 1)
        total = jnp.zeros((S, 128), F32)
        for i, col in enumerate(cols):
            total = total + jnp.where(lane == i, col, 0.0)
        ss[n] = total
        ph = seq_start(lambda to: ss.at[n], ssl.at[n, me])
        ssl[n, me] = total
        return ph

    def sums_wait(ph, n):
        seq_wait(ph, lambda frm: ssl.at[n, frm])
        return add_up(ssl.at[n]) * (1.0 / D)

    def pre_grads(k, d_act):
        gate, up = gsv[k, 0], gsv[k, 1]
        sig = 1.0 / (1.0 + jnp.exp(-gate))
        dg[k, cg, 0, rowslice(rg), :] = (d_act * up * sig * (1.0 + gate * (1.0 - sig))).astype(BF16)
        dg[k, cg, 1, rowslice(rg), :] = (d_act * (gate * sig)).astype(BF16)

    def act_piece(k):
        gate, up = gsv[k, 0], gsv[k, 1]
        act[k, cg, 0, rowslice(rg), :] = (gate / (1.0 + jnp.exp(-gate)) * up).astype(BF16)

    def in_grads(k):
        for half in range(2):
            for q in range(CG):
                eg[k, half, :, q * PC:(q + 1) * PC] = dot_tn(xr[k], dg[k, q, half]).astype(BF16)

    def down_grad(k):
        for q in range(CG):
            eg[k, 2, :, q * PC:(q + 1) * PC] = dot_tn(do[k], act[k, q, 0]).astype(BF16)

    seq_wait(ph_b, lambda frm: land.at[0, blk(frm), :])
    unpack(0)
    xr[0, rowslice(d), :] = rows[0, 0:RW, :].astype(BF16)
    ph_x = gather_dp(0, xr)
    seq_wait(ph_a, lambda frm: land.at[1, blk(frm), :])
    unpack(1)
    do[1, rowslice(d), :] = rows[1, C * S:2 * C * S, :].astype(BF16)
    ph_d2 = gather_dp(1, do)
    gather_dp_wait(ph_x, 0, xr)
    ph = gate_up(0)
    gather_dp_wait(ph_d2, 1, do)
    gsv[0] = gate_up_wait(ph, 0)
    act_piece(0)
    ph = spread_piece(act.at[0])
    spread_wait(ph, act.at[0])
    out = None
    for q in range(CG):
        part = dot_nt(act[0, q, 0], w[0, 2, :, q * PC:(q + 1) * PC])
        out = part if out is None else out + part
    ph = reduce_dp(0, out)
    ph_da2 = dact(1)
    seq_wait(ph_m, lambda frm: mland.at[frm])
    facts = jnp.sum(mland[...], axis=1)

    def fact(k):
        return facts[:, k:k + 1]

    def ov(j, i):
        return fact(16 + j * C + i)

    out = reduce_dp_wait(ph, 0)
    od[0:RW, :] = out.astype(BF16)
    cols = []
    for i in range(C):
        before = rows_at(0, i) + fact(i) * out[i * S:(i + 1) * S]
        before = before.astype(BF16).astype(F32)
        pv[i * S:(i + 1) * S, :] = before
        cols.append(jnp.sum(before * before, axis=1, keepdims=True))
    for j in range(C):
        before = rows_at(0, C + j)
        for i in range(C):
            before = before + (ov(j, i) * fact(i)) * out[i * S:(i + 1) * S]
        before = before.astype(BF16).astype(F32)
        pv[(C + j) * S:(C + j + 1) * S, :] = before
        cols.append(jnp.sum(before * before, axis=1, keepdims=True))
    ph = sums_start(0, cols)
    gain_h, gain_e = g2[0:1, :], g2[1:2, :]
    scale = lax.rsqrt(sums_wait(ph, 0) + eps_norm)

    for j in range(C):
        unit = pv[(C + j) * S:(C + j + 1) * S, :] * scale[:, C + j:C + j + 1]
        mixed = unit * gain_h + (rows_at(1, j) * fact(8 + j)) * gain_e
        od[RW + j * S:RW + (j + 1) * S, :] = mixed.astype(BF16)
    xr[1, rowslice(d), :] = od[RW:2 * RW, :]
    ph = gather_dp(1, xr)
    gather_dp_wait(ph, 1, xr)
    ph = gate_up(1)
    d_act = dact_wait(ph_da2, 1)
    gsv[1] = gate_up_wait(ph, 1)
    pre_grads(1, d_act)
    ph = spread_piece(dg.at[1])
    act_piece(1)
    ph_a2 = spread_piece(act.at[1])
    spread_wait(ph, dg.at[1])
    ph = reduce_dp(1, drows(1))
    in_grads(1)
    back = reduce_dp_wait(ph, 1)
    od[RW:2 * RW, :] = back.astype(BF16)
    cols, keep_u, keep_n = [], [], []
    for i in range(C):
        cot = rows_at(1, 2 * C + i) if i < PK - 2 * C else rows_at(0, 2 * C + i - (PK - 2 * C))
        for j in range(C):
            cot = cot + ov(j, i) * back[j * S:(j + 1) * S]
        u = cot * gain_h
        unit = pv[i * S:(i + 1) * S, :] * scale[:, i:i + 1]
        keep_u.append(u)
        keep_n.append(unit)
        cols.append(jnp.sum(u * unit, axis=1, keepdims=True))
    ph = sums_start(1, cols)

    def send_back(k, lo_row, hi_row):
        r = lax.broadcasted_iota(jnp.int32, (S * PK, hi_row - lo_row), 0)
        c = lax.broadcasted_iota(jnp.int32, (S * PK, hi_row - lo_row), 1)
        perm = jnp.where(c == (r % PK) * S + r // PK, 1.0, 0.0).astype(BF16)
        rb[k] = dot_nn(perm, od[lo_row:hi_row, :]).astype(BF16)
        ph = seq_start(lambda to: rb.at[k, blk(to), :], ret.at[k, me])
        ret[k, me] = rb[k, blk(me), :]
        return ph

    inner = sums_wait(ph, 1)

    for i in range(C):
        back = (keep_u[i] - keep_n[i] * inner[:, i:i + 1]) * scale[:, i:i + 1]
        rows[1, i * S:(i + 1) * S, :] = back * fact(i)
    do[0, rowslice(d), :] = rows[1, 0:RW, :].astype(BF16)
    ph = gather_dp(0, do)
    gather_dp_wait(ph, 0, do)
    ph = dact(0)
    spread_wait(ph_a2, act.at[1])
    down_grad(1)
    down_grad(0)
    d_act = dact_wait(ph, 0)
    pre_grads(0, d_act)
    ph = spread_piece(dg.at[0])
    ph_r0 = send_back(0, 0, 2 * RW)
    spread_wait(ph, dg.at[0])
    ph = reduce_dp(2, drows(0))
    in_grads(0)
    back = reduce_dp_wait(ph, 2)
    od[2 * RW:3 * RW, :] = back.astype(BF16)
    ph_r1 = send_back(1, 2 * RW, 3 * RW)
    seq_wait(ph_r0, lambda frm: ret.at[0, frm])
    seq_wait(ph_r1, lambda frm: ret.at[1, frm])
    wires.drain()


def chain(pk, meta, g2, w, C, D):
    S, Q = lax.axis_size("seq"), lax.axis_size("dp")
    DS, HS = w.shape[2], w.shape[3]
    RW = C * S
    NR = Q * RW
    CG = S // Q
    PC = HS // CG
    vm = pltpu.VMEM
    phases = 24
    return pl.pallas_call(
        functools.partial(chain_kernel, S, Q, C, D),
        out_shape=(
            jax.ShapeDtypeStruct(w.shape, BF16),
            jax.ShapeDtypeStruct((2, S, PK, DS), BF16),
        ),
        in_specs=[pl.BlockSpec(memory_space=vm)] * 4,
        out_specs=(pl.BlockSpec(memory_space=vm),) * 2,
        scratch_shapes=[
            vm((2, S * PK, DS), BF16),
            vm((S, 8, 128), F32),
            vm((2, S * PK, DS), F32),
            vm((2, NR, DS), BF16),
            vm((2, NR, DS), BF16),
            vm((2, CG, 2, NR, PC), BF16),
            vm((2, S, 2, RW, PC), BF16),
            vm((2, CG, 1, NR, PC), BF16),
            vm((2, S, 1, RW, PC), BF16),
            vm((2, CG, 1, NR, PC), BF16),
            vm((2, CG, 2, NR, PC), BF16),
            vm((3, NR, DS), BF16),
            vm((3, Q, RW, DS), BF16),
            vm((2 * RW, DS), F32),
            vm((2, S, 128), F32),
            vm((2, S, S, 128), F32),
            vm((3 * RW, DS), BF16),
            vm((2, S * PK, DS), BF16),
            vm((2, 2, RW, PC), F32),
            pltpu.SemaphoreType.DMA((phases, S)),
            pltpu.SemaphoreType.DMA((phases, S)),
        ],
        compiler_params=pltpu.CompilerParams(
            collective_id=0, has_side_effects=True, vmem_limit_bytes=56 * 1024 * 1024
        ),
        cost_estimate=pl.CostEstimate(flops=4 * 10**9, bytes_accessed=150 * 10**6, transcendentals=10**6),
        name="expert_chain",
    )(pk, meta, g2, w)


def gain_kernel(S, Q, parts, total, land, mine, land2, send, recv):
    me = lax.axis_index("seq")
    d = lax.axis_index("dp")
    wires = Wires(send, recv)
    greet((("seq", S, me), ("dp", Q, d)))
    ph = wires.start("seq", S, me, lambda to: parts.at[to], land.at[me])
    land[me] = parts[me]
    wires.wait(ph, "seq", S, me, lambda frm: land.at[frm])
    value = land[0]
    for b in range(1, S):
        value = value + land[b]
    mine[...] = value
    ph = wires.start("dp", Q, d, lambda to: mine, land2.at[d])
    land2[d] = value
    wires.wait(ph, "dp", Q, d, lambda frm: land2.at[frm])
    value = land2[0]
    for b in range(1, Q):
        value = value + land2[b]
    total[...] = value
    wires.drain()


def gain_sum(parts):
    S, Q = lax.axis_size("seq"), lax.axis_size("dp")
    shape = parts.shape[1:]
    vm = pltpu.VMEM
    return pl.pallas_call(
        functools.partial(gain_kernel, S, Q),
        out_shape=jax.ShapeDtypeStruct(shape, F32),
        in_specs=[pl.BlockSpec(memory_space=vm)],
        out_specs=pl.BlockSpec(memory_space=vm),
        scratch_shapes=[
            vm((S,) + shape, F32),
            vm(shape, F32),
            vm((Q,) + shape, F32),
            pltpu.SemaphoreType.DMA((2, S)),
            pltpu.SemaphoreType.DMA((2, S)),
        ],
        compiler_params=pltpu.CompilerParams(collective_id=1, has_side_effects=True),
        cost_estimate=pl.CostEstimate(flops=10**6, bytes_accessed=30 * 10**6, transcendentals=0),
        name="gain_sum",
    )(parts)


def pick(index, count):
    return (index[:, None] == jnp.arange(count, dtype=jnp.int32)[None, :]).astype(BF16)


def put_rows(tokens, rows, weight, count):
    at = (jnp.arange(count, dtype=jnp.int32)[:, None] == tokens[None, :]).astype(F32)
    at = at * weight[None, :]
    total = None
    for i in range(rows.shape[0]):
        part = at[:, i:i + 1] * rows[i:i + 1]
        total = part if total is None else total + part
    return total


def local(main_hidden, embedded, cotangent, slot_token, slot_count, route_gate, norm_gain, w):
    S = lax.axis_size("seq")
    me = lax.axis_index("seq")
    tokens_here, D = main_hidden.shape[2:]
    C = slot_token.shape[3]
    DS = D // S
    tok = slot_token[0, 0]
    live = (jnp.arange(C, dtype=jnp.int32)[None, :] < slot_count[0, 0]).astype(F32)
    weight = route_gate[0, 0] * live
    own, cot = embedded[0, 0], cotangent[0, 0]
    ahead = from_ahead(own[:2], "seq", 1)

    asked = from_behind(tok, "section", -1).reshape(-1)
    sent = dot_nn(pick(asked, tokens_here), main_hidden[0, 0]).astype(BF16)
    h_rows = from_behind(sent, "section", 1)
    bulk, h_rows = lax.optimization_barrier((main_hidden, h_rows))
    hidden = from_behind(bulk, "section", 1)[0, 0]

    flat = tok.reshape(-1)
    places = jnp.concatenate([flat + 1, tok[1] + 2])
    e_pick = pick(places, tokens_here + 2)
    e_rows = dot_nn(e_pick[:, :tokens_here], own) + dot_nn(e_pick[:, tokens_here:], ahead)
    c_rows = dot_nn(pick(flat, tokens_here), cot)
    unit_h, _ = normed(h_rows)
    unit_e, _ = normed(e_rows[:2 * C])
    mixed = (unit_h * norm_gain[0, 0] + unit_e * norm_gain[0, 1]).astype(BF16)
    e2 = e_rows[2 * C:]
    _, se2 = normed(e2)
    m1 = mixed[:C] * live[0][:, None].astype(BF16)
    e2 = (e2 * live[1][:, None]).astype(BF16)
    dout2 = (c_rows[C:] * weight[1][:, None]).astype(BF16)
    c1 = c_rows[:C].astype(BF16)
    cut = PK - 2 * C
    pad = jnp.zeros((2 * PK - 5 * C, D), BF16)
    pk_b = jnp.concatenate([m1, mixed[C:], c1[cut:], pad], 0)
    pk_a = jnp.concatenate([e2, dout2, c1[:cut]], 0)
    pk = jnp.stack([pk_b, pk_a]).reshape(2, PK, S, DS).transpose(0, 2, 1, 3)
    same = (tok[1][:, None] == tok[0][None, :]).astype(F32) * live[1][:, None] * live[0][None, :]
    facts = jnp.concatenate(
        [weight[0], jnp.zeros((8 - C,), F32), se2[:, 0], jnp.zeros((8 - C,), F32), same.reshape(-1)]
    )
    meta = jnp.zeros((8, 128), F32).at[0, :facts.shape[0]].set(facts)
    g2 = lax.dynamic_slice(norm_gain[1], (0, me * DS), (2, DS))
    g2 = jnp.concatenate([g2, jnp.zeros((6, DS), F32)], 0)

    expert_grad, ret = chain(pk, meta, g2, w, C, D)
    ret = ret.transpose(0, 2, 1, 3).reshape(2, PK, D).astype(F32)
    out1, back2, back1 = ret[0, :C], ret[0, C:2 * C], ret[1, :C]

    padded = jnp.concatenate([own, ahead], 0)
    unit_h1, scale_h1 = normed(hidden)
    unit_e1, _ = normed(padded[1:1 + tokens_here])
    unit_e2, _ = normed(padded[2:2 + tokens_here])
    mixed1 = (unit_h1 * norm_gain[0, 0] + unit_e1 * norm_gain[0, 1]).astype(BF16)
    prev2 = (mixed1.astype(F32) + put_rows(tok[0], out1, weight[0], tokens_here)).astype(BF16)
    unit_h2, scale_h2 = normed(prev2)
    dm2 = cot.astype(F32) + put_rows(tok[1], back2, live[1], tokens_here)
    g2h, g2e = jnp.sum(dm2 * unit_h2, 0), jnp.sum(dm2 * unit_e2, 0)
    grad1 = norm_back(dm2 * norm_gain[1, 0], unit_h2, scale_h2)
    dm1 = grad1 + put_rows(tok[0], back1, live[0], tokens_here)
    g1h, g1e = jnp.sum(dm1 * unit_h1, 0), jnp.sum(dm1 * unit_e1, 0)
    grad0 = norm_back(dm1 * norm_gain[0, 0], unit_h1, scale_h1)
    hidden_grad = from_behind(grad0.astype(BF16)[None, None], "section", -1)

    parts = jnp.stack([g1h, g1e, g2h, g2e]).reshape(4, S, DS).transpose(1, 0, 2)
    parts = jnp.concatenate([parts, jnp.zeros((S, 4, DS), F32)], 1)
    total = gain_sum(parts)
    Q = lax.axis_size("dp")
    wide = DS // Q
    gain_grad = lax.dynamic_slice(total, (0, lax.axis_index("dp") * wide), (4, wide))
    return (hidden_grad, expert_grad[None], gain_grad.reshape(1, 2, 2, wide))


def solution(mesh):
    return jax.shard_map(
        local,
        mesh=mesh,
        in_specs=(
            P("section", "dp", "seq", None),
            P("section", "dp", "seq", None),
            P("section", "dp", "seq", None),
            P("section", "dp", None, "seq"),
            P("section", "dp", None, "seq"),
            P("section", "dp", None, "seq"),
            P(),
            P(None, None, "seq", "dp"),
        ),
        out_specs=(
            P("section", "dp", "seq", None),
            P("section", None, None, "seq", "dp"),
            P("section", None, None, ("seq", "dp")),
        ),
        check_vma=False,
    )
```

```python
import functools

import jax
import jax.numpy as jnp
from jax import lax
from jax.experimental import pallas as pl
from jax.experimental.pallas import tpu as pltpu
from jax.sharding import PartitionSpec as P

eps_norm = 1e-06
MESH = pl.DeviceIdType.MESH
F32 = jnp.float32
BF16 = jnp.bfloat16
PK = 16


def from_behind(value, axis, steps):
    count = lax.axis_size(axis)
    pairs = [(source, (source + steps) % count) for source in range(count)]
    return lax.ppermute(value, axis, pairs)


def from_ahead(array, axis, by):
    size = lax.axis_size(axis)
    pairs = [(i, i - by) for i in range(size) if 0 <= i - by < size]
    return lax.ppermute(array, axis, pairs)


def normed(value):
    wide = value.astype(F32)
    scale = lax.rsqrt(jnp.mean(wide * wide, axis=-1, keepdims=True) + eps_norm)
    return (wide * scale, scale)


def norm_back(grad, unit, scale):
    inner = jnp.mean(grad * unit, axis=-1, keepdims=True)
    return (grad - unit * inner) * scale


def dot_nn(a, b):
    return lax.dot_general(a, b, (((1,), (0,)), ((), ())), preferred_element_type=F32)


def dot_nt(a, b):
    return lax.dot_general(a, b, (((1,), (1,)), ((), ())), preferred_element_type=F32)


def dot_tn(a, b):
    return lax.dot_general(a, b, (((0,), (0,)), ((), ())), preferred_element_type=F32)


class Wires:
    def __init__(self, send, recv):
        self.send, self.recv = send, recv
        self.phases = 0
        self.open = []

    def copy(self, src, dst, ph, slot_s, slot_r, axis, to):
        return pltpu.make_async_remote_copy(
            src_ref=src,
            dst_ref=dst,
            send_sem=self.send.at[ph, slot_s],
            recv_sem=self.recv.at[ph, slot_r],
            device_id={axis: to},
            device_id_type=MESH,
        )

    def start(self, axis, size, me, src_of, dst):
        ph = self.phases
        self.phases += 1

        def body(o, c):
            to = lax.rem(me + o, size)
            self.copy(src_of(to), dst, ph, o, me, axis, to).start()
            return c

        lax.fori_loop(1, size, body, 0)
        self.open.append((ph, axis, size, me, src_of))
        return ph

    def wait(self, ph, axis, size, me, dst_of):
        def body(o, c):
            frm = lax.rem(me + o, size)
            self.copy(dst_of(frm), dst_of(frm), ph, o, frm, axis, frm).wait_recv()
            return c

        lax.fori_loop(1, size, body, 0)

    def drain(self):
        for ph, axis, size, me, src_of in self.open:

            def body(o, c):
                to = lax.rem(me + o, size)
                self.copy(src_of(to), src_of(to), ph, o, me, axis, to).wait_send()
                return c

            lax.fori_loop(1, size, body, 0)


def greet(axes, sections=()):
    barrier = pltpu.get_barrier_semaphore()
    total = 0
    for axis, size, me in axes:

        def body(o, c):
            to = lax.rem(me + o, size)
            pl.semaphore_signal(barrier, inc=1, device_id={axis: to}, device_id_type=MESH)
            return c

        lax.fori_loop(1, size, body, 0)
        total += size - 1
    for to in sections:
        pl.semaphore_signal(barrier, inc=1, device_id={"section": to}, device_id_type=MESH)
        total += 1
    pl.semaphore_wait(barrier, total)


def chain_kernel(S, Q, X, C, D, pk, meta, slots, g2, w, mh, ext, cot, sl, ng, eg, hg, slr, gains,
                 ret, land, mland, rows, xr, do, gu, lg, da, ld, act, dg, op, lo, pv, ss, ssl, od, rb, gsv,
                 hid, hgs, es, mx, dmx, ad, sls, gacc, gsrc, gland, gown, gland2, send, recv, xsend, xrecv):
    me = lax.axis_index("seq")
    d = lax.axis_index("dp")
    sec = lax.axis_index("section")
    after, before_me = lax.rem(sec + 1, X), lax.rem(sec + X - 1, X)
    DS, HS = w.shape[2], w.shape[3]
    RW = C * S
    CG = S // Q
    PC = HS // CG
    rg, cg = me // CG, lax.rem(me, CG)
    wires = Wires(send, recv)

    def rowslice(g):
        return pl.ds(pl.multiple_of(g * RW, 32 if RW % 32 == 0 else 8), RW)

    def piece_of(ref):
        def src(to):
            return ref.at[to % CG, :, rowslice(to // CG), :]
        return src

    def seq_start(src_of, dst):
        return wires.start("seq", S, me, src_of, dst)

    def seq_wait(ph, dst_of):
        wires.wait(ph, "seq", S, me, dst_of)

    def dp_start(src_of, dst):
        return wires.start("dp", Q, d, src_of, dst)

    def dp_wait(ph, dst_of):
        wires.wait(ph, "dp", Q, d, dst_of)

    greet((("seq", S, me), ("dp", Q, d)), (after, before_me))

    NC = mh.shape[0] // PK

    def chunk(c):
        return pl.ds(pl.multiple_of(c * PK, PK), PK)

    def hop(src, dst, slot, to):
        return pltpu.make_async_remote_copy(
            src_ref=src, dst_ref=dst, send_sem=xsend.at[slot], recv_sem=xrecv.at[slot],
            device_id={"section": to}, device_id_type=MESH,
        )

    def hid_copy(c):
        return hop(mh.at[chunk(c), :], hid.at[chunk(c), :], c, after)

    def hg_copy(c):
        return hop(hgs.at[chunk(c), :], hg.at[chunk(c), :], NC + c, before_me)

    def each_chunk(fn, first=0, last=NC):
        def body(c, carry):
            fn(c)
            return carry

        lax.fori_loop(first, last, body, 0)

    each_chunk(lambda c: hid_copy(c).start())

    def blk(b):
        return pl.ds(pl.multiple_of(b * PK, PK), PK)

    ph_b = seq_start(lambda to: pk.at[0, to], land.at[0, blk(me), :])
    ph_m = seq_start(lambda to: meta, mland.at[me])
    ph_a = seq_start(lambda to: pk.at[1, to], land.at[1, blk(me), :])
    land[0, blk(me), :] = pk[0, me]
    land[1, blk(me), :] = pk[1, me]
    mland[me] = meta[...]

    def unpack(k):
        r = lax.broadcasted_iota(jnp.int32, (S * PK, S * PK), 0)
        c = lax.broadcasted_iota(jnp.int32, (S * PK, S * PK), 1)
        perm = jnp.where(c == (r % S) * PK + r // S, 1.0, 0.0).astype(BF16)
        rows[k] = dot_nn(perm, land[k])

    def rows_at(k, slot):
        return rows[k, slot * S:(slot + 1) * S, :]

    def gather_dp(k, dst):
        return dp_start(lambda to: dst.at[k, rowslice(d), :], dst.at[k, rowslice(d), :])

    def gather_dp_wait(ph, k, dst):
        dp_wait(ph, lambda frm: dst.at[k, rowslice(frm), :])

    def gate_up(k):
        for half in range(2):
            full = dot_nn(xr[k], w[k, half]).astype(BF16)
            for q in range(CG):
                gu[k, q, half] = full[:, q * PC:(q + 1) * PC]
        ph = seq_start(piece_of(gu.at[k]), lg.at[k, me])
        lg[k, me] = gu[k, cg, :, rowslice(rg), :]
        return ph

    def gate_up_wait(ph, k):
        seq_wait(ph, lambda frm: lg.at[k, frm])
        return add_up(lg.at[k])

    def add_up(ref):
        total = ref[0].astype(F32)
        for b in range(1, ref.shape[0]):
            total = total + ref[b].astype(F32)
        return total

    def dact(k):
        full = dot_nn(do[k], w[k, 2]).astype(BF16)
        for q in range(CG):
            da[k, q, 0] = full[:, q * PC:(q + 1) * PC]
        ph = seq_start(piece_of(da.at[k]), ld.at[k, me])
        ld[k, me] = da[k, cg, :, rowslice(rg), :]
        return ph

    def dact_wait(ph, k):
        seq_wait(ph, lambda frm: ld.at[k, frm])
        return add_up(ld.at[k])[0]

    def spread_piece(ref):
        mine = ref.at[cg, :, rowslice(rg), :]
        return seq_start(lambda to: mine, mine)

    def spread_wait(ph, ref):
        seq_wait(ph, lambda frm: ref.at[lax.rem(frm, CG), :, rowslice(frm // CG), :])

    def reduce_dp(n, full):
        op[n] = full.astype(BF16)
        ph = dp_start(lambda to: op.at[n, rowslice(to), :], lo.at[n, d])
        lo[n, d] = op[n, rowslice(d), :]
        return ph

    def reduce_dp_wait(ph, n):
        dp_wait(ph, lambda frm: lo.at[n, frm])
        return add_up(lo.at[n])

    def drows(k):
        total = None
        for q in range(CG):
            cols = slice(q * PC, (q + 1) * PC)
            part = dot_nt(dg[k, q, 0], w[k, 0, :, cols]) + dot_nt(dg[k, q, 1], w[k, 1, :, cols])
            total = part if total is None else total + part
        return total

    def sums_start(n, cols):
        lane = lax.broadcasted_iota(jnp.int32, (S, 128), 1)
        total = jnp.zeros((S, 128), F32)
        for i, col in enumerate(cols):
            total = total + jnp.where(lane == i, col, 0.0)
        ss[n] = total
        ph = seq_start(lambda to: ss.at[n], ssl.at[n, me])
        ssl[n, me] = total
        return ph

    def sums_wait(ph, n):
        seq_wait(ph, lambda frm: ssl.at[n, frm])
        return add_up(ssl.at[n]) * (1.0 / D)

    def pre_grads(k, d_act):
        gate, up = gsv[k, 0], gsv[k, 1]
        sig = 1.0 / (1.0 + jnp.exp(-gate))
        dg[k, cg, 0, rowslice(rg), :] = (d_act * up * sig * (1.0 + gate * (1.0 - sig))).astype(BF16)
        dg[k, cg, 1, rowslice(rg), :] = (d_act * (gate * sig)).astype(BF16)

    def act_piece(k):
        gate, up = gsv[k, 0], gsv[k, 1]
        act[k, cg, 0, rowslice(rg), :] = (gate / (1.0 + jnp.exp(-gate)) * up).astype(BF16)

    def in_grads(k):
        for half in range(2):
            for q in range(CG):
                eg[k, half, :, q * PC:(q + 1) * PC] = dot_tn(xr[k], dg[k, q, half]).astype(BF16)

    def down_grad(k):
        for q in range(CG):
            eg[k, 2, :, q * PC:(q + 1) * PC] = dot_tn(do[k], act[k, q, 0]).astype(BF16)

    LB = 256
    NB = D // LB

    def lanes(b):
        return pl.ds(pl.multiple_of(b * LB, LB), LB)

    def sweep(fn, count):
        zero = jnp.zeros((PK, LB), F32)
        total = lax.fori_loop(0, NB, lambda b, acc: fn(lanes(b), acc), (zero,) * count)
        return [jnp.sum(t, axis=1, keepdims=True) * (1.0 / D) for t in total]

    def gain(k, at):
        return ng[k:k + 1, at]

    def collect(k, at, value, mask):
        value = value * mask
        gacc[k, :, at] += value[:8] + value[8:]

    def rows_pass_1(h_at, e_at, c_at, mask, prev_add, dm2_add):
        def squares(at, acc):
            h, e1, e2 = h_at(at), e_at(0, at), e_at(1, at)
            return acc[0] + h * h, acc[1] + e1 * e1, acc[2] + e2 * e2

        sh, se1, se2 = [lax.rsqrt(v + eps_norm) for v in sweep(squares, 3)]

        def mix(at, acc):
            m = (h_at(at) * sh) * gain(0, at) + (e_at(0, at) * se1) * gain(1, at)
            m = m.astype(BF16).astype(F32)
            if prev_add is not None:
                m = (m + prev_add(at)).astype(BF16).astype(F32)
            mx[:, at] = m
            return (acc[0] + m * m,)

        s2, = [lax.rsqrt(v + eps_norm) for v in sweep(mix, 1)]

        def top(at, acc):
            n2 = mx[:, at] * s2
            dm2 = c_at(at)
            if dm2_add is not None:
                dm2 = dm2 + dm2_add(at)
            collect(2, at, dm2 * n2, mask)
            collect(3, at, dm2 * (e_at(1, at) * se2), mask)
            u = dm2 * gain(2, at)
            dmx[:, at] = u
            return (acc[0] + u * n2,)

        inner, = sweep(top, 1)

        def middle(at, acc):
            dmx[:, at] = (dmx[:, at] - (mx[:, at] * s2) * inner) * s2
            return acc

        sweep(middle, 0)
        return sh, se1

    def rows_pass_2(h_at, e_at, mask, sh, se1, dm1_add, store):
        def low(at, acc):
            dm1 = dmx[:, at]
            if dm1_add is not None:
                dm1 = dm1 + dm1_add(at)
            n1 = h_at(at) * sh
            collect(0, at, dm1 * n1, mask)
            collect(1, at, dm1 * (e_at(0, at) * se1), mask)
            u = dm1 * gain(0, at)
            dmx[:, at] = u
            return (acc[0] + u * n1,)

        inner, = sweep(low, 1)

        def last(at, acc):
            store(at, ((dmx[:, at] - (h_at(at) * sh) * inner) * sh).astype(BF16))
            return acc

        sweep(last, 0)

    slot_row, live_row, weight_row, fresh_row = (slots[k:k + 1, :] for k in range(4))
    lane16 = lax.broadcasted_iota(jnp.int32, (PK, 128), 1)
    line16 = lax.broadcasted_iota(jnp.int32, (PK, 128), 0)

    def column(row):
        return jnp.sum(jnp.where(lane16 == line16, row, 0.0), axis=1, keepdims=True)

    def bulk_chunk(c):
        hid_copy(c).wait_recv()
        r = lax.broadcasted_iota(jnp.int32, (2 * PK, 2 * PK), 0)
        k = lax.broadcasted_iota(jnp.int32, (2 * PK, 2 * PK), 1)
        shift = jnp.where(k == r % PK + 1 + r // PK, 1.0, 0.0).astype(BF16)
        es[...] = dot_nn(shift, ext[pl.ds(pl.multiple_of(c * PK, PK), 2 * PK), :]).astype(BF16)
        place = (line16 + c * PK).astype(F32)
        hit = jnp.sum(jnp.where(place == slot_row, live_row, 0.0), axis=1, keepdims=True)
        mask = jnp.where(hit > 0.5, 0.0, 1.0)

        def h_at(at):
            return hid[chunk(c), at].astype(F32)

        def e_at(k, at):
            return es[k * PK:(k + 1) * PK, at].astype(F32)

        sh, se1 = rows_pass_1(h_at, e_at, lambda at: cot[chunk(c), at].astype(F32), mask, None, None)

        def store(at, value):
            hgs[chunk(c), at] = value

        rows_pass_2(h_at, e_at, mask, sh, se1, None, store)
        hg_copy(c).start()

    def bulk(first, last):
        each_chunk(bulk_chunk, first, last)

    gacc[...] = jnp.zeros_like(gacc)

    def slot_h(at):
        return sl[0, :, at].astype(F32)

    def slot_e(k, at):
        return sl[1 + k, :, at].astype(F32)

    slot_mask = column(fresh_row)
    slot_tok = column(slot_row)
    same_tok = jnp.where(slot_tok == slot_row, live_row, 0.0)
    prev_sel = jnp.where(lane16 < C, same_tok, 0.0)
    prev_w = jnp.sum(prev_sel * weight_row, axis=1, keepdims=True)
    dm2_sel = jnp.where((lane16 >= C) & (lane16 < 2 * C), same_tok, 0.0)

    def widen(n, sel, k, scale_by):
        for b in range(S):
            part = dot_nn(sel[:, :PK].astype(BF16), ret[k, b])
            if scale_by is not None:
                part = part * scale_by
            ad[n, :, b * DS:(b + 1) * DS] = part

    seq_wait(ph_b, lambda frm: land.at[0, blk(frm), :])
    unpack(0)
    xr[0, rowslice(d), :] = rows[0, 0:RW, :].astype(BF16)
    ph_x = gather_dp(0, xr)
    seq_wait(ph_a, lambda frm: land.at[1, blk(frm), :])
    unpack(1)
    do[1, rowslice(d), :] = rows[1, C * S:2 * C * S, :].astype(BF16)
    ph_d2 = gather_dp(1, do)
    gather_dp_wait(ph_x, 0, xr)
    ph = gate_up(0)
    gather_dp_wait(ph_d2, 1, do)
    gsv[0] = gate_up_wait(ph, 0)
    act_piece(0)
    ph = spread_piece(act.at[0])
    bulk(0, 3 * NC // 8)
    spread_wait(ph, act.at[0])
    out = None
    for q in range(CG):
        part = dot_nt(act[0, q, 0], w[0, 2, :, q * PC:(q + 1) * PC])
        out = part if out is None else out + part
    ph = reduce_dp(0, out)
    ph_da2 = dact(1)
    bulk(3 * NC // 8, NC // 2)
    seq_wait(ph_m, lambda frm: mland.at[frm])
    facts = jnp.sum(mland[...], axis=1)

    def fact(k):
        return facts[:, k:k + 1]

    def ov(j, i):
        return fact(16 + j * C + i)

    out = reduce_dp_wait(ph, 0)
    od[0:RW, :] = out.astype(BF16)
    cols = []
    for i in range(C):
        before = rows_at(0, i) + fact(i) * out[i * S:(i + 1) * S]
        before = before.astype(BF16).astype(F32)
        pv[i * S:(i + 1) * S, :] = before
        cols.append(jnp.sum(before * before, axis=1, keepdims=True))
    for j in range(C):
        before = rows_at(0, C + j)
        for i in range(C):
            before = before + (ov(j, i) * fact(i)) * out[i * S:(i + 1) * S]
        before = before.astype(BF16).astype(F32)
        pv[(C + j) * S:(C + j + 1) * S, :] = before
        cols.append(jnp.sum(before * before, axis=1, keepdims=True))
    ph = sums_start(0, cols)
    gain_h, gain_e = g2[0:1, :], g2[1:2, :]
    scale = lax.rsqrt(sums_wait(ph, 0) + eps_norm)

    for j in range(C):
        unit = pv[(C + j) * S:(C + j + 1) * S, :] * scale[:, C + j:C + j + 1]
        mixed = unit * gain_h + (rows_at(1, j) * fact(8 + j)) * gain_e
        od[RW + j * S:RW + (j + 1) * S, :] = mixed.astype(BF16)
    xr[1, rowslice(d), :] = od[RW:2 * RW, :]
    ph = gather_dp(1, xr)
    gather_dp_wait(ph, 1, xr)
    ph = gate_up(1)
    bulk(NC // 2, NC)
    d_act = dact_wait(ph_da2, 1)
    gsv[1] = gate_up_wait(ph, 1)
    pre_grads(1, d_act)
    ph = spread_piece(dg.at[1])
    act_piece(1)
    ph_a2 = spread_piece(act.at[1])
    spread_wait(ph, dg.at[1])
    ph = reduce_dp(1, drows(1))
    in_grads(1)
    back = reduce_dp_wait(ph, 1)
    od[RW:2 * RW, :] = back.astype(BF16)
    cols, keep_u, keep_n = [], [], []
    for i in range(C):
        cot = rows_at(1, 2 * C + i) if i < PK - 2 * C else rows_at(0, 2 * C + i - (PK - 2 * C))
        for j in range(C):
            cot = cot + ov(j, i) * back[j * S:(j + 1) * S]
        u = cot * gain_h
        unit = pv[i * S:(i + 1) * S, :] * scale[:, i:i + 1]
        keep_u.append(u)
        keep_n.append(unit)
        cols.append(jnp.sum(u * unit, axis=1, keepdims=True))
    ph = sums_start(1, cols)

    def send_back(k, lo_row, hi_row):
        r = lax.broadcasted_iota(jnp.int32, (S * PK, hi_row - lo_row), 0)
        c = lax.broadcasted_iota(jnp.int32, (S * PK, hi_row - lo_row), 1)
        perm = jnp.where(c == (r % PK) * S + r // PK, 1.0, 0.0).astype(BF16)
        rb[k] = dot_nn(perm, od[lo_row:hi_row, :]).astype(BF16)
        ph = seq_start(lambda to: rb.at[k, blk(to), :], ret.at[k, me])
        ret[k, me] = rb[k, blk(me), :]
        return ph

    inner = sums_wait(ph, 1)

    for i in range(C):
        back = (keep_u[i] - keep_n[i] * inner[:, i:i + 1]) * scale[:, i:i + 1]
        rows[1, i * S:(i + 1) * S, :] = back * fact(i)
    do[0, rowslice(d), :] = rows[1, 0:RW, :].astype(BF16)
    ph = gather_dp(0, do)
    gather_dp_wait(ph, 0, do)
    ph = dact(0)
    spread_wait(ph_a2, act.at[1])
    down_grad(1)
    down_grad(0)
    d_act = dact_wait(ph, 0)
    pre_grads(0, d_act)
    ph = spread_piece(dg.at[0])
    ph_r0 = send_back(0, 0, 2 * RW)
    seq_wait(ph_r0, lambda frm: ret.at[0, frm])
    widen(0, prev_sel, 0, prev_w)
    widen(1, dm2_sel, 0, None)
    slot_sh, slot_se1 = rows_pass_1(
        slot_h, slot_e, lambda at: sl[3, :, at].astype(F32), slot_mask, lambda at: ad[0, :, at], lambda at: ad[1, :, at]
    )
    spread_wait(ph, dg.at[0])
    ph = reduce_dp(2, drows(0))
    in_grads(0)
    back = reduce_dp_wait(ph, 2)
    od[2 * RW:3 * RW, :] = back.astype(BF16)
    ph_r1 = send_back(1, 2 * RW, 3 * RW)
    seq_wait(ph_r1, lambda frm: ret.at[1, frm])
    widen(2, prev_sel, 1, None)

    def slot_store(at, value):
        sls[:, at] = value

    rows_pass_2(slot_h, slot_e, slot_mask, slot_sh, slot_se1, lambda at: ad[2, :, at], slot_store)
    back_rows = hop(sls, slr, 2 * NC, before_me)
    back_rows.start()

    for b in range(S):
        part = gacc[:, :, b * DS:(b + 1) * DS]
        gsrc[b] = jnp.sum(part, axis=1)
    ph = seq_start(lambda to: gsrc.at[to], gland.at[me])
    gland[me] = gsrc[me]
    seq_wait(ph, lambda frm: gland.at[frm])
    value = add_up(gland)
    gown[...] = value
    ph = dp_start(lambda to: gown, gland2.at[d])
    gland2[d] = value
    dp_wait(ph, lambda frm: gland2.at[frm])
    gains[...] = add_up(gland2)

    def finish(c):
        hid_copy(c).wait_send()
        hg_copy(c).wait_send()
        hg_copy(c).wait_recv()

    each_chunk(finish)
    back_rows.wait()
    wires.drain()


def chain(pk, meta, slots, g2, w, mh, ext, cot, sl, ng, C):
    S, Q, X = lax.axis_size("seq"), lax.axis_size("dp"), lax.axis_size("section")
    DS, HS = w.shape[2], w.shape[3]
    T, D = mh.shape
    RW = C * S
    NR = Q * RW
    CG = S // Q
    PC = HS // CG
    NC = T // PK
    vm = pltpu.VMEM
    phases = 24
    return pl.pallas_call(
        functools.partial(chain_kernel, S, Q, X, C, D),
        out_shape=(
            jax.ShapeDtypeStruct(w.shape, BF16),
            jax.ShapeDtypeStruct((T, D), BF16),
            jax.ShapeDtypeStruct((PK, D), BF16),
            jax.ShapeDtypeStruct((4, DS), F32),
        ),
        in_specs=[pl.BlockSpec(memory_space=vm)] * 10,
        out_specs=(pl.BlockSpec(memory_space=vm),) * 4,
        scratch_shapes=[
            vm((2, S, PK, DS), BF16),
            vm((2, S * PK, DS), BF16),
            vm((S, 8, 128), F32),
            vm((2, S * PK, DS), F32),
            vm((2, NR, DS), BF16),
            vm((2, NR, DS), BF16),
            vm((2, CG, 2, NR, PC), BF16),
            vm((2, S, 2, RW, PC), BF16),
            vm((2, CG, 1, NR, PC), BF16),
            vm((2, S, 1, RW, PC), BF16),
            vm((2, CG, 1, NR, PC), BF16),
            vm((2, CG, 2, NR, PC), BF16),
            vm((3, NR, DS), BF16),
            vm((3, Q, RW, DS), BF16),
            vm((2 * RW, DS), F32),
            vm((2, S, 128), F32),
            vm((2, S, S, 128), F32),
            vm((3 * RW, DS), BF16),
            vm((2, S * PK, DS), BF16),
            vm((2, 2, RW, PC), F32),
            vm((T, D), BF16),
            vm((T, D), BF16),
            vm((2 * PK, D), BF16),
            vm((PK, D), F32),
            vm((PK, D), F32),
            vm((3, PK, D), F32),
            vm((PK, D), BF16),
            vm((4, 8, D), F32),
            vm((S, 4, DS), F32),
            vm((S, 4, DS), F32),
            vm((4, DS), F32),
            vm((Q, 4, DS), F32),
            pltpu.SemaphoreType.DMA((phases, S)),
            pltpu.SemaphoreType.DMA((phases, S)),
            pltpu.SemaphoreType.DMA((2 * NC + 1,)),
            pltpu.SemaphoreType.DMA((2 * NC + 1,)),
        ],
        compiler_params=pltpu.CompilerParams(
            collective_id=0, has_side_effects=True, vmem_limit_bytes=60 * 1024 * 1024
        ),
        name="expert_chain",
    )(pk, meta, slots, g2, w, mh, ext, cot, sl, ng)


def pick(index, count):
    return (index[:, None] == jnp.arange(count, dtype=jnp.int32)[None, :]).astype(BF16)


def local(main_hidden, embedded, cotangent, slot_token, slot_count, route_gate, norm_gain, w):
    S = lax.axis_size("seq")
    me = lax.axis_index("seq")
    tokens_here, D = main_hidden.shape[2:]
    C = slot_token.shape[3]
    DS = D // S
    tok = slot_token[0, 0]
    live = (jnp.arange(C, dtype=jnp.int32)[None, :] < slot_count[0, 0]).astype(F32)
    weight = route_gate[0, 0] * live
    own, cot, mh = embedded[0, 0], cotangent[0, 0], main_hidden[0, 0]
    ahead = from_ahead(own[:2], "seq", 1)
    same = (tok[1][:, None] == tok[0][None, :]).astype(F32) * live[1][:, None] * live[0][None, :]
    fresh = jnp.stack([live[0], live[1] * (1.0 - jnp.max(same, axis=1))]).reshape(-1)
    flat = tok.reshape(-1)
    merge = jnp.where(fresh > 0.5, flat, -1)

    asked, back_to = from_behind(jnp.stack([flat, merge]), "section", -1)
    sent = dot_nn(pick(asked, tokens_here), mh).astype(BF16)
    h_rows = from_behind(sent, "section", 1)

    places = jnp.concatenate([flat + 1, flat + 2])
    e_pick = pick(places, tokens_here + 2)
    e_rows = dot_nn(e_pick[:, :tokens_here], own) + dot_nn(e_pick[:, tokens_here:], ahead)
    c_rows = dot_nn(pick(flat, tokens_here), cot)
    unit_h, _ = normed(h_rows)
    unit_e, _ = normed(e_rows[:2 * C])
    mixed = (unit_h * norm_gain[0, 0] + unit_e * norm_gain[0, 1]).astype(BF16)
    e2 = e_rows[3 * C:]
    _, se2 = normed(e2)
    m1 = mixed[:C] * live[0][:, None].astype(BF16)
    e2 = (e2 * live[1][:, None]).astype(BF16)
    dout2 = (c_rows[C:] * weight[1][:, None]).astype(BF16)
    c1 = c_rows[:C].astype(BF16)
    cut = PK - 2 * C
    pad = jnp.zeros((2 * PK - 5 * C, D), BF16)
    pk_b = jnp.concatenate([m1, mixed[C:], c1[cut:], pad], 0)
    pk_a = jnp.concatenate([e2, dout2, c1[:cut]], 0)
    pk = jnp.stack([pk_b, pk_a]).reshape(2, PK, S, DS).transpose(0, 2, 1, 3)
    facts = jnp.concatenate(
        [weight[0], jnp.zeros((8 - C,), F32), se2[:, 0], jnp.zeros((8 - C,), F32), same.reshape(-1)]
    )
    meta = jnp.pad(facts[None, :], ((0, 7), (0, 128 - facts.shape[0])))
    slots = jnp.stack([flat.astype(F32), live.reshape(-1), weight.reshape(-1), fresh])
    slots = jnp.pad(slots, ((0, 4), (0, 128 - 2 * C)))
    g2 = lax.dynamic_slice(norm_gain[1], (0, me * DS), (2, DS))
    g2 = jnp.concatenate([g2, jnp.zeros((6, DS), F32)], 0)
    ng = jnp.concatenate([norm_gain.reshape(4, D), jnp.zeros((4, D), F32)], 0)
    ext = jnp.concatenate([own, ahead, jnp.zeros((PK - 2, D), BF16)], 0)
    sl = jnp.stack([h_rows, e_rows[:2 * C].astype(BF16), e_rows[2 * C:].astype(BF16), c_rows.astype(BF16)])
    sl = jnp.pad(sl, ((0, 0), (0, PK - 2 * C), (0, 0)))

    expert_grad, grads, slot_grads, total = chain(pk, meta, slots, g2, w, mh, ext, cot, sl, ng, C)
    put = pick(back_to, tokens_here)
    hit = jnp.sum(put.astype(F32), axis=0)
    placed = lax.dot_general(
        put, slot_grads[:2 * C], (((0,), (0,)), ((), ())), preferred_element_type=F32
    )
    hidden_grad = jnp.where(hit[:, None] > 0.5, placed.astype(BF16), grads)
    Q = lax.axis_size("dp")
    wide = DS // Q
    gain_grad = lax.dynamic_slice(total, (0, lax.axis_index("dp") * wide), (4, wide))
    return (hidden_grad[None, None], expert_grad[None], gain_grad.reshape(1, 2, 2, wide))


def solution(mesh):
    return jax.shard_map(
        local,
        mesh=mesh,
        in_specs=(
            P("section", "dp", "seq", None),
            P("section", "dp", "seq", None),
            P("section", "dp", "seq", None),
            P("section", "dp", None, "seq"),
            P("section", "dp", None, "seq"),
            P("section", "dp", None, "seq"),
            P(),
            P(None, None, "seq", "dp"),
        ),
        out_specs=(
            P("section", "dp", "seq", None),
            P("section", None, None, "seq", "dp"),
            P("section", None, None, ("seq", "dp")),
        ),
        check_vma=False,
    )
```

```python
import functools

import jax
import jax.numpy as jnp
from jax import lax
from jax.experimental import pallas as pl
from jax.experimental.pallas import tpu as pltpu
from jax.sharding import PartitionSpec as P

eps_norm = 1e-06
MESH = pl.DeviceIdType.MESH
F32 = jnp.float32
BF16 = jnp.bfloat16
PK = 16


def from_behind(value, axis, steps):
    count = lax.axis_size(axis)
    pairs = [(source, (source + steps) % count) for source in range(count)]
    return lax.ppermute(value, axis, pairs)


def from_ahead(array, axis, by):
    size = lax.axis_size(axis)
    pairs = [(i, i - by) for i in range(size) if 0 <= i - by < size]
    return lax.ppermute(array, axis, pairs)


def normed(value):
    wide = value.astype(F32)
    scale = lax.rsqrt(jnp.mean(wide * wide, axis=-1, keepdims=True) + eps_norm)
    return (wide * scale, scale)


def norm_back(grad, unit, scale):
    inner = jnp.mean(grad * unit, axis=-1, keepdims=True)
    return (grad - unit * inner) * scale


def dot_nn(a, b):
    return lax.dot_general(a, b, (((1,), (0,)), ((), ())), preferred_element_type=F32)


def dot_nt(a, b):
    return lax.dot_general(a, b, (((1,), (1,)), ((), ())), preferred_element_type=F32)


def dot_tn(a, b):
    return lax.dot_general(a, b, (((0,), (0,)), ((), ())), preferred_element_type=F32)


class Wires:
    def __init__(self, send, recv):
        self.send, self.recv = send, recv
        self.phases = 0
        self.open = []

    def copy(self, src, dst, ph, slot_s, slot_r, axis, to):
        return pltpu.make_async_remote_copy(
            src_ref=src,
            dst_ref=dst,
            send_sem=self.send.at[ph, slot_s],
            recv_sem=self.recv.at[ph, slot_r],
            device_id={axis: to},
            device_id_type=MESH,
        )

    def start(self, axis, size, me, src_of, dst):
        ph = self.phases
        self.phases += 1

        def body(o, c):
            to = lax.rem(me + o, size)
            self.copy(src_of(to), dst, ph, o, me, axis, to).start()
            return c

        lax.fori_loop(1, size, body, 0)
        self.open.append((ph, axis, size, me, src_of))
        return ph

    def wait(self, ph, axis, size, me, dst_of):
        def body(o, c):
            frm = lax.rem(me + o, size)
            self.copy(dst_of(frm), dst_of(frm), ph, o, frm, axis, frm).wait_recv()
            return c

        lax.fori_loop(1, size, body, 0)

    def drain(self):
        for ph, axis, size, me, src_of in self.open:

            def body(o, c):
                to = lax.rem(me + o, size)
                self.copy(src_of(to), src_of(to), ph, o, me, axis, to).wait_send()
                return c

            lax.fori_loop(1, size, body, 0)


def greet(axes, sections=()):
    barrier = pltpu.get_barrier_semaphore()
    total = 0
    for axis, size, me in axes:

        def body(o, c):
            to = lax.rem(me + o, size)
            pl.semaphore_signal(barrier, inc=1, device_id={axis: to}, device_id_type=MESH)
            return c

        lax.fori_loop(1, size, body, 0)
        total += size - 1
    for to in sections:
        pl.semaphore_signal(barrier, inc=1, device_id={"section": to}, device_id_type=MESH)
        total += 1
    return lambda: pl.semaphore_wait(barrier, total)


def chain_kernel(S, Q, X, C, D, slots, g2, w, mh, own, ahead, cot, ng, eg, hg, slr, gains, asks,
                 ext, hsend, hrow, se, sc, pka, pkb, landa, landb, meta, mland, rows, ret, rb, xr, do, gu, lg, da,
                 ld, act, dg, op, lo, pv, ss, ssl, od, gsv, hid, hgs, es, mx, dmx, ad, sls, gacc, gsrc, gland,
                 gown, gland2, send, recv, xsend, xrecv):
    me = lax.axis_index("seq")
    d = lax.axis_index("dp")
    sec = lax.axis_index("section")
    after, before_me = lax.rem(sec + 1, X), lax.rem(sec + X - 1, X)
    DS, HS = w.shape[2], w.shape[3]
    RW = C * S
    CG = S // Q
    PC = HS // CG
    rg, cg = me // CG, lax.rem(me, CG)
    wires = Wires(send, recv)

    def rowslice(g):
        return pl.ds(pl.multiple_of(g * RW, 32 if RW % 32 == 0 else 8), RW)

    def piece_of(ref):
        def src(to):
            return ref.at[to % CG, :, rowslice(to // CG), :]
        return src

    def seq_start(src_of, dst):
        return wires.start("seq", S, me, src_of, dst)

    def seq_wait(ph, dst_of):
        wires.wait(ph, "seq", S, me, dst_of)

    def dp_start(src_of, dst):
        return wires.start("dp", Q, d, src_of, dst)

    def dp_wait(ph, dst_of):
        wires.wait(ph, "dp", Q, d, dst_of)

    barrier_axes = (("seq", S, me), ("dp", Q, d))
    greet_all = greet(barrier_axes, (after, before_me))
    NC = mh.shape[0] // PK
    T = mh.shape[0]

    def chunk(c):
        return pl.ds(pl.multiple_of(c * PK, PK), PK)

    def hop(src, dst, slot, to):
        return pltpu.make_async_remote_copy(
            src_ref=src, dst_ref=dst, send_sem=xsend.at[slot], recv_sem=xrecv.at[slot],
            device_id={"section": to}, device_id_type=MESH,
        )

    def hid_copy(c):
        return hop(mh.at[chunk(c), :], hid.at[chunk(c), :], c, after)

    def hg_copy(c):
        return hop(hgs.at[chunk(c), :], hg.at[chunk(c), :], NC + c, before_me)

    ask_hop = hop(slots, asks, 2 * NC + 1, before_me)
    row_hop = hop(hsend, hrow, 2 * NC + 2, after)

    def each_chunk(fn, first=0, last=NC):
        def body(c, carry):
            fn(c)
            return carry

        lax.fori_loop(first, last, body, 0)

    slot_row, live_row, weight_row, fresh_row = (slots[k:k + 1, :] for k in range(4))
    lane16 = lax.broadcasted_iota(jnp.int32, (PK, 128), 1)
    line16 = lax.broadcasted_iota(jnp.int32, (PK, 128), 0)
    line1 = lax.broadcasted_iota(jnp.int32, (PK, 1), 0)

    def column(row):
        return jnp.sum(jnp.where(lane16 == line16, row, 0.0), axis=1, keepdims=True)

    def line(col, first):
        return jnp.sum(jnp.where((lane16 == line16 + first) & (line16 < C), col, 0.0), axis=0, keepdims=True)

    slot_tok, slot_live, slot_w = column(slot_row), column(live_row), column(weight_row)

    ext[0:T, :] = own[...]
    ext[T:T + PK, :] = ahead[...]
    wide = lax.broadcasted_iota(jnp.int32, (PK, T + PK), 1).astype(F32)
    for k in range(2):
        se[k] = dot_nn(jnp.where(wide == slot_tok + (k + 1.0), 1.0, 0.0).astype(BF16), ext[...]).astype(BF16)
    sc[...] = dot_nn(jnp.where(lane16.astype(F32) == slot_tok, 1.0, 0.0).astype(BF16), cot[...]).astype(BF16)

    greet_all()
    ask_hop.start()

    first_rows = line1 < C

    def dslice(b):
        return slice(b * DS, (b + 1) * DS)

    cot_w = jnp.where(first_rows, 1.0, slot_w)
    for b in range(S):
        pka[0, b] = (sc[:, dslice(b)].astype(F32) * cot_w).astype(BF16)
    ph_a = seq_start(lambda to: pka.at[0, to], landa.at[0, me])
    landa[0, me] = pka[0, me]
    e_live = jnp.where(first_rows, 1.0, slot_live)
    for b in range(S):
        both = jnp.where(first_rows, se[0, :, dslice(b)].astype(F32), se[1, :, dslice(b)].astype(F32))
        pka[1, b] = (both * e_live).astype(BF16)

    ask_hop.wait_recv()
    asked = jnp.sum(jnp.where(lane16 == line16, asks[0:1, :], 0.0), axis=1, keepdims=True)
    hsend[...] = dot_nn(jnp.where(lane16.astype(F32) == asked, 1.0, 0.0).astype(BF16), mh[...]).astype(BF16)
    row_hop.start()
    each_chunk(lambda c: hid_copy(c).start())
    ph_e = seq_start(lambda to: pka.at[1, to], landa.at[1, me])
    landa[1, me] = pka[1, me]

    def unpack(k, land, height, first):
        n = S * height
        r = lax.broadcasted_iota(jnp.int32, (n, n), 0)
        c = lax.broadcasted_iota(jnp.int32, (n, n), 1)
        perm = jnp.where(c == (r % S) * height + r // S, 1.0, 0.0).astype(BF16)
        flat = land[...].astype(F32).reshape(n, DS).astype(BF16)
        rows[k, first * S:(first + height) * S, :] = dot_nn(perm, flat)

    def rows_at(k, slot):
        return rows[k, slot * S:(slot + 1) * S, :]

    def gather_dp(k, dst):
        return dp_start(lambda to: dst.at[k, rowslice(d), :], dst.at[k, rowslice(d), :])

    def gather_dp_wait(ph, k, dst):
        dp_wait(ph, lambda frm: dst.at[k, rowslice(frm), :])

    def gate_up(k):
        for half in range(2):
            full = dot_nn(xr[k], w[k, half]).astype(BF16)
            for q in range(CG):
                gu[k, q, half] = full[:, q * PC:(q + 1) * PC]
        ph = seq_start(piece_of(gu.at[k]), lg.at[k, me])
        lg[k, me] = gu[k, cg, :, rowslice(rg), :]
        return ph

    def gate_up_wait(ph, k):
        seq_wait(ph, lambda frm: lg.at[k, frm])
        return add_up(lg.at[k])

    def add_up(ref):
        total = ref[0].astype(F32)
        for b in range(1, ref.shape[0]):
            total = total + ref[b].astype(F32)
        return total

    def dact(k):
        full = dot_nn(do[k], w[k, 2]).astype(BF16)
        for q in range(CG):
            da[k, q, 0] = full[:, q * PC:(q + 1) * PC]
        ph = seq_start(piece_of(da.at[k]), ld.at[k, me])
        ld[k, me] = da[k, cg, :, rowslice(rg), :]
        return ph

    def dact_wait(ph, k):
        seq_wait(ph, lambda frm: ld.at[k, frm])
        return add_up(ld.at[k])[0]

    def spread_piece(ref):
        mine = ref.at[cg, :, rowslice(rg), :]
        return seq_start(lambda to: mine, mine)

    def spread_wait(ph, ref):
        seq_wait(ph, lambda frm: ref.at[lax.rem(frm, CG), :, rowslice(frm // CG), :])

    def reduce_dp(n, full):
        op[n] = full.astype(BF16)
        ph = dp_start(lambda to: op.at[n, rowslice(to), :], lo.at[n, d])
        lo[n, d] = op[n, rowslice(d), :]
        return ph

    def reduce_dp_wait(ph, n):
        dp_wait(ph, lambda frm: lo.at[n, frm])
        return add_up(lo.at[n])

    def drows(k):
        total = None
        for q in range(CG):
            cols = slice(q * PC, (q + 1) * PC)
            part = dot_nt(dg[k, q, 0], w[k, 0, :, cols]) + dot_nt(dg[k, q, 1], w[k, 1, :, cols])
            total = part if total is None else total + part
        return total

    def sums_start(n, cols):
        lane = lax.broadcasted_iota(jnp.int32, (S, 128), 1)
        total = jnp.zeros((S, 128), F32)
        for i, col in enumerate(cols):
            total = total + jnp.where(lane == i, col, 0.0)
        ss[n] = total
        ph = seq_start(lambda to: ss.at[n], ssl.at[n, me])
        ssl[n, me] = total
        return ph

    def sums_wait(ph, n):
        seq_wait(ph, lambda frm: ssl.at[n, frm])
        return add_up(ssl.at[n]) * (1.0 / D)

    def pre_grads(k, d_act):
        gate, up = gsv[k, 0], gsv[k, 1]
        sig = 1.0 / (1.0 + jnp.exp(-gate))
        dg[k, cg, 0, rowslice(rg), :] = (d_act * up * sig * (1.0 + gate * (1.0 - sig))).astype(BF16)
        dg[k, cg, 1, rowslice(rg), :] = (d_act * (gate * sig)).astype(BF16)

    def act_piece(k):
        gate, up = gsv[k, 0], gsv[k, 1]
        act[k, cg, 0, rowslice(rg), :] = (gate / (1.0 + jnp.exp(-gate)) * up).astype(BF16)

    def in_grads(k):
        for half in range(2):
            for q in range(CG):
                eg[k, half, :, q * PC:(q + 1) * PC] = dot_tn(xr[k], dg[k, q, half]).astype(BF16)

    def down_grad(k):
        for q in range(CG):
            eg[k, 2, :, q * PC:(q + 1) * PC] = dot_tn(do[k], act[k, q, 0]).astype(BF16)

    LB = 256
    NB = D // LB

    def lanes(b):
        return pl.ds(pl.multiple_of(b * LB, LB), LB)

    def sweep(fn, count):
        zero = jnp.zeros((PK, LB), F32)
        total = lax.fori_loop(0, NB, lambda b, acc: fn(lanes(b), acc), (zero,) * count)
        return [jnp.sum(t, axis=1, keepdims=True) * (1.0 / D) for t in total]

    def gain(k, at):
        return ng[k:k + 1, at]

    def collect(k, at, value, mask):
        value = value * mask
        gacc[k, :, at] += value[:8] + value[8:]

    def rows_pass_1(h_at, e_at, c_at, mask, prev_add, dm2_add):
        def squares(at, acc):
            h, e1, e2 = h_at(at), e_at(0, at), e_at(1, at)
            return acc[0] + h * h, acc[1] + e1 * e1, acc[2] + e2 * e2

        sh, se1, se2 = [lax.rsqrt(v + eps_norm) for v in sweep(squares, 3)]

        def mix(at, acc):
            m = (h_at(at) * sh) * gain(0, at) + (e_at(0, at) * se1) * gain(1, at)
            m = m.astype(BF16).astype(F32)
            if prev_add is not None:
                m = (m + prev_add(at)).astype(BF16).astype(F32)
            mx[:, at] = m
            return (acc[0] + m * m,)

        s2, = [lax.rsqrt(v + eps_norm) for v in sweep(mix, 1)]

        def top(at, acc):
            n2 = mx[:, at] * s2
            dm2 = c_at(at)
            if dm2_add is not None:
                dm2 = dm2 + dm2_add(at)
            collect(2, at, dm2 * n2, mask)
            collect(3, at, dm2 * (e_at(1, at) * se2), mask)
            u = dm2 * gain(2, at)
            dmx[:, at] = u
            return (acc[0] + u * n2,)

        inner, = sweep(top, 1)

        def middle(at, acc):
            dmx[:, at] = (dmx[:, at] - (mx[:, at] * s2) * inner) * s2
            return acc

        sweep(middle, 0)
        return sh, se1

    def rows_pass_2(h_at, e_at, mask, sh, se1, dm1_add, store):
        def low(at, acc):
            dm1 = dmx[:, at]
            if dm1_add is not None:
                dm1 = dm1 + dm1_add(at)
            n1 = h_at(at) * sh
            if mask is not None:
                collect(0, at, dm1 * n1, mask)
                collect(1, at, dm1 * (e_at(0, at) * se1), mask)
            u = dm1 * gain(0, at)
            dmx[:, at] = u
            return (acc[0] + u * n1,)

        inner, = sweep(low, 1)

        def last(at, acc):
            store(at, ((dmx[:, at] - (h_at(at) * sh) * inner) * sh).astype(BF16))
            return acc

        sweep(last, 0)

    def bulk_chunk(c):
        hid_copy(c).wait_recv()
        r = lax.broadcasted_iota(jnp.int32, (2 * PK, 2 * PK), 0)
        k = lax.broadcasted_iota(jnp.int32, (2 * PK, 2 * PK), 1)
        shift = jnp.where(k == r % PK + 1 + r // PK, 1.0, 0.0).astype(BF16)
        es[...] = dot_nn(shift, ext[pl.ds(pl.multiple_of(c * PK, PK), 2 * PK), :]).astype(BF16)
        place = (line16 + c * PK).astype(F32)
        hit = jnp.sum(jnp.where(place == slot_row, live_row, 0.0), axis=1, keepdims=True)
        mask = jnp.where(hit > 0.5, 0.0, 1.0)

        def h_at(at):
            return hid[chunk(c), at].astype(F32)

        def e_at(k, at):
            return es[k * PK:(k + 1) * PK, at].astype(F32)

        sh, se1 = rows_pass_1(h_at, e_at, lambda at: cot[chunk(c), at].astype(F32), mask, None, None)

        def store(at, value):
            hgs[chunk(c), at] = value

        rows_pass_2(h_at, e_at, mask, sh, se1, None, store)
        hg_copy(c).start()

    def bulk(first, last):
        each_chunk(bulk_chunk, first, last)

    gacc[...] = jnp.zeros_like(gacc)

    def slot_h(at):
        return hrow[:, at].astype(F32)

    def slot_e(k, at):
        return se[k, :, at].astype(F32)

    slot_mask = column(fresh_row)
    same_tok = jnp.where(slot_tok == slot_row, live_row, 0.0)
    prev_sel = jnp.where(lane16 < C, same_tok, 0.0)
    prev_w = jnp.sum(prev_sel * weight_row, axis=1, keepdims=True)
    dm2_tok = jnp.where(slot_tok == slots[5:6, :], slots[6:7, :], 0.0)
    dm2_sel = jnp.where(lane16 < C, dm2_tok, 0.0)

    def widen(n, sel, k, scale_by):
        for b in range(S):
            part = dot_nn(sel[:, :8].astype(BF16), ret[k, b])
            if scale_by is not None:
                part = part * scale_by
            ad[n, :, dslice(b)] = part

    def send_back(k):
        r = lax.broadcasted_iota(jnp.int32, (S * 8, RW), 0)
        c = lax.broadcasted_iota(jnp.int32, (S * 8, RW), 1)
        perm = jnp.where(c == (r % 8) * S + r // 8, 1.0, 0.0).astype(BF16)
        rb[k] = dot_nn(perm, od[k * RW:(k + 1) * RW, :]).reshape(S, 8, DS).astype(BF16)
        ph = seq_start(lambda to: rb.at[k, to], ret.at[k, me])
        ret[k, me] = rb[k, me]
        return ph

    seq_wait(ph_a, lambda frm: landa.at[0, frm])
    unpack(0, landa.at[0], PK, 0)
    do[1, rowslice(d), :] = rows[0, RW:2 * RW, :].astype(BF16)
    ph_d2 = gather_dp(1, do)

    row_hop.wait_recv()

    def slot_squares(at, acc):
        h, e1, e2 = slot_h(at), slot_e(0, at), slot_e(1, at)
        return acc[0] + h * h, acc[1] + e1 * e1, acc[2] + e2 * e2

    sh, se1, se2 = [lax.rsqrt(v + eps_norm) for v in sweep(slot_squares, 3)]

    def slot_mix(at, acc):
        m = (slot_h(at) * sh) * gain(0, at) + (slot_e(0, at) * se1) * gain(1, at)
        mx[:, at] = m.astype(BF16).astype(F32) * slot_live
        return acc

    sweep(slot_mix, 0)
    for b in range(S):
        part = mx[:, dslice(b)]
        pkb[0, b] = part[:8].astype(BF16)
        pkb[1, b] = part[8:].astype(BF16)
        pkb[2, b] = hrow[:, dslice(b)].astype(F32)[:8].astype(BF16)
    ph_b = seq_start(lambda to: pkb.at[0, to], landb.at[0, me])
    se2_t2 = pltpu.roll(jnp.broadcast_to(se2, (PK, 128)), PK - C, 0)
    top = slots[4:5, :] + line(se2_t2, 8) + line(sh, 52) + line(se1, 58)
    meta[...] = jnp.broadcast_to(top, (8, 128)) * jnp.where(line16[:8] == 0, 1.0, 0.0)
    ph_m = seq_start(lambda to: meta, mland.at[me])
    mland[me] = meta[...]
    ph_b1 = seq_start(lambda to: pkb.at[1, to], landb.at[1, me])
    ph_b2 = seq_start(lambda to: pkb.at[2, to], landb.at[2, me])
    for k in range(3):
        landb[k, me] = pkb[k, me]
    gather_dp_wait(ph_d2, 1, do)
    seq_wait(ph_b, lambda frm: landb.at[0, frm])
    unpack(1, landb.at[0], 8, 0)
    xr[0, rowslice(d), :] = rows[1, 0:RW, :].astype(BF16)
    ph_x = gather_dp(0, xr)
    ph_da2 = dact(1)
    seq_wait(ph_b1, lambda frm: landb.at[1, frm])
    unpack(1, landb.at[1], 8, 8)
    seq_wait(ph_e, lambda frm: landa.at[1, frm])
    unpack(2, landa.at[1], PK, 0)
    gather_dp_wait(ph_x, 0, xr)
    ph = gate_up(0)
    gsv[0] = gate_up_wait(ph, 0)
    act_piece(0)
    ph = spread_piece(act.at[0])
    bulk(0, 3 * NC // 8)
    spread_wait(ph, act.at[0])
    out = None
    for q in range(CG):
        part = dot_nt(act[0, q, 0], w[0, 2, :, q * PC:(q + 1) * PC])
        out = part if out is None else out + part
    ph = reduce_dp(0, out)
    bulk(3 * NC // 8, NC // 2)
    seq_wait(ph_m, lambda frm: mland.at[frm])
    facts = jnp.sum(mland[...], axis=1)

    def fact(k):
        return facts[:, k:k + 1]

    def ov(j, i):
        return fact(16 + j * C + i)

    out = reduce_dp_wait(ph, 0)
    od[0:RW, :] = out.astype(BF16)
    cols = []
    for i in range(C):
        before = rows_at(1, i) + fact(i) * out[i * S:(i + 1) * S]
        before = before.astype(BF16).astype(F32)
        pv[i * S:(i + 1) * S, :] = before
        cols.append(jnp.sum(before * before, axis=1, keepdims=True))
    for j in range(C):
        before = rows_at(1, C + j)
        for i in range(C):
            before = before + (ov(j, i) * fact(i)) * out[i * S:(i + 1) * S]
        before = before.astype(BF16).astype(F32)
        pv[(C + j) * S:(C + j + 1) * S, :] = before
        cols.append(jnp.sum(before * before, axis=1, keepdims=True))
    ph = sums_start(0, cols)
    gain_h, gain_e = g2[0:1, :], g2[1:2, :]
    scale = lax.rsqrt(sums_wait(ph, 0) + eps_norm)

    for j in range(C):
        unit = pv[(C + j) * S:(C + j + 1) * S, :] * scale[:, C + j:C + j + 1]
        mixed = unit * gain_h + (rows_at(2, C + j) * fact(8 + j)) * gain_e
        od[3 * RW + j * S:3 * RW + (j + 1) * S, :] = mixed.astype(BF16)
    xr[1, rowslice(d), :] = od[3 * RW:4 * RW, :]
    ph = gather_dp(1, xr)
    ph_r0 = send_back(0)
    gather_dp_wait(ph, 1, xr)
    ph = gate_up(1)
    bulk(NC // 2, NC)
    d_act = dact_wait(ph_da2, 1)
    gsv[1] = gate_up_wait(ph, 1)
    pre_grads(1, d_act)
    ph = spread_piece(dg.at[1])
    act_piece(1)
    ph_a2 = spread_piece(act.at[1])
    spread_wait(ph, dg.at[1])
    ph = reduce_dp(1, drows(1))
    in_grads(1)
    back = reduce_dp_wait(ph, 1)
    od[RW:2 * RW, :] = back.astype(BF16)
    cols, keep_u, keep_n = [], [], []
    for i in range(C):
        top = rows_at(0, i)
        for j in range(C):
            top = top + ov(j, i) * back[j * S:(j + 1) * S]
        u = top * gain_h
        unit = pv[i * S:(i + 1) * S, :] * scale[:, i:i + 1]
        keep_u.append(u)
        keep_n.append(unit)
        cols.append(jnp.sum(u * unit, axis=1, keepdims=True))
    ph = sums_start(1, cols)

    inner = sums_wait(ph, 1)

    for i in range(C):
        back = (keep_u[i] - keep_n[i] * inner[:, i:i + 1]) * scale[:, i:i + 1]
        od[3 * RW + i * S:3 * RW + (i + 1) * S, :] = (back * fact(i)).astype(BF16)
    do[0, rowslice(d), :] = od[3 * RW:4 * RW, :]
    ph = gather_dp(0, do)
    ph_r1 = send_back(1)
    gather_dp_wait(ph, 0, do)
    ph = dact(0)
    spread_wait(ph_a2, act.at[1])
    seq_wait(ph_r0, lambda frm: ret.at[0, frm])
    seq_wait(ph_r1, lambda frm: ret.at[1, frm])
    widen(0, prev_sel, 0, prev_w)
    widen(1, dm2_sel, 1, None)
    slot_sh, slot_se1 = rows_pass_1(
        slot_h, slot_e, lambda at: sc[:, at].astype(F32), slot_mask, lambda at: ad[0, :, at], lambda at: ad[1, :, at]
    )

    def early(at, acc):
        collect(0, at, dmx[:, at] * (slot_h(at) * slot_sh), slot_mask)
        collect(1, at, dmx[:, at] * (slot_e(0, at) * slot_se1), slot_mask)
        return acc

    sweep(early, 0)
    d_act = dact_wait(ph, 0)
    pre_grads(0, d_act)
    ph = spread_piece(dg.at[0])
    down_grad(1)
    down_grad(0)
    spread_wait(ph, dg.at[0])
    for b in range(S):
        gsrc[b] = jnp.sum(gacc[:, :, dslice(b)], axis=1)
    ph_g = seq_start(lambda to: gsrc.at[to], gland.at[me])
    gland[me] = gsrc[me]
    ph = reduce_dp(2, drows(0))
    in_grads(0)
    back = reduce_dp_wait(ph, 2)
    od[2 * RW:3 * RW, :] = back.astype(BF16)
    ph_r2 = send_back(2)

    seq_wait(ph_b2, lambda frm: landb.at[2, frm])
    unpack(1, landb.at[2], 8, 0)
    late_h = jnp.zeros((S, DS), F32)
    late_e = jnp.zeros((S, DS), F32)
    for i in range(C):
        part = back[i * S:(i + 1) * S]
        late_h = late_h + part * (rows_at(1, i) * fact(52 + i))
        late_e = late_e + part * (rows_at(2, i) * fact(58 + i))
    seq_wait(ph_g, lambda frm: gland.at[frm])
    value = add_up(gland)
    late = jnp.concatenate(
        [jnp.sum(late_h, axis=0, keepdims=True), jnp.sum(late_e, axis=0, keepdims=True), jnp.zeros((2, DS), F32)], 0
    )
    value = value + late
    QS = DS // Q
    for q in range(Q):
        gown[q] = value[:, q * QS:(q + 1) * QS]
    ph_q = dp_start(lambda to: gown.at[to], gland2.at[d])
    gland2[d] = gown[d]

    seq_wait(ph_r2, lambda frm: ret.at[2, frm])
    widen(2, prev_sel, 2, None)

    def slot_store(at, value):
        sls[:, at] = value

    rows_pass_2(slot_h, slot_e, None, slot_sh, slot_se1, lambda at: ad[2, :, at], slot_store)
    back_rows = hop(sls, slr, 2 * NC, before_me)
    back_rows.start()
    dp_wait(ph_q, lambda frm: gland2.at[frm])
    gains[...] = add_up(gland2)

    def finish(c):
        hid_copy(c).wait_send()
        hg_copy(c).wait_send()
        hg_copy(c).wait_recv()

    each_chunk(finish)
    ask_hop.wait_send()
    row_hop.wait_send()
    back_rows.wait()
    wires.drain()


def chain(slots, g2, w, mh, own, ahead, cot, ng, C):
    S, Q, X = lax.axis_size("seq"), lax.axis_size("dp"), lax.axis_size("section")
    DS, HS = w.shape[2], w.shape[3]
    T, D = mh.shape
    RW = C * S
    NR = Q * RW
    CG = S // Q
    PC = HS // CG
    NC = T // PK
    vm = pltpu.VMEM
    phases = 30
    return pl.pallas_call(
        functools.partial(chain_kernel, S, Q, X, C, D),
        out_shape=(
            jax.ShapeDtypeStruct(w.shape, BF16),
            jax.ShapeDtypeStruct((T, D), BF16),
            jax.ShapeDtypeStruct((PK, D), BF16),
            jax.ShapeDtypeStruct((4, DS // Q), F32),
            jax.ShapeDtypeStruct((8, 128), F32),
        ),
        in_specs=[pl.BlockSpec(memory_space=vm)] * 8,
        out_specs=(pl.BlockSpec(memory_space=vm),) * 5,
        scratch_shapes=[
            vm((T + PK, D), BF16),
            vm((PK, D), BF16),
            vm((PK, D), BF16),
            vm((2, PK, D), BF16),
            vm((PK, D), BF16),
            vm((2, S, PK, DS), BF16),
            vm((3, S, 8, DS), BF16),
            vm((2, S, PK, DS), BF16),
            vm((3, S, 8, DS), BF16),
            vm((8, 128), F32),
            vm((S, 8, 128), F32),
            vm((3, S * PK, DS), F32),
            vm((3, S, 8, DS), BF16),
            vm((3, S, 8, DS), BF16),
            vm((2, NR, DS), BF16),
            vm((2, NR, DS), BF16),
            vm((2, CG, 2, NR, PC), BF16),
            vm((2, S, 2, RW, PC), BF16),
            vm((2, CG, 1, NR, PC), BF16),
            vm((2, S, 1, RW, PC), BF16),
            vm((2, CG, 1, NR, PC), BF16),
            vm((2, CG, 2, NR, PC), BF16),
            vm((3, NR, DS), BF16),
            vm((3, Q, RW, DS), BF16),
            vm((2 * RW, DS), F32),
            vm((2, S, 128), F32),
            vm((2, S, S, 128), F32),
            vm((4 * RW, DS), BF16),
            vm((2, 2, RW, PC), F32),
            vm((T, D), BF16),
            vm((T, D), BF16),
            vm((2 * PK, D), BF16),
            vm((PK, D), F32),
            vm((PK, D), F32),
            vm((3, PK, D), F32),
            vm((PK, D), BF16),
            vm((4, 8, D), F32),
            vm((S, 4, DS), F32),
            vm((S, 4, DS), F32),
            vm((Q, 4, DS // Q), F32),
            vm((Q, 4, DS // Q), F32),
            pltpu.SemaphoreType.DMA((phases, S)),
            pltpu.SemaphoreType.DMA((phases, S)),
            pltpu.SemaphoreType.DMA((2 * NC + 3,)),
            pltpu.SemaphoreType.DMA((2 * NC + 3,)),
        ],
        compiler_params=pltpu.CompilerParams(
            collective_id=0, has_side_effects=True, vmem_limit_bytes=60 * 1024 * 1024
        ),
        name="expert_chain",
    )(slots, g2, w, mh, own, ahead, cot, ng)


def pick(index, count):
    return (index[:, None] == jnp.arange(count, dtype=jnp.int32)[None, :]).astype(BF16)


def local(main_hidden, embedded, cotangent, slot_token, slot_count, route_gate, norm_gain, w):
    S = lax.axis_size("seq")
    me = lax.axis_index("seq")
    tokens_here, D = main_hidden.shape[2:]
    C = slot_token.shape[3]
    DS = D // S
    tok = slot_token[0, 0]
    live = (jnp.arange(C, dtype=jnp.int32)[None, :] < slot_count[0, 0]).astype(F32)
    weight = route_gate[0, 0] * live
    own, cot, mh = embedded[0, 0], cotangent[0, 0], main_hidden[0, 0]
    ahead = from_ahead(own[:2], "seq", 1)
    same = (tok[1][:, None] == tok[0][None, :]).astype(F32) * live[1][:, None] * live[0][None, :]
    fresh = jnp.stack([live[0], live[1] * (1.0 - jnp.max(same, axis=1))]).reshape(-1)
    flat = tok.reshape(-1)

    def lanes(*parts):
        row = jnp.concatenate(parts)
        return jnp.pad(row, (0, 128 - row.shape[0]))

    slots = jnp.stack([
        lanes(flat.astype(F32)),
        lanes(live.reshape(-1)),
        lanes(weight.reshape(-1)),
        lanes(fresh),
        lanes(weight[0], jnp.zeros((16 - C,), F32), same.reshape(-1)),
        lanes(tok[1].astype(F32)),
        lanes(live[1]),
        lanes(flat[:1].astype(F32) * 0.0),
    ])
    g2 = lax.dynamic_slice(norm_gain[1], (0, me * DS), (2, DS))
    g2 = jnp.concatenate([g2, jnp.zeros((6, DS), F32)], 0)
    ahead = jnp.pad(ahead, ((0, PK - 2), (0, 0)))
    ng = norm_gain.reshape(4, D)

    expert_grad, grads, slot_grads, total, asks = chain(slots, g2, w, mh, own, ahead, cot, ng, C)
    back_to = jnp.where(asks[3, :2 * C] > 0.5, asks[0, :2 * C], -1.0).astype(jnp.int32)
    put = pick(back_to, tokens_here)
    hit = jnp.sum(put.astype(F32), axis=0)
    placed = lax.dot_general(
        put, slot_grads[:2 * C], (((0,), (0,)), ((), ())), preferred_element_type=F32
    )
    hidden_grad = jnp.where(hit[:, None] > 0.5, placed.astype(BF16), grads)
    return (hidden_grad[None, None], expert_grad[None], total.reshape(1, 2, 2, -1))


def solution(mesh):
    return jax.shard_map(
        local,
        mesh=mesh,
        in_specs=(
            P("section", "dp", "seq", None),
            P("section", "dp", "seq", None),
            P("section", "dp", "seq", None),
            P("section", "dp", None, "seq"),
            P("section", "dp", None, "seq"),
            P("section", "dp", None, "seq"),
            P(),
            P(None, None, "seq", "dp"),
        ),
        out_specs=(
            P("section", "dp", "seq", None),
            P("section", None, None, "seq", "dp"),
            P("section", None, None, ("seq", "dp")),
        ),
        check_vma=False,
    )
```

```python
import functools

import jax
import jax.numpy as jnp
from jax import lax
from jax.experimental import pallas as pl
from jax.experimental.pallas import tpu as pltpu
from jax.sharding import PartitionSpec as P

eps_norm = 1e-06
MESH = pl.DeviceIdType.MESH
F32 = jnp.float32
BF16 = jnp.bfloat16
PK = 16


def from_behind(value, axis, steps):
    count = lax.axis_size(axis)
    pairs = [(source, (source + steps) % count) for source in range(count)]
    return lax.ppermute(value, axis, pairs)


def from_ahead(array, axis, by):
    size = lax.axis_size(axis)
    pairs = [(i, i - by) for i in range(size) if 0 <= i - by < size]
    return lax.ppermute(array, axis, pairs)


def normed(value):
    wide = value.astype(F32)
    scale = lax.rsqrt(jnp.mean(wide * wide, axis=-1, keepdims=True) + eps_norm)
    return (wide * scale, scale)


def norm_back(grad, unit, scale):
    inner = jnp.mean(grad * unit, axis=-1, keepdims=True)
    return (grad - unit * inner) * scale


def dot_nn(a, b):
    return lax.dot_general(a, b, (((1,), (0,)), ((), ())), preferred_element_type=F32)


def dot_nt(a, b):
    return lax.dot_general(a, b, (((1,), (1,)), ((), ())), preferred_element_type=F32)


def dot_tn(a, b):
    return lax.dot_general(a, b, (((0,), (0,)), ((), ())), preferred_element_type=F32)


class Wires:
    def __init__(self, send, recv):
        self.send, self.recv = send, recv
        self.phases = 0
        self.open = []
        self.singles = []

    def copy(self, src, dst, ph, slot_s, slot_r, axis, to):
        return pltpu.make_async_remote_copy(
            src_ref=src,
            dst_ref=dst,
            send_sem=self.send.at[ph, slot_s],
            recv_sem=self.recv.at[ph, slot_r],
            device_id={axis: to},
            device_id_type=MESH,
        )

    def start(self, axis, size, me, src_of, dst):
        ph = self.phases
        self.phases += 1

        def body(o, c):
            to = lax.rem(me + o, size)
            self.copy(src_of(to), dst, ph, o, me, axis, to).start()
            return c

        lax.fori_loop(1, size, body, 0)
        self.open.append((ph, axis, size, me, src_of))
        return ph

    def wait(self, ph, axis, size, me, dst_of):
        def body(o, c):
            frm = lax.rem(me + o, size)
            self.copy(dst_of(frm), dst_of(frm), ph, o, frm, axis, frm).wait_recv()
            return c

        lax.fori_loop(1, size, body, 0)

    def phase(self):
        self.phases += 1
        return self.phases - 1

    def one(self, src, dst, ph, slot_s, slot_r, axis, to):
        copy = self.copy(src, dst, ph, slot_s, slot_r, axis, to)
        copy.start()
        self.singles.append(copy)

    def drain(self):
        for copy in self.singles:
            copy.wait_send()
        for ph, axis, size, me, src_of in self.open:

            def body(o, c):
                to = lax.rem(me + o, size)
                self.copy(src_of(to), src_of(to), ph, o, me, axis, to).wait_send()
                return c

            lax.fori_loop(1, size, body, 0)


def greet(axes, sections=()):
    barrier = pltpu.get_barrier_semaphore()
    total = 0
    for axis, size, me in axes:

        def body(o, c):
            to = lax.rem(me + o, size)
            pl.semaphore_signal(barrier, inc=1, device_id={axis: to}, device_id_type=MESH)
            return c

        lax.fori_loop(1, size, body, 0)
        total += size - 1
    for to in sections:
        pl.semaphore_signal(barrier, inc=1, device_id={"section": to}, device_id_type=MESH)
        total += 1
    return lambda: pl.semaphore_wait(barrier, total)


def chain_kernel(S, Q, X, C, D, slots, g2, w, mh, own, ahead, cot, ng, eg, hg, slr, gains, asks,
                 ext, hsend, hrow, se, sc, pka, pkb, landa, landb, meta, mland, rows, ret, rb, xr, do, gu, lg, ly, cmb, gf, da,
                 ld, act, dg, op, lo, pv, ss, ssl, od, gsv, hid, hgs, es, mx, dmx, ad, sls, gacc, gsrc, gland,
                 gown, gland2, send, recv, xsend, xrecv):
    me = lax.axis_index("seq")
    d = lax.axis_index("dp")
    sec = lax.axis_index("section")
    after, before_me = lax.rem(sec + 1, X), lax.rem(sec + X - 1, X)
    DS, HS = w.shape[2], w.shape[3]
    RW = C * S
    CG = S // Q
    PC = HS // CG
    rg, cg = me // CG, lax.rem(me, CG)
    wires = Wires(send, recv)

    def rowslice(g):
        return pl.ds(pl.multiple_of(g * RW, 32 if RW % 32 == 0 else 8), RW)

    def piece_of(ref):
        def src(to):
            return ref.at[to % CG, :, rowslice(to // CG), :]
        return src

    def seq_start(src_of, dst):
        return wires.start("seq", S, me, src_of, dst)

    def seq_wait(ph, dst_of):
        wires.wait(ph, "seq", S, me, dst_of)

    def dp_start(src_of, dst):
        return wires.start("dp", Q, d, src_of, dst)

    def dp_wait(ph, dst_of):
        wires.wait(ph, "dp", Q, d, dst_of)

    barrier_axes = (("seq", S, me), ("dp", Q, d))
    greet_all = greet(barrier_axes, (after, before_me))
    NC = mh.shape[0] // PK
    T = mh.shape[0]

    def chunk(c):
        return pl.ds(pl.multiple_of(c * PK, PK), PK)

    def hop(src, dst, slot, to):
        return pltpu.make_async_remote_copy(
            src_ref=src, dst_ref=dst, send_sem=xsend.at[slot], recv_sem=xrecv.at[slot],
            device_id={"section": to}, device_id_type=MESH,
        )

    def hid_copy(c):
        return hop(mh.at[chunk(c), :], hid.at[chunk(c), :], c, after)

    def hg_copy(c):
        return hop(hgs.at[chunk(c), :], hg.at[chunk(c), :], NC + c, before_me)

    ask_hop = hop(slots, asks, 2 * NC + 1, before_me)
    row_hop = hop(hsend, hrow, 2 * NC + 2, after)

    def each_chunk(fn, first=0, last=NC):
        def body(c, carry):
            fn(c)
            return carry

        lax.fori_loop(first, last, body, 0)

    slot_row, live_row, weight_row, fresh_row = (slots[k:k + 1, :] for k in range(4))
    lane16 = lax.broadcasted_iota(jnp.int32, (PK, 128), 1)
    line16 = lax.broadcasted_iota(jnp.int32, (PK, 128), 0)
    line1 = lax.broadcasted_iota(jnp.int32, (PK, 1), 0)

    def column(row):
        return jnp.sum(jnp.where(lane16 == line16, row, 0.0), axis=1, keepdims=True)

    def line(col, first):
        return jnp.sum(jnp.where((lane16 == line16 + first) & (line16 < C), col, 0.0), axis=0, keepdims=True)

    slot_tok, slot_live, slot_w = column(slot_row), column(live_row), column(weight_row)

    ext[0:T, :] = own[...]
    ext[T:T + PK, :] = ahead[...]
    wide = lax.broadcasted_iota(jnp.int32, (PK, T + PK), 1).astype(F32)
    for k in range(2):
        se[k] = dot_nn(jnp.where(wide == slot_tok + (k + 1.0), 1.0, 0.0).astype(BF16), ext[...]).astype(BF16)
    sc[...] = dot_nn(jnp.where(lane16.astype(F32) == slot_tok, 1.0, 0.0).astype(BF16), cot[...]).astype(BF16)

    greet_all()
    ask_hop.start()

    first_rows = line1 < C

    def dslice(b):
        return slice(b * DS, (b + 1) * DS)

    cot_w = jnp.where(first_rows, 1.0, slot_w)
    for b in range(S):
        pka[0, b] = (sc[:, dslice(b)].astype(F32) * cot_w).astype(BF16)
    ph_a = seq_start(lambda to: pka.at[0, to], landa.at[0, me])
    landa[0, me] = pka[0, me]
    e_live = jnp.where(first_rows, 1.0, slot_live)
    for b in range(S):
        both = jnp.where(first_rows, se[0, :, dslice(b)].astype(F32), se[1, :, dslice(b)].astype(F32))
        pka[1, b] = (both * e_live).astype(BF16)

    ask_hop.wait_recv()
    asked = jnp.sum(jnp.where(lane16 == line16, asks[0:1, :], 0.0), axis=1, keepdims=True)
    hsend[...] = dot_nn(jnp.where(lane16.astype(F32) == asked, 1.0, 0.0).astype(BF16), mh[...]).astype(BF16)
    row_hop.start()
    each_chunk(lambda c: hid_copy(c).start())
    ph_e = seq_start(lambda to: pka.at[1, to], landa.at[1, me])
    landa[1, me] = pka[1, me]

    def unpack(k, land, height, first):
        n = S * height
        r = lax.broadcasted_iota(jnp.int32, (n, n), 0)
        c = lax.broadcasted_iota(jnp.int32, (n, n), 1)
        perm = jnp.where(c == (r % S) * height + r // S, 1.0, 0.0).astype(BF16)
        flat = land[...].astype(F32).reshape(n, DS).astype(BF16)
        rows[k, first * S:(first + height) * S, :] = dot_nn(perm, flat)

    def rows_at(k, slot):
        return rows[k, slot * S:(slot + 1) * S, :]

    def gather_dp(k, dst):
        return dp_start(lambda to: dst.at[k, rowslice(d), :], dst.at[k, rowslice(d), :])

    def gather_dp_wait(ph, k, dst):
        dp_wait(ph, lambda frm: dst.at[k, rowslice(frm), :])

    def gate_up(k, work=None):
        far = [h for h in reversed(near)] + [0]
        for half in range(2):
            full = dot_nn(xr[k], w[k, half])
            for q in range(CG):
                cols = slice(q * PC, (q + 1) * PC)
                gf[q, half] = full[:, cols]
                gu[k, q, half] = full[:, cols].astype(BF16)

        def piece(ref, t):
            return ref.at[lax.rem(t, CG), :, rowslice(t // CG), :]

        ph = wires.phase()
        for h in far:
            z = lax.rem(zme + h, n)
            wires.one(piece(gu.at[k], at_z(h, 1 - yme)), ly.at[k, z], ph, h, h, "seq", yn)
        ph2 = wires.phase()
        for h in far:
            z = lax.rem(zme + h, n)
            wires.copy(ly.at[k, z], ly.at[k, z], ph, h, h, "seq", yn).wait_recv()
            both = piece(gf, at_z(h, yme))[...] + ly[k, z].astype(F32)
            if h == 0:
                total = both
            else:
                cmb[k, z] = both.astype(BF16)
                wires.one(cmb.at[k, z], lg.at[k, zme], ph2, h, h, "seq", at_z(h, yme))
        if work is not None:
            work()
        for h in near:
            z = lax.rem(zme + n - h, n)
            wires.copy(lg.at[k, z], lg.at[k, z], ph2, h, h, "seq", at_z(n - h, yme)).wait_recv()
            total = total + lg[k, z].astype(F32)
        return total

    def add_up(ref):
        total = ref[0].astype(F32)
        for b in range(1, ref.shape[0]):
            total = total + ref[b].astype(F32)
        return total

    def dact(k):
        full = dot_nn(do[k], w[k, 2]).astype(BF16)
        for q in range(CG):
            da[k, q, 0] = full[:, q * PC:(q + 1) * PC]
        ph = seq_start(piece_of(da.at[k]), ld.at[k, me])
        ld[k, me] = da[k, cg, :, rowslice(rg), :]
        return ph

    def dact_wait(ph, k):
        seq_wait(ph, lambda frm: ld.at[k, frm])
        return add_up(ld.at[k])[0]

    def spread_piece(ref):
        mine = ref.at[cg, :, rowslice(rg), :]
        return seq_start(lambda to: mine, mine)

    n = S // 2
    zme, yme = me // 2, lax.rem(me, 2)
    yn = me + 1 - 2 * yme
    near = sorted(range(1, n), key=lambda h: (min(h, n - h), h))

    def at_z(h, parity):
        return 2 * lax.rem(zme + h, n) + parity

    def spread(ref, work=None):
        def piece(t):
            return ref.at[lax.rem(t, CG), :, rowslice(t // CG), :]

        ph = wires.phase()
        mine = piece(me)
        for h in reversed(near):
            wires.one(mine, mine, ph, h, h, "seq", at_z(h, yme))
        wires.one(mine, mine, ph, 0, n, "seq", yn)
        for h in near:
            frm = at_z(n - h, yme)
            wires.copy(piece(frm), piece(frm), ph, h, h, "seq", frm).wait_recv()
            wires.one(piece(frm), piece(frm), ph, n + h, n + h, "seq", yn)
        if work is not None:
            work()
        for h in [0] + near:
            frm = at_z(n - h, 1 - yme)
            wires.copy(piece(frm), piece(frm), ph, n + h, n + h, "seq", yn).wait_recv()

    def spread_wait(ph, ref):
        seq_wait(ph, lambda frm: ref.at[lax.rem(frm, CG), :, rowslice(frm // CG), :])

    def reduce_dp(n, full):
        op[n] = full.astype(BF16)
        ph = dp_start(lambda to: op.at[n, rowslice(to), :], lo.at[n, d])
        lo[n, d] = op[n, rowslice(d), :]
        return ph

    def reduce_dp_wait(ph, n):
        dp_wait(ph, lambda frm: lo.at[n, frm])
        return add_up(lo.at[n])

    def drows(k):
        total = None
        for q in range(CG):
            cols = slice(q * PC, (q + 1) * PC)
            part = dot_nt(dg[k, q, 0], w[k, 0, :, cols]) + dot_nt(dg[k, q, 1], w[k, 1, :, cols])
            total = part if total is None else total + part
        return total

    def sums_start(n, cols):
        lane = lax.broadcasted_iota(jnp.int32, (S, 128), 1)
        total = jnp.zeros((S, 128), F32)
        for i, col in enumerate(cols):
            total = total + jnp.where(lane == i, col, 0.0)
        ss[n] = total
        ph = seq_start(lambda to: ss.at[n], ssl.at[n, me])
        ssl[n, me] = total
        return ph

    def sums_wait(ph, n):
        seq_wait(ph, lambda frm: ssl.at[n, frm])
        return add_up(ssl.at[n]) * (1.0 / D)

    def pre_grads(k, d_act):
        gate, up = gsv[k, 0], gsv[k, 1]
        sig = 1.0 / (1.0 + jnp.exp(-gate))
        dg[k, cg, 0, rowslice(rg), :] = (d_act * up * sig * (1.0 + gate * (1.0 - sig))).astype(BF16)
        dg[k, cg, 1, rowslice(rg), :] = (d_act * (gate * sig)).astype(BF16)

    def act_piece(k):
        gate, up = gsv[k, 0], gsv[k, 1]
        act[k, cg, 0, rowslice(rg), :] = (gate / (1.0 + jnp.exp(-gate)) * up).astype(BF16)

    def in_grads(k):
        for half in range(2):
            for q in range(CG):
                eg[k, half, :, q * PC:(q + 1) * PC] = dot_tn(xr[k], dg[k, q, half]).astype(BF16)

    def down_grad(k):
        for q in range(CG):
            eg[k, 2, :, q * PC:(q + 1) * PC] = dot_tn(do[k], act[k, q, 0]).astype(BF16)

    LB = 256
    NB = D // LB

    def lanes(b):
        return pl.ds(pl.multiple_of(b * LB, LB), LB)

    def sweep(fn, count):
        zero = jnp.zeros((PK, LB), F32)
        total = lax.fori_loop(0, NB, lambda b, acc: fn(lanes(b), acc), (zero,) * count)
        return [jnp.sum(t, axis=1, keepdims=True) * (1.0 / D) for t in total]

    def gain(k, at):
        return ng[k:k + 1, at]

    def collect(k, at, value, mask):
        value = value * mask
        gacc[k, :, at] += value[:8] + value[8:]

    def rows_pass_1(h_at, e_at, c_at, mask, prev_add, dm2_add):
        def squares(at, acc):
            h, e1, e2 = h_at(at), e_at(0, at), e_at(1, at)
            return acc[0] + h * h, acc[1] + e1 * e1, acc[2] + e2 * e2

        sh, se1, se2 = [lax.rsqrt(v + eps_norm) for v in sweep(squares, 3)]

        def mix(at, acc):
            m = (h_at(at) * sh) * gain(0, at) + (e_at(0, at) * se1) * gain(1, at)
            m = m.astype(BF16).astype(F32)
            if prev_add is not None:
                m = (m + prev_add(at)).astype(BF16).astype(F32)
            mx[:, at] = m
            return (acc[0] + m * m,)

        s2, = [lax.rsqrt(v + eps_norm) for v in sweep(mix, 1)]

        def top(at, acc):
            n2 = mx[:, at] * s2
            dm2 = c_at(at)
            if dm2_add is not None:
                dm2 = dm2 + dm2_add(at)
            collect(2, at, dm2 * n2, mask)
            collect(3, at, dm2 * (e_at(1, at) * se2), mask)
            u = dm2 * gain(2, at)
            dmx[:, at] = u
            return (acc[0] + u * n2,)

        inner, = sweep(top, 1)

        def middle(at, acc):
            dmx[:, at] = (dmx[:, at] - (mx[:, at] * s2) * inner) * s2
            return acc

        sweep(middle, 0)
        return sh, se1

    def rows_pass_2(h_at, e_at, mask, sh, se1, dm1_add, store):
        def low(at, acc):
            dm1 = dmx[:, at]
            if dm1_add is not None:
                dm1 = dm1 + dm1_add(at)
            n1 = h_at(at) * sh
            if mask is not None:
                collect(0, at, dm1 * n1, mask)
                collect(1, at, dm1 * (e_at(0, at) * se1), mask)
            u = dm1 * gain(0, at)
            dmx[:, at] = u
            return (acc[0] + u * n1,)

        inner, = sweep(low, 1)

        def last(at, acc):
            store(at, ((dmx[:, at] - (h_at(at) * sh) * inner) * sh).astype(BF16))
            return acc

        sweep(last, 0)

    def bulk_chunk(c):
        hid_copy(c).wait_recv()
        r = lax.broadcasted_iota(jnp.int32, (2 * PK, 2 * PK), 0)
        k = lax.broadcasted_iota(jnp.int32, (2 * PK, 2 * PK), 1)
        shift = jnp.where(k == r % PK + 1 + r // PK, 1.0, 0.0).astype(BF16)
        es[...] = dot_nn(shift, ext[pl.ds(pl.multiple_of(c * PK, PK), 2 * PK), :]).astype(BF16)
        place = (line16 + c * PK).astype(F32)
        hit = jnp.sum(jnp.where(place == slot_row, live_row, 0.0), axis=1, keepdims=True)
        mask = jnp.where(hit > 0.5, 0.0, 1.0)

        def h_at(at):
            return hid[chunk(c), at].astype(F32)

        def e_at(k, at):
            return es[k * PK:(k + 1) * PK, at].astype(F32)

        sh, se1 = rows_pass_1(h_at, e_at, lambda at: cot[chunk(c), at].astype(F32), mask, None, None)

        def store(at, value):
            hgs[chunk(c), at] = value

        rows_pass_2(h_at, e_at, mask, sh, se1, None, store)
        hg_copy(c).start()

    def bulk(first, last):
        each_chunk(bulk_chunk, first, last)

    gacc[...] = jnp.zeros_like(gacc)

    def slot_h(at):
        return hrow[:, at].astype(F32)

    def slot_e(k, at):
        return se[k, :, at].astype(F32)

    slot_mask = column(fresh_row)
    same_tok = jnp.where(slot_tok == slot_row, live_row, 0.0)
    prev_sel = jnp.where(lane16 < C, same_tok, 0.0)
    prev_w = jnp.sum(prev_sel * weight_row, axis=1, keepdims=True)
    dm2_tok = jnp.where(slot_tok == slots[5:6, :], slots[6:7, :], 0.0)
    dm2_sel = jnp.where(lane16 < C, dm2_tok, 0.0)

    def widen(n, sel, k, scale_by):
        for b in range(S):
            part = dot_nn(sel[:, :8].astype(BF16), ret[k, b])
            if scale_by is not None:
                part = part * scale_by
            ad[n, :, dslice(b)] = part

    def send_back(k):
        r = lax.broadcasted_iota(jnp.int32, (S * 8, RW), 0)
        c = lax.broadcasted_iota(jnp.int32, (S * 8, RW), 1)
        perm = jnp.where(c == (r % 8) * S + r // 8, 1.0, 0.0).astype(BF16)
        rb[k] = dot_nn(perm, od[k * RW:(k + 1) * RW, :]).reshape(S, 8, DS).astype(BF16)
        ph = seq_start(lambda to: rb.at[k, to], ret.at[k, me])
        ret[k, me] = rb[k, me]
        return ph

    seq_wait(ph_a, lambda frm: landa.at[0, frm])
    unpack(0, landa.at[0], PK, 0)
    do[1, rowslice(d), :] = rows[0, RW:2 * RW, :].astype(BF16)
    ph_d2 = gather_dp(1, do)

    row_hop.wait_recv()

    def slot_squares(at, acc):
        h, e1, e2 = slot_h(at), slot_e(0, at), slot_e(1, at)
        return acc[0] + h * h, acc[1] + e1 * e1, acc[2] + e2 * e2

    sh, se1, se2 = [lax.rsqrt(v + eps_norm) for v in sweep(slot_squares, 3)]

    def slot_mix(at, acc):
        m = (slot_h(at) * sh) * gain(0, at) + (slot_e(0, at) * se1) * gain(1, at)
        mx[:, at] = m.astype(BF16).astype(F32) * slot_live
        return acc

    sweep(slot_mix, 0)
    for b in range(S):
        part = mx[:, dslice(b)]
        pkb[0, b] = part[:8].astype(BF16)
        pkb[1, b] = part[8:].astype(BF16)
        pkb[2, b] = hrow[:, dslice(b)].astype(F32)[:8].astype(BF16)
    ph_b = seq_start(lambda to: pkb.at[0, to], landb.at[0, me])
    se2_t2 = pltpu.roll(jnp.broadcast_to(se2, (PK, 128)), PK - C, 0)
    top = slots[4:5, :] + line(se2_t2, 8) + line(sh, 52) + line(se1, 58)
    meta[...] = jnp.broadcast_to(top, (8, 128)) * jnp.where(line16[:8] == 0, 1.0, 0.0)
    ph_m = seq_start(lambda to: meta, mland.at[me])
    mland[me] = meta[...]
    ph_b1 = seq_start(lambda to: pkb.at[1, to], landb.at[1, me])
    ph_b2 = seq_start(lambda to: pkb.at[2, to], landb.at[2, me])
    for k in range(3):
        landb[k, me] = pkb[k, me]
    gather_dp_wait(ph_d2, 1, do)
    seq_wait(ph_b, lambda frm: landb.at[0, frm])
    unpack(1, landb.at[0], 8, 0)
    xr[0, rowslice(d), :] = rows[1, 0:RW, :].astype(BF16)
    ph_x = gather_dp(0, xr)
    ph_da2 = dact(1)
    seq_wait(ph_b1, lambda frm: landb.at[1, frm])
    unpack(1, landb.at[1], 8, 8)
    seq_wait(ph_e, lambda frm: landa.at[1, frm])
    unpack(2, landa.at[1], PK, 0)
    gather_dp_wait(ph_x, 0, xr)
    gsv[0] = gate_up(0)
    act_piece(0)
    spread(act.at[0])
    out = None
    for q in range(CG):
        part = dot_nt(act[0, q, 0], w[0, 2, :, q * PC:(q + 1) * PC])
        out = part if out is None else out + part
    ph = reduce_dp(0, out)
    bulk(0, NC // 8)
    seq_wait(ph_m, lambda frm: mland.at[frm])
    facts = jnp.sum(mland[...], axis=1)

    def fact(k):
        return facts[:, k:k + 1]

    def ov(j, i):
        return fact(16 + j * C + i)

    out = reduce_dp_wait(ph, 0)
    od[0:RW, :] = out.astype(BF16)
    cols = []
    for i in range(C):
        before = rows_at(1, i) + fact(i) * out[i * S:(i + 1) * S]
        before = before.astype(BF16).astype(F32)
        pv[i * S:(i + 1) * S, :] = before
        cols.append(jnp.sum(before * before, axis=1, keepdims=True))
    for j in range(C):
        before = rows_at(1, C + j)
        for i in range(C):
            before = before + (ov(j, i) * fact(i)) * out[i * S:(i + 1) * S]
        before = before.astype(BF16).astype(F32)
        pv[(C + j) * S:(C + j + 1) * S, :] = before
        cols.append(jnp.sum(before * before, axis=1, keepdims=True))
    ph = sums_start(0, cols)
    bulk(NC // 8, 2 * NC // 8)
    gain_h, gain_e = g2[0:1, :], g2[1:2, :]
    scale = lax.rsqrt(sums_wait(ph, 0) + eps_norm)

    for j in range(C):
        unit = pv[(C + j) * S:(C + j + 1) * S, :] * scale[:, C + j:C + j + 1]
        mixed = unit * gain_h + (rows_at(2, C + j) * fact(8 + j)) * gain_e
        od[3 * RW + j * S:3 * RW + (j + 1) * S, :] = mixed.astype(BF16)
    xr[1, rowslice(d), :] = od[3 * RW:4 * RW, :]
    ph = gather_dp(1, xr)
    ph_r0 = send_back(0)
    bulk(2 * NC // 8, 3 * NC // 8)
    gather_dp_wait(ph, 1, xr)
    gsv[1] = gate_up(1, lambda: bulk(3 * NC // 8, NC // 2))
    d_act = dact_wait(ph_da2, 1)
    pre_grads(1, d_act)
    act_piece(1)
    spread(dg.at[1])
    ph = reduce_dp(1, drows(1))
    ph_a2 = spread_piece(act.at[1])
    in_grads(1)
    bulk(NC // 2, 5 * NC // 8)
    back = reduce_dp_wait(ph, 1)
    od[RW:2 * RW, :] = back.astype(BF16)
    cols, keep_u, keep_n = [], [], []
    for i in range(C):
        top = rows_at(0, i)
        for j in range(C):
            top = top + ov(j, i) * back[j * S:(j + 1) * S]
        u = top * gain_h
        unit = pv[i * S:(i + 1) * S, :] * scale[:, i:i + 1]
        keep_u.append(u)
        keep_n.append(unit)
        cols.append(jnp.sum(u * unit, axis=1, keepdims=True))
    ph = sums_start(1, cols)

    bulk(5 * NC // 8, 6 * NC // 8)
    inner = sums_wait(ph, 1)

    for i in range(C):
        back = (keep_u[i] - keep_n[i] * inner[:, i:i + 1]) * scale[:, i:i + 1]
        od[3 * RW + i * S:3 * RW + (i + 1) * S, :] = (back * fact(i)).astype(BF16)
    do[0, rowslice(d), :] = od[3 * RW:4 * RW, :]
    ph = gather_dp(0, do)
    ph_r1 = send_back(1)
    bulk(6 * NC // 8, 7 * NC // 8)
    gather_dp_wait(ph, 0, do)
    ph = dact(0)
    bulk(7 * NC // 8, NC)
    seq_wait(ph_r0, lambda frm: ret.at[0, frm])
    seq_wait(ph_r1, lambda frm: ret.at[1, frm])
    widen(0, prev_sel, 0, prev_w)
    widen(1, dm2_sel, 1, None)
    slot_sh, slot_se1 = rows_pass_1(
        slot_h, slot_e, lambda at: sc[:, at].astype(F32), slot_mask, lambda at: ad[0, :, at], lambda at: ad[1, :, at]
    )

    def early(at, acc):
        collect(0, at, dmx[:, at] * (slot_h(at) * slot_sh), slot_mask)
        collect(1, at, dmx[:, at] * (slot_e(0, at) * slot_se1), slot_mask)
        return acc

    sweep(early, 0)
    d_act = dact_wait(ph, 0)
    pre_grads(0, d_act)
    spread(dg.at[0])
    for b in range(S):
        gsrc[b] = jnp.sum(gacc[:, :, dslice(b)], axis=1)
    ph_g = seq_start(lambda to: gsrc.at[to], gland.at[me])
    gland[me] = gsrc[me]
    ph = reduce_dp(2, drows(0))
    spread_wait(ph_a2, act.at[1])
    down_grad(1)
    down_grad(0)
    in_grads(0)
    back = reduce_dp_wait(ph, 2)
    od[2 * RW:3 * RW, :] = back.astype(BF16)
    ph_r2 = send_back(2)

    seq_wait(ph_b2, lambda frm: landb.at[2, frm])
    unpack(1, landb.at[2], 8, 0)
    late_h = jnp.zeros((S, DS), F32)
    late_e = jnp.zeros((S, DS), F32)
    for i in range(C):
        part = back[i * S:(i + 1) * S]
        late_h = late_h + part * (rows_at(1, i) * fact(52 + i))
        late_e = late_e + part * (rows_at(2, i) * fact(58 + i))
    seq_wait(ph_g, lambda frm: gland.at[frm])
    value = add_up(gland)
    late = jnp.concatenate(
        [jnp.sum(late_h, axis=0, keepdims=True), jnp.sum(late_e, axis=0, keepdims=True), jnp.zeros((2, DS), F32)], 0
    )
    value = value + late
    QS = DS // Q
    for q in range(Q):
        gown[q] = value[:, q * QS:(q + 1) * QS]
    ph_q = dp_start(lambda to: gown.at[to], gland2.at[d])
    gland2[d] = gown[d]

    seq_wait(ph_r2, lambda frm: ret.at[2, frm])
    widen(2, prev_sel, 2, None)

    def slot_store(at, value):
        sls[:, at] = value

    rows_pass_2(slot_h, slot_e, None, slot_sh, slot_se1, lambda at: ad[2, :, at], slot_store)
    back_rows = hop(sls, slr, 2 * NC, before_me)
    back_rows.start()
    dp_wait(ph_q, lambda frm: gland2.at[frm])
    gains[...] = add_up(gland2)

    def finish(c):
        hid_copy(c).wait_send()
        hg_copy(c).wait_send()
        hg_copy(c).wait_recv()

    each_chunk(finish)
    ask_hop.wait_send()
    row_hop.wait_send()
    back_rows.wait()
    wires.drain()


def chain(slots, g2, w, mh, own, ahead, cot, ng, C):
    S, Q, X = lax.axis_size("seq"), lax.axis_size("dp"), lax.axis_size("section")
    DS, HS = w.shape[2], w.shape[3]
    T, D = mh.shape
    RW = C * S
    NR = Q * RW
    CG = S // Q
    PC = HS // CG
    NC = T // PK
    vm = pltpu.VMEM
    phases = 32
    return pl.pallas_call(
        functools.partial(chain_kernel, S, Q, X, C, D),
        out_shape=(
            jax.ShapeDtypeStruct(w.shape, BF16),
            jax.ShapeDtypeStruct((T, D), BF16),
            jax.ShapeDtypeStruct((PK, D), BF16),
            jax.ShapeDtypeStruct((4, DS // Q), F32),
            jax.ShapeDtypeStruct((8, 128), F32),
        ),
        in_specs=[pl.BlockSpec(memory_space=vm)] * 8,
        out_specs=(pl.BlockSpec(memory_space=vm),) * 5,
        scratch_shapes=[
            vm((T + PK, D), BF16),
            vm((PK, D), BF16),
            vm((PK, D), BF16),
            vm((2, PK, D), BF16),
            vm((PK, D), BF16),
            vm((2, S, PK, DS), BF16),
            vm((3, S, 8, DS), BF16),
            vm((2, S, PK, DS), BF16),
            vm((3, S, 8, DS), BF16),
            vm((8, 128), F32),
            vm((S, 8, 128), F32),
            vm((3, S * PK, DS), F32),
            vm((3, S, 8, DS), BF16),
            vm((3, S, 8, DS), BF16),
            vm((2, NR, DS), BF16),
            vm((2, NR, DS), BF16),
            vm((2, CG, 2, NR, PC), BF16),
            vm((2, S // 2, 2, RW, PC), BF16),
            vm((2, S // 2, 2, RW, PC), BF16),
            vm((2, S // 2, 2, RW, PC), BF16),
            vm((CG, 2, NR, PC), F32),
            vm((2, CG, 1, NR, PC), BF16),
            vm((2, S, 1, RW, PC), BF16),
            vm((2, CG, 1, NR, PC), BF16),
            vm((2, CG, 2, NR, PC), BF16),
            vm((3, NR, DS), BF16),
            vm((3, Q, RW, DS), BF16),
            vm((2 * RW, DS), F32),
            vm((2, S, 128), F32),
            vm((2, S, S, 128), F32),
            vm((4 * RW, DS), BF16),
            vm((2, 2, RW, PC), F32),
            vm((T, D), BF16),
            vm((T, D), BF16),
            vm((2 * PK, D), BF16),
            vm((PK, D), F32),
            vm((PK, D), F32),
            vm((3, PK, D), F32),
            vm((PK, D), BF16),
            vm((4, 8, D), F32),
            vm((S, 4, DS), F32),
            vm((S, 4, DS), F32),
            vm((Q, 4, DS // Q), F32),
            vm((Q, 4, DS // Q), F32),
            pltpu.SemaphoreType.DMA((phases, S)),
            pltpu.SemaphoreType.DMA((phases, S)),
            pltpu.SemaphoreType.DMA((2 * NC + 3,)),
            pltpu.SemaphoreType.DMA((2 * NC + 3,)),
        ],
        compiler_params=pltpu.CompilerParams(
            collective_id=0, has_side_effects=True, vmem_limit_bytes=60 * 1024 * 1024
        ),
        name="expert_chain",
    )(slots, g2, w, mh, own, ahead, cot, ng)


def pick(index, count):
    return (index[:, None] == jnp.arange(count, dtype=jnp.int32)[None, :]).astype(BF16)


def local(main_hidden, embedded, cotangent, slot_token, slot_count, route_gate, norm_gain, w):
    S = lax.axis_size("seq")
    me = lax.axis_index("seq")
    tokens_here, D = main_hidden.shape[2:]
    C = slot_token.shape[3]
    DS = D // S
    tok = slot_token[0, 0]
    live = (jnp.arange(C, dtype=jnp.int32)[None, :] < slot_count[0, 0]).astype(F32)
    weight = route_gate[0, 0] * live
    own, cot, mh = embedded[0, 0], cotangent[0, 0], main_hidden[0, 0]
    ahead = from_ahead(own[:2], "seq", 1)
    same = (tok[1][:, None] == tok[0][None, :]).astype(F32) * live[1][:, None] * live[0][None, :]
    fresh = jnp.stack([live[0], live[1] * (1.0 - jnp.max(same, axis=1))]).reshape(-1)
    flat = tok.reshape(-1)

    def lanes(*parts):
        row = jnp.concatenate(parts)
        return jnp.pad(row, (0, 128 - row.shape[0]))

    slots = jnp.stack([
        lanes(flat.astype(F32)),
        lanes(live.reshape(-1)),
        lanes(weight.reshape(-1)),
        lanes(fresh),
        lanes(weight[0], jnp.zeros((16 - C,), F32), same.reshape(-1)),
        lanes(tok[1].astype(F32)),
        lanes(live[1]),
        lanes(flat[:1].astype(F32) * 0.0),
    ])
    g2 = lax.dynamic_slice(norm_gain[1], (0, me * DS), (2, DS))
    g2 = jnp.concatenate([g2, jnp.zeros((6, DS), F32)], 0)
    ahead = jnp.pad(ahead, ((0, PK - 2), (0, 0)))
    ng = norm_gain.reshape(4, D)

    expert_grad, grads, slot_grads, total, asks = chain(slots, g2, w, mh, own, ahead, cot, ng, C)
    back_to = jnp.where(asks[3, :2 * C] > 0.5, asks[0, :2 * C], -1.0).astype(jnp.int32)
    put = pick(back_to, tokens_here)
    hit = jnp.sum(put.astype(F32), axis=0)
    placed = lax.dot_general(
        put, slot_grads[:2 * C], (((0,), (0,)), ((), ())), preferred_element_type=F32
    )
    hidden_grad = jnp.where(hit[:, None] > 0.5, placed.astype(BF16), grads)
    return (hidden_grad[None, None], expert_grad[None], total.reshape(1, 2, 2, -1))


def solution(mesh):
    return jax.shard_map(
        local,
        mesh=mesh,
        in_specs=(
            P("section", "dp", "seq", None),
            P("section", "dp", "seq", None),
            P("section", "dp", "seq", None),
            P("section", "dp", None, "seq"),
            P("section", "dp", None, "seq"),
            P("section", "dp", None, "seq"),
            P(),
            P(None, None, "seq", "dp"),
        ),
        out_specs=(
            P("section", "dp", "seq", None),
            P("section", None, None, "seq", "dp"),
            P("section", None, None, ("seq", "dp")),
        ),
        check_vma=False,
    )
```

```python
import functools

import jax
import jax.numpy as jnp
from jax import lax
from jax.experimental import pallas as pl
from jax.experimental.pallas import tpu as pltpu
from jax.sharding import PartitionSpec as P

eps_norm = 1e-06
MESH = pl.DeviceIdType.MESH
F32 = jnp.float32
BF16 = jnp.bfloat16
PK = 16


def from_behind(value, axis, steps):
    count = lax.axis_size(axis)
    pairs = [(source, (source + steps) % count) for source in range(count)]
    return lax.ppermute(value, axis, pairs)


def from_ahead(array, axis, by):
    size = lax.axis_size(axis)
    pairs = [(i, i - by) for i in range(size) if 0 <= i - by < size]
    return lax.ppermute(array, axis, pairs)


def normed(value):
    wide = value.astype(F32)
    scale = lax.rsqrt(jnp.mean(wide * wide, axis=-1, keepdims=True) + eps_norm)
    return (wide * scale, scale)


def norm_back(grad, unit, scale):
    inner = jnp.mean(grad * unit, axis=-1, keepdims=True)
    return (grad - unit * inner) * scale


def dot_nn(a, b):
    return lax.dot_general(a, b, (((1,), (0,)), ((), ())), preferred_element_type=F32)


def dot_nt(a, b):
    return lax.dot_general(a, b, (((1,), (1,)), ((), ())), preferred_element_type=F32)


def dot_tn(a, b):
    return lax.dot_general(a, b, (((0,), (0,)), ((), ())), preferred_element_type=F32)


class Wires:
    def __init__(self, send, recv):
        self.send, self.recv = send, recv
        self.phases = 0
        self.open = []
        self.singles = []

    def copy(self, src, dst, ph, slot_s, slot_r, axis, to):
        return pltpu.make_async_remote_copy(
            src_ref=src,
            dst_ref=dst,
            send_sem=self.send.at[ph, slot_s],
            recv_sem=self.recv.at[ph, slot_r],
            device_id={axis: to},
            device_id_type=MESH,
        )

    def start(self, axis, size, me, src_of, dst):
        ph = self.phases
        self.phases += 1

        def body(o, c):
            to = lax.rem(me + o, size)
            self.copy(src_of(to), dst, ph, o, me, axis, to).start()
            return c

        lax.fori_loop(1, size, body, 0)
        self.open.append((ph, axis, size, me, src_of))
        return ph

    def wait(self, ph, axis, size, me, dst_of):
        def body(o, c):
            frm = lax.rem(me + o, size)
            self.copy(dst_of(frm), dst_of(frm), ph, o, frm, axis, frm).wait_recv()
            return c

        lax.fori_loop(1, size, body, 0)

    def phase(self):
        self.phases += 1
        return self.phases - 1

    def one(self, src, dst, ph, slot_s, slot_r, axis, to):
        copy = self.copy(src, dst, ph, slot_s, slot_r, axis, to)
        copy.start()
        self.singles.append(copy)

    def drain(self):
        for copy in self.singles:
            copy.wait_send()
        for ph, axis, size, me, src_of in self.open:

            def body(o, c):
                to = lax.rem(me + o, size)
                self.copy(src_of(to), src_of(to), ph, o, me, axis, to).wait_send()
                return c

            lax.fori_loop(1, size, body, 0)


def greet(axes, sections=()):
    barrier = pltpu.get_barrier_semaphore()
    total = 0
    for axis, size, me in axes:

        def body(o, c):
            to = lax.rem(me + o, size)
            pl.semaphore_signal(barrier, inc=1, device_id={axis: to}, device_id_type=MESH)
            return c

        lax.fori_loop(1, size, body, 0)
        total += size - 1
    for to in sections:
        pl.semaphore_signal(barrier, inc=1, device_id={"section": to}, device_id_type=MESH)
        total += 1
    return lambda: pl.semaphore_wait(barrier, total)


def chain_kernel(S, Q, X, C, D, slots, w, mh, own, ahead, cot, ng, eg, hg, slr, gains, asks,
                 ext, hsend, hrow, se, sc, pka, pkb, landa, landb, meta, mland, rows, ret, rb, xr, do, gu, lg, ly, cmb, gf, da,
                 ld, act, dg, op, lo, pv, ss, ssl, od, gsv, hid, hgs, es, mx, dmx, dmu, ad, sls, gacc, gsrc, gland,
                 gown, gland2, send, recv, xsend, xrecv):
    me = lax.axis_index("seq")
    d = lax.axis_index("dp")
    sec = lax.axis_index("section")
    after, before_me = lax.rem(sec + 1, X), lax.rem(sec + X - 1, X)
    DS, HS = w.shape[2], w.shape[3]
    RW = C * S
    CG = S // Q
    PC = HS // CG
    rg, cg = me // CG, lax.rem(me, CG)
    wires = Wires(send, recv)

    def rowslice(g):
        return pl.ds(pl.multiple_of(g * RW, 32 if RW % 32 == 0 else 8), RW)

    def piece_of(ref):
        def src(to):
            return ref.at[to % CG, :, rowslice(to // CG), :]
        return src

    def seq_start(src_of, dst):
        return wires.start("seq", S, me, src_of, dst)

    def seq_wait(ph, dst_of):
        wires.wait(ph, "seq", S, me, dst_of)

    def dp_start(src_of, dst):
        return wires.start("dp", Q, d, src_of, dst)

    def dp_wait(ph, dst_of):
        wires.wait(ph, "dp", Q, d, dst_of)

    barrier_axes = (("seq", S, me), ("dp", Q, d))
    greet_all = greet(barrier_axes, (after, before_me))
    NC = mh.shape[0] // PK
    T = mh.shape[0]

    def chunk(c):
        return pl.ds(pl.multiple_of(c * PK, PK), PK)

    def hop(src, dst, slot, to):
        return pltpu.make_async_remote_copy(
            src_ref=src, dst_ref=dst, send_sem=xsend.at[slot], recv_sem=xrecv.at[slot],
            device_id={"section": to}, device_id_type=MESH,
        )

    def hid_copy(c):
        return hop(mh.at[chunk(c), :], hid.at[chunk(c), :], c, after)

    def hg_copy(c):
        return hop(hgs.at[chunk(c), :], hg.at[chunk(c), :], NC + c, before_me)

    ask_hop = hop(slots, asks, 2 * NC + 1, before_me)
    row_hop = hop(hsend, hrow, 2 * NC + 2, after)

    def each_chunk(fn, first=0, last=NC):
        def body(c, carry):
            fn(c)
            return carry

        lax.fori_loop(first, last, body, 0)

    slot_row, live_row, weight_row, fresh_row = (slots[k:k + 1, :] for k in range(4))
    lane16 = lax.broadcasted_iota(jnp.int32, (PK, 128), 1)
    line16 = lax.broadcasted_iota(jnp.int32, (PK, 128), 0)
    line1 = lax.broadcasted_iota(jnp.int32, (PK, 1), 0)

    def column(row):
        return jnp.sum(jnp.where(lane16 == line16, row, 0.0), axis=1, keepdims=True)

    def line(col, first):
        return jnp.sum(jnp.where((lane16 == line16 + first) & (line16 < C), col, 0.0), axis=0, keepdims=True)

    slot_tok, slot_live, slot_w = column(slot_row), column(live_row), column(weight_row)

    ext[0:T, :] = own[...]
    ext[T:T + PK, :] = jnp.zeros((PK, D), BF16)
    ext[T:T + 2, :] = ahead[...]
    wide = lax.broadcasted_iota(jnp.int32, (PK, T + PK), 1).astype(F32)
    for k in range(2):
        se[k] = dot_nn(jnp.where(wide == slot_tok + (k + 1.0), 1.0, 0.0).astype(BF16), ext[...]).astype(BF16)
    sc[...] = dot_nn(jnp.where(lane16.astype(F32) == slot_tok, 1.0, 0.0).astype(BF16), cot[...]).astype(BF16)

    greet_all()
    ask_hop.start()

    first_rows = line1 < C

    def dslice(b):
        return slice(b * DS, (b + 1) * DS)

    cot_w = jnp.where(first_rows, 1.0, slot_w)
    for b in range(S):
        pka[0, b] = (sc[:, dslice(b)].astype(F32) * cot_w).astype(BF16)
    ph_a = seq_start(lambda to: pka.at[0, to], landa.at[0, me])
    landa[0, me] = pka[0, me]
    e_live = jnp.where(first_rows, 1.0, slot_live)
    for b in range(S):
        both = jnp.where(first_rows, se[0, :, dslice(b)].astype(F32), se[1, :, dslice(b)].astype(F32))
        pka[1, b] = (both * e_live).astype(BF16)

    ask_hop.wait_recv()
    asked = jnp.sum(jnp.where(lane16 == line16, asks[0:1, :], 0.0), axis=1, keepdims=True)
    hsend[...] = dot_nn(jnp.where(lane16.astype(F32) == asked, 1.0, 0.0).astype(BF16), mh[...]).astype(BF16)
    row_hop.start()
    each_chunk(lambda c: hid_copy(c).start())
    ph_e = seq_start(lambda to: pka.at[1, to], landa.at[1, me])
    landa[1, me] = pka[1, me]

    def unpack(k, land, height, first):
        n = S * height
        r = lax.broadcasted_iota(jnp.int32, (n, n), 0)
        c = lax.broadcasted_iota(jnp.int32, (n, n), 1)
        perm = jnp.where(c == (r % S) * height + r // S, 1.0, 0.0).astype(BF16)
        flat = land[...].astype(F32).reshape(n, DS).astype(BF16)
        rows[k, first * S:(first + height) * S, :] = dot_nn(perm, flat)

    def rows_at(k, slot):
        return rows[k, slot * S:(slot + 1) * S, :]

    def gather_dp(k, dst):
        return dp_start(lambda to: dst.at[k, rowslice(d), :], dst.at[k, rowslice(d), :])

    def gather_dp_wait(ph, k, dst):
        dp_wait(ph, lambda frm: dst.at[k, rowslice(frm), :])

    def gate_up(k, work=None):
        far = [h for h in reversed(near)] + [0]
        for half in range(2):
            full = dot_nn(xr[k], w[k, half])
            for q in range(CG):
                cols = slice(q * PC, (q + 1) * PC)
                gf[q, half] = full[:, cols]
                gu[k, q, half] = full[:, cols].astype(BF16)

        def piece(ref, t):
            return ref.at[lax.rem(t, CG), :, rowslice(t // CG), :]

        ph = wires.phase()
        for h in far:
            z = lax.rem(zme + h, n)
            wires.one(piece(gu.at[k], at_z(h, 1 - yme)), ly.at[k, z], ph, h, h, "seq", yn)
        ph2 = wires.phase()
        for h in far:
            z = lax.rem(zme + h, n)
            wires.copy(ly.at[k, z], ly.at[k, z], ph, h, h, "seq", yn).wait_recv()
            both = piece(gf, at_z(h, yme))[...] + ly[k, z].astype(F32)
            if h == 0:
                total = both
            else:
                cmb[k, z] = both.astype(BF16)
                wires.one(cmb.at[k, z], lg.at[k, zme], ph2, h, h, "seq", at_z(h, yme))
        if work is not None:
            work()
        for h in near:
            z = lax.rem(zme + n - h, n)
            wires.copy(lg.at[k, z], lg.at[k, z], ph2, h, h, "seq", at_z(n - h, yme)).wait_recv()
            total = total + lg[k, z].astype(F32)
        return total

    def add_up(ref):
        total = ref[0].astype(F32)
        for b in range(1, ref.shape[0]):
            total = total + ref[b].astype(F32)
        return total

    def dact(k):
        full = dot_nn(do[k], w[k, 2]).astype(BF16)
        for q in range(CG):
            da[k, q, 0] = full[:, q * PC:(q + 1) * PC]
        ph = seq_start(piece_of(da.at[k]), ld.at[k, me])
        ld[k, me] = da[k, cg, :, rowslice(rg), :]
        return ph

    def dact_wait(ph, k):
        seq_wait(ph, lambda frm: ld.at[k, frm])
        return add_up(ld.at[k])[0]

    def spread_piece(ref):
        mine = ref.at[cg, :, rowslice(rg), :]
        return seq_start(lambda to: mine, mine)

    n = S // 2
    zme, yme = me // 2, lax.rem(me, 2)
    yn = me + 1 - 2 * yme
    near = sorted(range(1, n), key=lambda h: (min(h, n - h), h))

    def at_z(h, parity):
        return 2 * lax.rem(zme + h, n) + parity

    def spread(ref, work=None):
        def piece(t):
            return ref.at[lax.rem(t, CG), :, rowslice(t // CG), :]

        ph = wires.phase()
        mine = piece(me)
        for h in reversed(near):
            wires.one(mine, mine, ph, h, h, "seq", at_z(h, yme))
        wires.one(mine, mine, ph, 0, n, "seq", yn)
        for h in near:
            frm = at_z(n - h, yme)
            wires.copy(piece(frm), piece(frm), ph, h, h, "seq", frm).wait_recv()
            wires.one(piece(frm), piece(frm), ph, n + h, n + h, "seq", yn)
        if work is not None:
            work()
        for h in [0] + near:
            frm = at_z(n - h, 1 - yme)
            wires.copy(piece(frm), piece(frm), ph, n + h, n + h, "seq", yn).wait_recv()

    def spread_wait(ph, ref):
        seq_wait(ph, lambda frm: ref.at[lax.rem(frm, CG), :, rowslice(frm // CG), :])

    def reduce_dp(n, full):
        op[n] = full.astype(BF16)
        ph = dp_start(lambda to: op.at[n, rowslice(to), :], lo.at[n, d])
        lo[n, d] = op[n, rowslice(d), :]
        return ph

    def reduce_dp_wait(ph, n):
        dp_wait(ph, lambda frm: lo.at[n, frm])
        return add_up(lo.at[n])

    def drows(k):
        total = None
        for q in range(CG):
            cols = slice(q * PC, (q + 1) * PC)
            part = dot_nt(dg[k, q, 0], w[k, 0, :, cols]) + dot_nt(dg[k, q, 1], w[k, 1, :, cols])
            total = part if total is None else total + part
        return total

    laneS = lax.broadcasted_iota(jnp.int32, (S, 128), 1)
    lineS = lax.broadcasted_iota(jnp.int32, (S, 128), 0)

    def to_row(cols):
        total = jnp.zeros((1, 128), F32)
        for i, col in enumerate(cols):
            total = total + jnp.sum(jnp.where(laneS == lineS + i * S, col, 0.0), axis=0, keepdims=True)
        return total

    def to_col(row, i):
        return jnp.sum(jnp.where(laneS == lineS + i * S, row, 0.0), axis=1, keepdims=True)

    def sums_start(k, cols):
        ss[k, 0:1, :] = to_row(cols[:C])
        ss[k, 1:2, :] = to_row(cols[C:])
        ph = seq_start(lambda to: ss.at[k], ssl.at[k, me])
        ssl[k, me] = ss[k]
        return ph

    def sums_wait(ph, n):
        seq_wait(ph, lambda frm: ssl.at[n, frm])
        return add_up(ssl.at[n]) * (1.0 / D)

    def pre_grads(k, d_act):
        gate, up = gsv[k, 0], gsv[k, 1]
        sig = 1.0 / (1.0 + jnp.exp(-gate))
        dg[k, cg, 0, rowslice(rg), :] = (d_act * up * sig * (1.0 + gate * (1.0 - sig))).astype(BF16)
        dg[k, cg, 1, rowslice(rg), :] = (d_act * (gate * sig)).astype(BF16)

    def act_piece(k):
        gate, up = gsv[k, 0], gsv[k, 1]
        act[k, cg, 0, rowslice(rg), :] = (gate / (1.0 + jnp.exp(-gate)) * up).astype(BF16)

    def in_grads(k):
        for half in range(2):
            for q in range(CG):
                eg[k, half, :, q * PC:(q + 1) * PC] = dot_tn(xr[k], dg[k, q, half]).astype(BF16)

    def down_grad(k):
        for q in range(CG):
            eg[k, 2, :, q * PC:(q + 1) * PC] = dot_tn(do[k], act[k, q, 0]).astype(BF16)

    LB = 256
    NB = D // LB

    def lanes(b):
        return pl.ds(pl.multiple_of(b * LB, LB), LB)

    def sweep(fn, count):
        zero = jnp.zeros((PK, LB), F32)
        total = lax.fori_loop(0, NB, lambda b, acc: fn(lanes(b), acc), (zero,) * count)
        return [jnp.sum(t, axis=1, keepdims=True) * (1.0 / D) for t in total]

    def gain(k, at):
        return ng[k // 2, k % 2:k % 2 + 1, at]

    def collect(k, at, value, mask):
        value = value * mask
        gacc[k, :, at] += value[:8] + value[8:]

    def rows_pass_1(h_at, e_at, c_at, mask, prev_add, dm2_add):
        def squares(at, acc):
            h, e1, e2 = h_at(at), e_at(0, at), e_at(1, at)
            return acc[0] + h * h, acc[1] + e1 * e1, acc[2] + e2 * e2

        sh, se1, se2 = [lax.rsqrt(v + eps_norm) for v in sweep(squares, 3)]

        def mix(at, acc):
            m = (h_at(at) * sh) * gain(0, at) + (e_at(0, at) * se1) * gain(1, at)
            m = m.astype(BF16).astype(F32)
            if prev_add is not None:
                m = (m + prev_add(at)).astype(BF16).astype(F32)
            mx[:, at] = m
            return (acc[0] + m * m,)

        s2, = [lax.rsqrt(v + eps_norm) for v in sweep(mix, 1)]

        def top(at, acc):
            n2 = mx[:, at] * s2
            dm2 = c_at(at)
            if dm2_add is not None:
                dm2 = dm2 + dm2_add(at)
            collect(2, at, dm2 * n2, mask)
            collect(3, at, dm2 * (e_at(1, at) * se2), mask)
            u = dm2 * gain(2, at)
            dmx[:, at] = u
            return (acc[0] + u * n2,)

        inner, = sweep(top, 1)

        def middle(at, acc):
            dmx[:, at] = (dmx[:, at] - (mx[:, at] * s2) * inner) * s2
            return acc

        sweep(middle, 0)
        return sh, se1

    def rows_pass_2(h_at, e_at, mask, sh, se1, dm1_add, store):
        def low(at, acc):
            dm1 = dmx[:, at]
            if dm1_add is not None:
                dm1 = dm1 + dm1_add(at)
            n1 = h_at(at) * sh
            if mask is not None:
                collect(0, at, dm1 * n1, mask)
                collect(1, at, dm1 * (e_at(0, at) * se1), mask)
            u = dm1 * gain(0, at)
            dmu[:, at] = u
            return (acc[0] + u * n1,)

        inner, = sweep(low, 1)

        def last(at, acc):
            store(at, (dmu[:, at] - (h_at(at) * sh) * inner) * sh)
            return acc

        sweep(last, 0)

    def bulk_chunk(c):
        hid_copy(c).wait_recv()
        r = lax.broadcasted_iota(jnp.int32, (2 * PK, 2 * PK), 0)
        k = lax.broadcasted_iota(jnp.int32, (2 * PK, 2 * PK), 1)
        shift = jnp.where(k == r % PK + 1 + r // PK, 1.0, 0.0).astype(BF16)
        es[...] = dot_nn(shift, ext[pl.ds(pl.multiple_of(c * PK, PK), 2 * PK), :]).astype(BF16)
        place = (line16 + c * PK).astype(F32)
        hit = jnp.sum(jnp.where(place == slot_row, live_row, 0.0), axis=1, keepdims=True)
        mask = jnp.where(hit > 0.5, 0.0, 1.0)

        def h_at(at):
            return hid[chunk(c), at].astype(F32)

        def e_at(k, at):
            return es[k * PK:(k + 1) * PK, at].astype(F32)

        sh, se1 = rows_pass_1(h_at, e_at, lambda at: cot[chunk(c), at].astype(F32), mask, None, None)

        def store(at, value):
            hgs[chunk(c), at] = value.astype(BF16)

        rows_pass_2(h_at, e_at, mask, sh, se1, None, store)
        hg_copy(c).start()

    def bulk(first, last):
        each_chunk(bulk_chunk, first, last)

    gacc[...] = jnp.zeros_like(gacc)

    def slot_h(at):
        return hrow[:, at].astype(F32)

    def slot_e(k, at):
        return se[k, :, at].astype(F32)

    slot_mask = column(fresh_row)
    same_tok = jnp.where(slot_tok == slot_row, live_row, 0.0)
    prev_sel = jnp.where(lane16 < C, same_tok, 0.0)
    prev_w = jnp.sum(prev_sel * weight_row, axis=1, keepdims=True)
    dm2_tok = jnp.where(slot_tok == slots[5:6, :], slots[6:7, :], 0.0)
    dm2_sel = jnp.where(lane16 < C, dm2_tok, 0.0)

    def widen(n, sel, k, scale_by):
        for b in range(S):
            part = dot_nn(sel[:, :8].astype(BF16), ret[k, b])
            if scale_by is not None:
                part = part * scale_by
            ad[n, :, dslice(b)] = part

    def send_back(k):
        r = lax.broadcasted_iota(jnp.int32, (S * 8, RW), 0)
        c = lax.broadcasted_iota(jnp.int32, (S * 8, RW), 1)
        perm = jnp.where(c == (r % 8) * S + r // 8, 1.0, 0.0).astype(BF16)
        rb[k] = dot_nn(perm, od[k * RW:(k + 1) * RW, :]).reshape(S, 8, DS).astype(BF16)
        ph = seq_start(lambda to: rb.at[k, to], ret.at[k, me])
        ret[k, me] = rb[k, me]
        return ph

    seq_wait(ph_a, lambda frm: landa.at[0, frm])
    unpack(0, landa.at[0], PK, 0)
    do[1, rowslice(d), :] = rows[0, RW:2 * RW, :].astype(BF16)
    ph_d2 = gather_dp(1, do)

    row_hop.wait_recv()

    def slot_squares(at, acc):
        h, e1, e2 = slot_h(at), slot_e(0, at), slot_e(1, at)
        return acc[0] + h * h, acc[1] + e1 * e1, acc[2] + e2 * e2

    sh, se1, se2 = [lax.rsqrt(v + eps_norm) for v in sweep(slot_squares, 3)]

    def slot_mix(at, acc):
        m = (slot_h(at) * sh) * gain(0, at) + (slot_e(0, at) * se1) * gain(1, at)
        mx[:, at] = m.astype(BF16).astype(F32) * slot_live
        return acc

    sweep(slot_mix, 0)
    for b in range(S):
        part = mx[:, dslice(b)]
        pkb[0, b] = part[:8].astype(BF16)
        pkb[1, b] = part[8:].astype(BF16)
        pkb[2, b] = hrow[:, dslice(b)].astype(F32)[:8].astype(BF16)
    ph_b = seq_start(lambda to: pkb.at[0, to], landb.at[0, me])
    se2_t2 = pltpu.roll(jnp.broadcast_to(se2, (PK, 128)), PK - C, 0)
    top = slots[4:5, :] + line(se2_t2, 8) + line(sh, 52) + line(se1, 58)
    meta[...] = jnp.broadcast_to(top, (8, 128)) * jnp.where(line16[:8] == 0, 1.0, 0.0)
    ph_m = seq_start(lambda to: meta, mland.at[me])
    mland[me] = meta[...]
    ph_b1 = seq_start(lambda to: pkb.at[1, to], landb.at[1, me])
    ph_b2 = seq_start(lambda to: pkb.at[2, to], landb.at[2, me])
    for k in range(3):
        landb[k, me] = pkb[k, me]
    gather_dp_wait(ph_d2, 1, do)
    seq_wait(ph_b, lambda frm: landb.at[0, frm])
    unpack(1, landb.at[0], 8, 0)
    xr[0, rowslice(d), :] = rows[1, 0:RW, :].astype(BF16)
    ph_x = gather_dp(0, xr)
    ph_da2 = dact(1)
    seq_wait(ph_b1, lambda frm: landb.at[1, frm])
    unpack(1, landb.at[1], 8, 8)
    seq_wait(ph_e, lambda frm: landa.at[1, frm])
    unpack(2, landa.at[1], PK, 0)
    gather_dp_wait(ph_x, 0, xr)
    gsv[0] = gate_up(0)
    act_piece(0)
    spread(act.at[0])
    out = None
    for q in range(CG):
        part = dot_nt(act[0, q, 0], w[0, 2, :, q * PC:(q + 1) * PC])
        out = part if out is None else out + part
    ph = reduce_dp(0, out)
    bulk(0, NC // 8)
    seq_wait(ph_m, lambda frm: mland.at[frm])
    facts = jnp.sum(mland[...], axis=1)

    def fact(k):
        return facts[:, k:k + 1]

    def ov(j, i):
        return fact(16 + j * C + i)

    out = reduce_dp_wait(ph, 0)
    od[0:RW, :] = out.astype(BF16)
    cols = []
    for i in range(C):
        before = rows_at(1, i) + fact(i) * out[i * S:(i + 1) * S]
        before = before.astype(BF16).astype(F32)
        pv[i * S:(i + 1) * S, :] = before
        cols.append(jnp.sum(before * before, axis=1, keepdims=True))
    for j in range(C):
        before = rows_at(1, C + j)
        for i in range(C):
            before = before + (ov(j, i) * fact(i)) * out[i * S:(i + 1) * S]
        before = before.astype(BF16).astype(F32)
        pv[(C + j) * S:(C + j + 1) * S, :] = before
        cols.append(jnp.sum(before * before, axis=1, keepdims=True))
    ph = sums_start(0, cols)
    bulk(NC // 8, 2 * NC // 8)
    gain_h, gain_e = jnp.zeros((1, DS), F32), jnp.zeros((1, DS), F32)
    for b in range(S):
        gain_h = gain_h + jnp.where(me == b, ng[1, 0:1, dslice(b)], 0.0)
        gain_e = gain_e + jnp.where(me == b, ng[1, 1:2, dslice(b)], 0.0)
    scale = lax.rsqrt(sums_wait(ph, 0) + eps_norm)

    for j in range(C):
        unit = pv[(C + j) * S:(C + j + 1) * S, :] * to_col(scale[1:2], j)
        mixed = unit * gain_h + (rows_at(2, C + j) * fact(8 + j)) * gain_e
        od[3 * RW + j * S:3 * RW + (j + 1) * S, :] = mixed.astype(BF16)
    xr[1, rowslice(d), :] = od[3 * RW:4 * RW, :]
    ph = gather_dp(1, xr)
    ph_r0 = send_back(0)
    bulk(2 * NC // 8, 3 * NC // 8)
    gather_dp_wait(ph, 1, xr)
    gsv[1] = gate_up(1, lambda: bulk(3 * NC // 8, NC // 2))
    d_act = dact_wait(ph_da2, 1)
    pre_grads(1, d_act)
    act_piece(1)
    spread(dg.at[1])
    ph = reduce_dp(1, drows(1))
    ph_a2 = spread_piece(act.at[1])
    in_grads(1)
    bulk(NC // 2, 5 * NC // 8)
    back = reduce_dp_wait(ph, 1)
    od[RW:2 * RW, :] = back.astype(BF16)
    cols, keep_u, keep_n = [], [], []
    for i in range(C):
        top = rows_at(0, i)
        for j in range(C):
            top = top + ov(j, i) * back[j * S:(j + 1) * S]
        u = top * gain_h
        unit = pv[i * S:(i + 1) * S, :] * to_col(scale[0:1], i)
        keep_u.append(u)
        keep_n.append(unit)
        cols.append(jnp.sum(u * unit, axis=1, keepdims=True))
    ph = sums_start(1, cols)

    bulk(5 * NC // 8, 6 * NC // 8)
    inner = sums_wait(ph, 1)

    for i in range(C):
        back = (keep_u[i] - keep_n[i] * to_col(inner[0:1], i)) * to_col(scale[0:1], i)
        od[3 * RW + i * S:3 * RW + (i + 1) * S, :] = (back * fact(i)).astype(BF16)
    do[0, rowslice(d), :] = od[3 * RW:4 * RW, :]
    ph = gather_dp(0, do)
    ph_r1 = send_back(1)
    bulk(6 * NC // 8, 7 * NC // 8)
    gather_dp_wait(ph, 0, do)
    ph = dact(0)
    bulk(7 * NC // 8, NC)
    seq_wait(ph_r0, lambda frm: ret.at[0, frm])
    seq_wait(ph_r1, lambda frm: ret.at[1, frm])
    widen(0, prev_sel, 0, prev_w)
    widen(1, dm2_sel, 1, None)
    slot_sh, slot_se1 = rows_pass_1(
        slot_h, slot_e, lambda at: sc[:, at].astype(F32), slot_mask, lambda at: ad[0, :, at], lambda at: ad[1, :, at]
    )

    def early(at, acc):
        collect(0, at, dmx[:, at] * (slot_h(at) * slot_sh), slot_mask)
        collect(1, at, dmx[:, at] * (slot_e(0, at) * slot_se1), slot_mask)
        return acc

    sweep(early, 0)

    def early_store(at, value):
        sls[1, :, at] = value[8:].astype(BF16)

    back_early = hop(sls.at[1], slr.at[1], 2 * NC + 3, before_me)
    back_rows = hop(sls.at[0], slr.at[0], 2 * NC, before_me)
    d_act = dact_wait(ph, 0)
    pre_grads(0, d_act)
    spread(dg.at[0])
    for b in range(S):
        gsrc[b] = jnp.sum(gacc[:, :, dslice(b)], axis=1)
    ph_g = seq_start(lambda to: gsrc.at[to], gland.at[me])
    gland[me] = gsrc[me]
    ph = reduce_dp(2, drows(0))
    rows_pass_2(slot_h, slot_e, None, slot_sh, slot_se1, None, early_store)
    back_early.start()
    spread_wait(ph_a2, act.at[1])
    down_grad(1)
    down_grad(0)
    in_grads(0)
    back = reduce_dp_wait(ph, 2)
    od[2 * RW:3 * RW, :] = back.astype(BF16)
    ph_r2 = send_back(2)

    seq_wait(ph_b2, lambda frm: landb.at[2, frm])
    unpack(1, landb.at[2], 8, 0)
    late_h = jnp.zeros((S, DS), F32)
    late_e = jnp.zeros((S, DS), F32)
    for i in range(C):
        part = back[i * S:(i + 1) * S]
        late_h = late_h + part * (rows_at(1, i) * fact(52 + i))
        late_e = late_e + part * (rows_at(2, i) * fact(58 + i))
    seq_wait(ph_g, lambda frm: gland.at[frm])
    value = add_up(gland)
    late = jnp.concatenate(
        [jnp.sum(late_h, axis=0, keepdims=True), jnp.sum(late_e, axis=0, keepdims=True), jnp.zeros((2, DS), F32)], 0
    )
    value = value + late
    QS = DS // Q
    for q in range(Q):
        gown[q] = value[:, q * QS:(q + 1) * QS]
    ph_q = dp_start(lambda to: gown.at[to], gland2.at[d])
    gland2[d] = gown[d]

    seq_wait(ph_r2, lambda frm: ret.at[2, frm])
    widen(2, prev_sel, 2, None)

    def slot_store(at, value):
        sls[0, :, at] = value[:8].astype(BF16)

    rows_pass_2(slot_h, slot_e, None, slot_sh, slot_se1, lambda at: ad[2, :, at], slot_store)
    back_rows.start()
    dp_wait(ph_q, lambda frm: gland2.at[frm])
    gains[...] = add_up(gland2)

    def finish(c):
        hid_copy(c).wait_send()
        hg_copy(c).wait_send()
        hg_copy(c).wait_recv()

    each_chunk(finish)
    ask_hop.wait_send()
    row_hop.wait_send()
    back_rows.wait()
    back_early.wait()
    wires.drain()


def chain(slots, w, mh, own, ahead, cot, ng, C):
    S, Q, X = lax.axis_size("seq"), lax.axis_size("dp"), lax.axis_size("section")
    DS, HS = w.shape[2], w.shape[3]
    T, D = mh.shape
    RW = C * S
    NR = Q * RW
    CG = S // Q
    PC = HS // CG
    NC = T // PK
    vm = pltpu.VMEM
    phases = 32
    return pl.pallas_call(
        functools.partial(chain_kernel, S, Q, X, C, D),
        out_shape=(
            jax.ShapeDtypeStruct(w.shape, BF16),
            jax.ShapeDtypeStruct((T, D), BF16),
            jax.ShapeDtypeStruct((2, 8, D), BF16),
            jax.ShapeDtypeStruct((4, DS // Q), F32),
            jax.ShapeDtypeStruct((8, 128), F32),
        ),
        in_specs=[pl.BlockSpec(memory_space=vm)] * 7,
        out_specs=(pl.BlockSpec(memory_space=vm),) * 5,
        scratch_shapes=[
            vm((T + PK, D), BF16),
            vm((PK, D), BF16),
            vm((PK, D), BF16),
            vm((2, PK, D), BF16),
            vm((PK, D), BF16),
            vm((2, S, PK, DS), BF16),
            vm((3, S, 8, DS), BF16),
            vm((2, S, PK, DS), BF16),
            vm((3, S, 8, DS), BF16),
            vm((8, 128), F32),
            vm((S, 8, 128), F32),
            vm((3, S * PK, DS), F32),
            vm((3, S, 8, DS), BF16),
            vm((3, S, 8, DS), BF16),
            vm((2, NR, DS), BF16),
            vm((2, NR, DS), BF16),
            vm((2, CG, 2, NR, PC), BF16),
            vm((2, S // 2, 2, RW, PC), BF16),
            vm((2, S // 2, 2, RW, PC), BF16),
            vm((2, S // 2, 2, RW, PC), BF16),
            vm((CG, 2, NR, PC), F32),
            vm((2, CG, 1, NR, PC), BF16),
            vm((2, S, 1, RW, PC), BF16),
            vm((2, CG, 1, NR, PC), BF16),
            vm((2, CG, 2, NR, PC), BF16),
            vm((3, NR, DS), BF16),
            vm((3, Q, RW, DS), BF16),
            vm((2 * RW, DS), F32),
            vm((2, 2, 128), F32),
            vm((2, S, 2, 128), F32),
            vm((4 * RW, DS), BF16),
            vm((2, 2, RW, PC), F32),
            vm((T, D), BF16),
            vm((T, D), BF16),
            vm((2 * PK, D), BF16),
            vm((PK, D), F32),
            vm((PK, D), F32),
            vm((PK, D), F32),
            vm((3, PK, D), F32),
            vm((2, 8, D), BF16),
            vm((4, 8, D), F32),
            vm((S, 4, DS), F32),
            vm((S, 4, DS), F32),
            vm((Q, 4, DS // Q), F32),
            vm((Q, 4, DS // Q), F32),
            pltpu.SemaphoreType.DMA((phases, S)),
            pltpu.SemaphoreType.DMA((phases, S)),
            pltpu.SemaphoreType.DMA((2 * NC + 4,)),
            pltpu.SemaphoreType.DMA((2 * NC + 4,)),
        ],
        compiler_params=pltpu.CompilerParams(
            collective_id=0, has_side_effects=True, vmem_limit_bytes=60 * 1024 * 1024
        ),
        name="expert_chain",
    )(slots, w, mh, own, ahead, cot, ng)


def pick(index, count):
    return (index[:, None] == jnp.arange(count, dtype=jnp.int32)[None, :]).astype(BF16)


def local(main_hidden, embedded, cotangent, slot_token, slot_count, route_gate, norm_gain, w):
    S = lax.axis_size("seq")
    me = lax.axis_index("seq")
    tokens_here, D = main_hidden.shape[2:]
    C = slot_token.shape[3]
    DS = D // S
    tok = slot_token[0, 0]
    live = (jnp.arange(C, dtype=jnp.int32)[None, :] < slot_count[0, 0]).astype(F32)
    weight = route_gate[0, 0] * live
    own, cot, mh = embedded[0, 0], cotangent[0, 0], main_hidden[0, 0]
    ahead = from_ahead(own[:2], "seq", 1)
    same = (tok[1][:, None] == tok[0][None, :]).astype(F32) * live[1][:, None] * live[0][None, :]
    fresh = jnp.stack([live[0], live[1] * (1.0 - jnp.max(same, axis=1))]).reshape(-1)
    flat = tok.reshape(-1)

    def lanes(*parts):
        row = jnp.concatenate(parts)
        return jnp.pad(row, (0, 128 - row.shape[0]))

    slots = jnp.stack([
        lanes(flat.astype(F32)),
        lanes(live.reshape(-1)),
        lanes(weight.reshape(-1)),
        lanes(fresh),
        lanes(weight[0], jnp.zeros((16 - C,), F32), same.reshape(-1)),
        lanes(tok[1].astype(F32)),
        lanes(live[1]),
        lanes(flat[:1].astype(F32) * 0.0),
    ])

    expert_grad, grads, slot_grads, total, asks = chain(slots, w, mh, own, ahead, cot, norm_gain, C)
    back_to = jnp.where(asks[3, :2 * C] > 0.5, asks[0, :2 * C], -1.0).astype(jnp.int32)
    put = pick(back_to, tokens_here)
    hit = jnp.sum(put.astype(F32), axis=0)
    placed = lax.dot_general(
        put, slot_grads.reshape(PK, D)[:2 * C], (((0,), (0,)), ((), ())), preferred_element_type=F32
    )
    hidden_grad = jnp.where(hit[:, None] > 0.5, placed.astype(BF16), grads)
    return (hidden_grad[None, None], expert_grad[None], total.reshape(1, 2, 2, -1))


def solution(mesh):
    return jax.shard_map(
        local,
        mesh=mesh,
        in_specs=(
            P("section", "dp", "seq", None),
            P("section", "dp", "seq", None),
            P("section", "dp", "seq", None),
            P("section", "dp", None, "seq"),
            P("section", "dp", None, "seq"),
            P("section", "dp", None, "seq"),
            P(),
            P(None, None, "seq", "dp"),
        ),
        out_specs=(
            P("section", "dp", "seq", None),
            P("section", None, None, "seq", "dp"),
            P("section", None, None, ("seq", "dp")),
        ),
        check_vma=False,
    )
```

```python
import functools

import jax
import jax.numpy as jnp
from jax import lax
from jax.experimental import pallas as pl
from jax.experimental.pallas import tpu as pltpu
from jax.sharding import PartitionSpec as P

eps_norm = 1e-06
MESH = pl.DeviceIdType.MESH
F32 = jnp.float32
BF16 = jnp.bfloat16
PK = 16


def from_behind(value, axis, steps):
    count = lax.axis_size(axis)
    pairs = [(source, (source + steps) % count) for source in range(count)]
    return lax.ppermute(value, axis, pairs)


def from_ahead(array, axis, by):
    size = lax.axis_size(axis)
    pairs = [(i, i - by) for i in range(size) if 0 <= i - by < size]
    return lax.ppermute(array, axis, pairs)


def normed(value):
    wide = value.astype(F32)
    scale = lax.rsqrt(jnp.mean(wide * wide, axis=-1, keepdims=True) + eps_norm)
    return (wide * scale, scale)


def norm_back(grad, unit, scale):
    inner = jnp.mean(grad * unit, axis=-1, keepdims=True)
    return (grad - unit * inner) * scale


def dot_nn(a, b):
    return lax.dot_general(a, b, (((1,), (0,)), ((), ())), preferred_element_type=F32)


def dot_nt(a, b):
    return lax.dot_general(a, b, (((1,), (1,)), ((), ())), preferred_element_type=F32)


def dot_tn(a, b):
    return lax.dot_general(a, b, (((0,), (0,)), ((), ())), preferred_element_type=F32)


class Wires:
    def __init__(self, send, recv):
        self.send, self.recv = send, recv
        self.phases = 0
        self.open = []
        self.singles = []

    def copy(self, src, dst, ph, slot_s, slot_r, axis, to):
        return pltpu.make_async_remote_copy(
            src_ref=src,
            dst_ref=dst,
            send_sem=self.send.at[ph, slot_s],
            recv_sem=self.recv.at[ph, slot_r],
            device_id={axis: to},
            device_id_type=MESH,
        )

    def start(self, axis, size, me, src_of, dst):
        ph = self.phases
        self.phases += 1

        def body(o, c):
            to = lax.rem(me + o, size)
            self.copy(src_of(to), dst, ph, o, me, axis, to).start()
            return c

        lax.fori_loop(1, size, body, 0)
        self.open.append((ph, axis, size, me, src_of))
        return ph

    def wait(self, ph, axis, size, me, dst_of):
        def body(o, c):
            frm = lax.rem(me + o, size)
            self.copy(dst_of(frm), dst_of(frm), ph, o, frm, axis, frm).wait_recv()
            return c

        lax.fori_loop(1, size, body, 0)

    def phase(self):
        self.phases += 1
        return self.phases - 1

    def one(self, src, dst, ph, slot_s, slot_r, axis, to):
        copy = self.copy(src, dst, ph, slot_s, slot_r, axis, to)
        copy.start()
        self.singles.append(copy)

    def drain(self):
        for copy in self.singles:
            copy.wait_send()
        for ph, axis, size, me, src_of in self.open:

            def body(o, c):
                to = lax.rem(me + o, size)
                self.copy(src_of(to), src_of(to), ph, o, me, axis, to).wait_send()
                return c

            lax.fori_loop(1, size, body, 0)


def greet(axes, sections=()):
    barrier = pltpu.get_barrier_semaphore()
    total = 0
    for axis, size, me in axes:

        def body(o, c):
            to = lax.rem(me + o, size)
            pl.semaphore_signal(barrier, inc=1, device_id={axis: to}, device_id_type=MESH)
            return c

        lax.fori_loop(1, size, body, 0)
        total += size - 1
    for to in sections:
        pl.semaphore_signal(barrier, inc=1, device_id={"section": to}, device_id_type=MESH)
        total += 1
    return lambda: pl.semaphore_wait(barrier, total)


def chain_kernel(S, Q, X, C, D, slots, w, mh, own, ahead, cot, ng, eg, hg, slr, gains, asks,
                 ext, hsend, hrow, se, sc, pka, pkb, landa, landb, meta, mland, rows, ret, rb, xr, do, gu, lg, ly, cmb, gf, da,
                 ld, act, dg, op, lo, pv, ss, ssl, od, gsv, hid, hgs, es, mx, dmx, dmu, ad, sls, gacc, gsrc, gland,
                 gown, gland2, send, recv, xsend, xrecv):
    me = lax.axis_index("seq")
    d = lax.axis_index("dp")
    sec = lax.axis_index("section")
    after, before_me = lax.rem(sec + 1, X), lax.rem(sec + X - 1, X)
    DS, HS = w.shape[2], w.shape[3]
    RW = C * S
    CG = S // Q
    PC = HS // CG
    rg, cg = me // CG, lax.rem(me, CG)
    wires = Wires(send, recv)

    def rowslice(g):
        return pl.ds(pl.multiple_of(g * RW, 32 if RW % 32 == 0 else 8), RW)

    def piece_of(ref):
        def src(to):
            return ref.at[to % CG, :, rowslice(to // CG), :]
        return src

    def seq_start(src_of, dst):
        return wires.start("seq", S, me, src_of, dst)

    def seq_wait(ph, dst_of):
        wires.wait(ph, "seq", S, me, dst_of)

    def dp_start(src_of, dst):
        return wires.start("dp", Q, d, src_of, dst)

    def dp_wait(ph, dst_of):
        wires.wait(ph, "dp", Q, d, dst_of)

    barrier_axes = (("seq", S, me), ("dp", Q, d))
    greet_all = greet(barrier_axes, (after, before_me))
    NC = mh.shape[0] // PK
    T = mh.shape[0]

    def chunk(c):
        return pl.ds(pl.multiple_of(c * PK, PK), PK)

    def hop(src, dst, slot, to):
        return pltpu.make_async_remote_copy(
            src_ref=src, dst_ref=dst, send_sem=xsend.at[slot], recv_sem=xrecv.at[slot],
            device_id={"section": to}, device_id_type=MESH,
        )

    def hid_copy(c):
        return hop(mh.at[chunk(c), :], hid.at[chunk(c), :], c, after)

    def hg_copy(c):
        return hop(hgs.at[chunk(c), :], hg.at[chunk(c), :], NC + c, before_me)

    ask_hop = hop(slots, asks, 2 * NC + 1, before_me)
    row_hop = hop(hsend, hrow, 2 * NC + 2, after)

    def each_chunk(fn, first=0, last=NC):
        def body(c, carry):
            fn(c)
            return carry

        lax.fori_loop(first, last, body, 0)

    slot_row, live_row, weight_row, fresh_row = (slots[k:k + 1, :] for k in range(4))
    lane16 = lax.broadcasted_iota(jnp.int32, (PK, 128), 1)
    line16 = lax.broadcasted_iota(jnp.int32, (PK, 128), 0)
    line1 = lax.broadcasted_iota(jnp.int32, (PK, 1), 0)

    def column(row):
        return jnp.sum(jnp.where(lane16 == line16, row, 0.0), axis=1, keepdims=True)

    def line(col, first):
        return jnp.sum(jnp.where((lane16 == line16 + first) & (line16 < C), col, 0.0), axis=0, keepdims=True)

    slot_tok, slot_live, slot_w = column(slot_row), column(live_row), column(weight_row)

    ext[0:T, :] = own[...]
    ext[T:T + PK, :] = jnp.zeros((PK, D), BF16)
    ext[T:T + 2, :] = ahead[...]
    wide = lax.broadcasted_iota(jnp.int32, (PK, T + PK), 1).astype(F32)
    for k in range(2):
        se[k] = dot_nn(jnp.where(wide == slot_tok + (k + 1.0), 1.0, 0.0).astype(BF16), ext[...]).astype(BF16)
    sc[...] = dot_nn(jnp.where(lane16.astype(F32) == slot_tok, 1.0, 0.0).astype(BF16), cot[...]).astype(BF16)

    greet_all()
    ask_hop.start()

    first_rows = line1 < C

    def dslice(b):
        return slice(b * DS, (b + 1) * DS)

    cot_w = jnp.where(first_rows, 1.0, slot_w)
    for b in range(S):
        pka[0, b] = (sc[:, dslice(b)].astype(F32) * cot_w).astype(BF16)
    ph_a = seq_start(lambda to: pka.at[0, to], landa.at[0, me])
    landa[0, me] = pka[0, me]
    e_live = jnp.where(first_rows, 1.0, slot_live)
    for b in range(S):
        both = jnp.where(first_rows, se[0, :, dslice(b)].astype(F32), se[1, :, dslice(b)].astype(F32))
        pka[1, b] = (both * e_live).astype(BF16)

    ask_hop.wait_recv()
    asked = jnp.sum(jnp.where(lane16 == line16, asks[0:1, :], 0.0), axis=1, keepdims=True)
    hsend[...] = dot_nn(jnp.where(lane16.astype(F32) == asked, 1.0, 0.0).astype(BF16), mh[...]).astype(BF16)
    row_hop.start()
    each_chunk(lambda c: hid_copy(c).start())
    ph_e = seq_start(lambda to: pka.at[1, to], landa.at[1, me])
    landa[1, me] = pka[1, me]

    def unpack(k, land, height, first):
        n = S * height
        r = lax.broadcasted_iota(jnp.int32, (n, n), 0)
        c = lax.broadcasted_iota(jnp.int32, (n, n), 1)
        perm = jnp.where(c == (r % S) * height + r // S, 1.0, 0.0).astype(BF16)
        flat = land[...].astype(F32).reshape(n, DS).astype(BF16)
        rows[k, first * S:(first + height) * S, :] = dot_nn(perm, flat)

    def rows_at(k, slot):
        return rows[k, slot * S:(slot + 1) * S, :]

    def gather_dp(k, dst):
        return dp_start(lambda to: dst.at[k, rowslice(d), :], dst.at[k, rowslice(d), :])

    def gather_dp_wait(ph, k, dst):
        dp_wait(ph, lambda frm: dst.at[k, rowslice(frm), :])

    def gate_up(k, work=None):
        far = [h for h in reversed(near)] + [0]
        for half in range(2):
            full = dot_nn(xr[k], w[k, half])
            for q in range(CG):
                cols = slice(q * PC, (q + 1) * PC)
                gf[q, half] = full[:, cols]
                gu[k, q, half] = full[:, cols].astype(BF16)

        def piece(ref, t):
            return ref.at[lax.rem(t, CG), :, rowslice(t // CG), :]

        ph = wires.phase()
        for h in far:
            z = lax.rem(zme + h, n)
            wires.one(piece(gu.at[k], at_z(h, 1 - yme)), ly.at[k, z], ph, h, h, "seq", yn)
        ph2 = wires.phase()
        for h in far:
            z = lax.rem(zme + h, n)
            wires.copy(ly.at[k, z], ly.at[k, z], ph, h, h, "seq", yn).wait_recv()
            both = piece(gf, at_z(h, yme))[...] + ly[k, z].astype(F32)
            if h == 0:
                total = both
            else:
                cmb[k, z] = both.astype(BF16)
                wires.one(cmb.at[k, z], lg.at[k, zme], ph2, h, h, "seq", at_z(h, yme))
        if work is not None:
            work()
        for h in near:
            z = lax.rem(zme + n - h, n)
            wires.copy(lg.at[k, z], lg.at[k, z], ph2, h, h, "seq", at_z(n - h, yme)).wait_recv()
            total = total + lg[k, z].astype(F32)
        return total

    def add_up(ref):
        total = ref[0].astype(F32)
        for b in range(1, ref.shape[0]):
            total = total + ref[b].astype(F32)
        return total

    def dact(k):
        full = dot_nn(do[k], w[k, 2]).astype(BF16)
        for q in range(CG):
            da[k, q, 0] = full[:, q * PC:(q + 1) * PC]
        ph = seq_start(piece_of(da.at[k]), ld.at[k, me])
        ld[k, me] = da[k, cg, :, rowslice(rg), :]
        return ph

    def dact_wait(ph, k):
        seq_wait(ph, lambda frm: ld.at[k, frm])
        return add_up(ld.at[k])[0]

    def spread_piece(ref):
        mine = ref.at[cg, :, rowslice(rg), :]
        return seq_start(lambda to: mine, mine)

    n = S // 2
    zme, yme = me // 2, lax.rem(me, 2)
    yn = me + 1 - 2 * yme
    near = sorted(range(1, n), key=lambda h: (min(h, n - h), h))

    def at_z(h, parity):
        return 2 * lax.rem(zme + h, n) + parity

    def spread(ref, work=None):
        def piece(t):
            return ref.at[lax.rem(t, CG), :, rowslice(t // CG), :]

        ph = wires.phase()
        mine = piece(me)
        for h in reversed(near):
            wires.one(mine, mine, ph, h, h, "seq", at_z(h, yme))
        wires.one(mine, mine, ph, 0, n, "seq", yn)
        for h in near:
            frm = at_z(n - h, yme)
            wires.copy(piece(frm), piece(frm), ph, h, h, "seq", frm).wait_recv()
            wires.one(piece(frm), piece(frm), ph, n + h, n + h, "seq", yn)
        if work is not None:
            work()
        for h in [0] + near:
            frm = at_z(n - h, 1 - yme)
            wires.copy(piece(frm), piece(frm), ph, n + h, n + h, "seq", yn).wait_recv()

    def spread_wait(ph, ref):
        seq_wait(ph, lambda frm: ref.at[lax.rem(frm, CG), :, rowslice(frm // CG), :])

    def reduce_dp(n, full):
        op[n] = full.astype(BF16)
        ph = dp_start(lambda to: op.at[n, rowslice(to), :], lo.at[n, d])
        lo[n, d] = op[n, rowslice(d), :]
        return ph

    def reduce_dp_wait(ph, n):
        dp_wait(ph, lambda frm: lo.at[n, frm])
        return add_up(lo.at[n])

    def drows(k):
        total = None
        for q in range(CG):
            cols = slice(q * PC, (q + 1) * PC)
            part = dot_nt(dg[k, q, 0], w[k, 0, :, cols]) + dot_nt(dg[k, q, 1], w[k, 1, :, cols])
            total = part if total is None else total + part
        return total

    laneS = lax.broadcasted_iota(jnp.int32, (S, 128), 1)
    lineS = lax.broadcasted_iota(jnp.int32, (S, 128), 0)

    def to_row(cols):
        total = jnp.zeros((1, 128), F32)
        for i, col in enumerate(cols):
            total = total + jnp.sum(jnp.where(laneS == lineS + i * S, col, 0.0), axis=0, keepdims=True)
        return total

    def to_col(row, i):
        return jnp.sum(jnp.where(laneS == lineS + i * S, row, 0.0), axis=1, keepdims=True)

    def sums_start(k, cols):
        ss[k, 0:1, :] = to_row(cols[:C])
        ss[k, 1:2, :] = to_row(cols[C:])
        ph = seq_start(lambda to: ss.at[k], ssl.at[k, me])
        ssl[k, me] = ss[k]
        return ph

    def sums_wait(ph, n):
        seq_wait(ph, lambda frm: ssl.at[n, frm])
        return add_up(ssl.at[n]) * (1.0 / D)

    def pre_grads(k, d_act):
        gate, up = gsv[k, 0], gsv[k, 1]
        sig = 1.0 / (1.0 + jnp.exp(-gate))
        dg[k, cg, 0, rowslice(rg), :] = (d_act * up * sig * (1.0 + gate * (1.0 - sig))).astype(BF16)
        dg[k, cg, 1, rowslice(rg), :] = (d_act * (gate * sig)).astype(BF16)

    def act_piece(k):
        gate, up = gsv[k, 0], gsv[k, 1]
        act[k, cg, 0, rowslice(rg), :] = (gate / (1.0 + jnp.exp(-gate)) * up).astype(BF16)

    def in_grads(k):
        for half in range(2):
            for q in range(CG):
                eg[k, half, :, q * PC:(q + 1) * PC] = dot_tn(xr[k], dg[k, q, half]).astype(BF16)

    def down_grad(k):
        for q in range(CG):
            eg[k, 2, :, q * PC:(q + 1) * PC] = dot_tn(do[k], act[k, q, 0]).astype(BF16)

    LB = 256
    NB = D // LB

    def lanes(b):
        return pl.ds(pl.multiple_of(b * LB, LB), LB)

    def sweep(fn, count):
        zero = jnp.zeros((PK, LB), F32)
        total = lax.fori_loop(0, NB, lambda b, acc: fn(lanes(b), acc), (zero,) * count)
        return [jnp.sum(t, axis=1, keepdims=True) * (1.0 / D) for t in total]

    def gain(k, at):
        return ng[k // 2, k % 2:k % 2 + 1, at]

    def collect(k, at, value, mask):
        value = value * mask
        gacc[k, :, at] += value[:8] + value[8:]

    def rows_pass_1(h_at, e_at, c_at, mask, prev_add, dm2_add):
        def squares(at, acc):
            h, e1, e2 = h_at(at), e_at(0, at), e_at(1, at)
            return acc[0] + h * h, acc[1] + e1 * e1, acc[2] + e2 * e2

        sh, se1, se2 = [lax.rsqrt(v + eps_norm) for v in sweep(squares, 3)]

        def mix(at, acc):
            m = (h_at(at) * sh) * gain(0, at) + (e_at(0, at) * se1) * gain(1, at)
            m = m.astype(BF16).astype(F32)
            if prev_add is not None:
                m = (m + prev_add(at)).astype(BF16).astype(F32)
            mx[:, at] = m
            return (acc[0] + m * m,)

        s2, = [lax.rsqrt(v + eps_norm) for v in sweep(mix, 1)]

        def top(at, acc):
            n2 = mx[:, at] * s2
            dm2 = c_at(at)
            if dm2_add is not None:
                dm2 = dm2 + dm2_add(at)
            collect(2, at, dm2 * n2, mask)
            collect(3, at, dm2 * (e_at(1, at) * se2), mask)
            u = dm2 * gain(2, at)
            dmx[:, at] = u
            return (acc[0] + u * n2,)

        inner, = sweep(top, 1)

        def middle(at, acc):
            dmx[:, at] = (dmx[:, at] - (mx[:, at] * s2) * inner) * s2
            return acc

        sweep(middle, 0)
        return sh, se1

    def rows_pass_2(h_at, e_at, mask, sh, se1, dm1_add, store):
        def low(at, acc):
            dm1 = dmx[:, at]
            if dm1_add is not None:
                dm1 = dm1 + dm1_add(at)
            n1 = h_at(at) * sh
            if mask is not None:
                collect(0, at, dm1 * n1, mask)
                collect(1, at, dm1 * (e_at(0, at) * se1), mask)
            u = dm1 * gain(0, at)
            dmu[:, at] = u
            return (acc[0] + u * n1,)

        inner, = sweep(low, 1)

        def last(at, acc):
            store(at, (dmu[:, at] - (h_at(at) * sh) * inner) * sh)
            return acc

        sweep(last, 0)

    def bulk_chunk(c):
        hid_copy(c).wait_recv()
        r = lax.broadcasted_iota(jnp.int32, (2 * PK, 2 * PK), 0)
        k = lax.broadcasted_iota(jnp.int32, (2 * PK, 2 * PK), 1)
        shift = jnp.where(k == r % PK + 1 + r // PK, 1.0, 0.0).astype(BF16)
        es[...] = dot_nn(shift, ext[pl.ds(pl.multiple_of(c * PK, PK), 2 * PK), :]).astype(BF16)
        place = (line16 + c * PK).astype(F32)
        hit = jnp.sum(jnp.where(place == slot_row, live_row, 0.0), axis=1, keepdims=True)
        mask = jnp.where(hit > 0.5, 0.0, 1.0)

        def h_at(at):
            return hid[chunk(c), at].astype(F32)

        def e_at(k, at):
            return es[k * PK:(k + 1) * PK, at].astype(F32)

        sh, se1 = rows_pass_1(h_at, e_at, lambda at: cot[chunk(c), at].astype(F32), mask, None, None)

        def store(at, value):
            hgs[chunk(c), at] = value.astype(BF16)

        rows_pass_2(h_at, e_at, mask, sh, se1, None, store)
        hg_copy(c).start()

    def bulk(first, last):
        each_chunk(bulk_chunk, first, last)

    gacc[...] = jnp.zeros_like(gacc)

    def slot_h(at):
        return hrow[:, at].astype(F32)

    def slot_e(k, at):
        return se[k, :, at].astype(F32)

    slot_mask = column(fresh_row)
    same_tok = jnp.where(slot_tok == slot_row, live_row, 0.0)
    prev_sel = jnp.where(lane16 < C, same_tok, 0.0)
    prev_w = jnp.sum(prev_sel * weight_row, axis=1, keepdims=True)
    dm2_tok = jnp.where(slot_tok == slots[5:6, :], slots[6:7, :], 0.0)
    dm2_sel = jnp.where(lane16 < C, dm2_tok, 0.0)

    def widen(n, sel, k, scale_by):
        for b in range(S):
            part = dot_nn(sel[:, :8].astype(BF16), ret[k, b])
            if scale_by is not None:
                part = part * scale_by
            ad[n, :, dslice(b)] = part

    def send_back(k):
        r = lax.broadcasted_iota(jnp.int32, (S * 8, RW), 0)
        c = lax.broadcasted_iota(jnp.int32, (S * 8, RW), 1)
        perm = jnp.where(c == (r % 8) * S + r // 8, 1.0, 0.0).astype(BF16)
        rb[k] = dot_nn(perm, od[k * RW:(k + 1) * RW, :]).reshape(S, 8, DS).astype(BF16)
        ph = seq_start(lambda to: rb.at[k, to], ret.at[k, me])
        ret[k, me] = rb[k, me]
        return ph

    seq_wait(ph_a, lambda frm: landa.at[0, frm])
    unpack(0, landa.at[0], PK, 0)
    do[1, rowslice(d), :] = rows[0, RW:2 * RW, :].astype(BF16)
    ph_d2 = gather_dp(1, do)

    row_hop.wait_recv()

    def slot_squares(at, acc):
        h, e1, e2 = slot_h(at), slot_e(0, at), slot_e(1, at)
        return acc[0] + h * h, acc[1] + e1 * e1, acc[2] + e2 * e2

    sh, se1, se2 = [lax.rsqrt(v + eps_norm) for v in sweep(slot_squares, 3)]

    def slot_mix(at, acc):
        m = (slot_h(at) * sh) * gain(0, at) + (slot_e(0, at) * se1) * gain(1, at)
        mx[:, at] = m.astype(BF16).astype(F32) * slot_live
        return acc

    sweep(slot_mix, 0)
    for b in range(S):
        part = mx[:, dslice(b)]
        pkb[0, b] = part[:8].astype(BF16)
        pkb[1, b] = part[8:].astype(BF16)
        pkb[2, b] = hrow[:, dslice(b)].astype(F32)[:8].astype(BF16)
    ph_b = seq_start(lambda to: pkb.at[0, to], landb.at[0, me])
    se2_t2 = pltpu.roll(jnp.broadcast_to(se2, (PK, 128)), PK - C, 0)
    top = slots[4:5, :] + line(se2_t2, 8) + line(sh, 52) + line(se1, 58)
    meta[...] = jnp.broadcast_to(top, (8, 128)) * jnp.where(line16[:8] == 0, 1.0, 0.0)
    ph_m = seq_start(lambda to: meta, mland.at[me])
    mland[me] = meta[...]
    ph_b1 = seq_start(lambda to: pkb.at[1, to], landb.at[1, me])
    ph_b2 = seq_start(lambda to: pkb.at[2, to], landb.at[2, me])
    for k in range(3):
        landb[k, me] = pkb[k, me]
    gather_dp_wait(ph_d2, 1, do)
    seq_wait(ph_b, lambda frm: landb.at[0, frm])
    unpack(1, landb.at[0], 8, 0)
    xr[0, rowslice(d), :] = rows[1, 0:RW, :].astype(BF16)
    ph_x = gather_dp(0, xr)
    ph_da2 = dact(1)
    seq_wait(ph_b1, lambda frm: landb.at[1, frm])
    unpack(1, landb.at[1], 8, 8)
    seq_wait(ph_e, lambda frm: landa.at[1, frm])
    unpack(2, landa.at[1], PK, 0)
    gather_dp_wait(ph_x, 0, xr)
    gsv[0] = gate_up(0, lambda: bulk(0, NC // 8))
    act_piece(0)
    spread(act.at[0], lambda: bulk(NC // 8, 2 * NC // 8))
    out = None
    for q in range(CG):
        part = dot_nt(act[0, q, 0], w[0, 2, :, q * PC:(q + 1) * PC])
        out = part if out is None else out + part
    ph = reduce_dp(0, out)
    bulk(2 * NC // 8, 3 * NC // 8)
    seq_wait(ph_m, lambda frm: mland.at[frm])
    facts = jnp.sum(mland[...], axis=1)

    def fact(k):
        return facts[:, k:k + 1]

    def ov(j, i):
        return fact(16 + j * C + i)

    out = reduce_dp_wait(ph, 0)
    od[0:RW, :] = out.astype(BF16)
    cols = []
    for i in range(C):
        before = rows_at(1, i) + fact(i) * out[i * S:(i + 1) * S]
        before = before.astype(BF16).astype(F32)
        pv[i * S:(i + 1) * S, :] = before
        cols.append(jnp.sum(before * before, axis=1, keepdims=True))
    for j in range(C):
        before = rows_at(1, C + j)
        for i in range(C):
            before = before + (ov(j, i) * fact(i)) * out[i * S:(i + 1) * S]
        before = before.astype(BF16).astype(F32)
        pv[(C + j) * S:(C + j + 1) * S, :] = before
        cols.append(jnp.sum(before * before, axis=1, keepdims=True))
    ph = sums_start(0, cols)
    bulk(3 * NC // 8, 4 * NC // 8)
    gain_h, gain_e = jnp.zeros((1, DS), F32), jnp.zeros((1, DS), F32)
    for b in range(S):
        gain_h = gain_h + jnp.where(me == b, ng[1, 0:1, dslice(b)], 0.0)
        gain_e = gain_e + jnp.where(me == b, ng[1, 1:2, dslice(b)], 0.0)
    scale = lax.rsqrt(sums_wait(ph, 0) + eps_norm)

    for j in range(C):
        unit = pv[(C + j) * S:(C + j + 1) * S, :] * to_col(scale[1:2], j)
        mixed = unit * gain_h + (rows_at(2, C + j) * fact(8 + j)) * gain_e
        od[3 * RW + j * S:3 * RW + (j + 1) * S, :] = mixed.astype(BF16)
    xr[1, rowslice(d), :] = od[3 * RW:4 * RW, :]
    ph = gather_dp(1, xr)
    ph_r0 = send_back(0)
    gather_dp_wait(ph, 1, xr)
    gsv[1] = gate_up(1, lambda: bulk(4 * NC // 8, 5 * NC // 8))
    d_act = dact_wait(ph_da2, 1)
    pre_grads(1, d_act)
    act_piece(1)
    spread(dg.at[1])
    ph = reduce_dp(1, drows(1))
    ph_a2 = spread_piece(act.at[1])
    in_grads(1)
    bulk(5 * NC // 8, 6 * NC // 8)
    back = reduce_dp_wait(ph, 1)
    od[RW:2 * RW, :] = back.astype(BF16)
    cols, keep_u, keep_n = [], [], []
    for i in range(C):
        top = rows_at(0, i)
        for j in range(C):
            top = top + ov(j, i) * back[j * S:(j + 1) * S]
        u = top * gain_h
        unit = pv[i * S:(i + 1) * S, :] * to_col(scale[0:1], i)
        keep_u.append(u)
        keep_n.append(unit)
        cols.append(jnp.sum(u * unit, axis=1, keepdims=True))
    ph = sums_start(1, cols)

    bulk(6 * NC // 8, 7 * NC // 8)
    inner = sums_wait(ph, 1)

    for i in range(C):
        back = (keep_u[i] - keep_n[i] * to_col(inner[0:1], i)) * to_col(scale[0:1], i)
        od[3 * RW + i * S:3 * RW + (i + 1) * S, :] = (back * fact(i)).astype(BF16)
    do[0, rowslice(d), :] = od[3 * RW:4 * RW, :]
    ph = gather_dp(0, do)
    ph_r1 = send_back(1)
    bulk(7 * NC // 8, NC)
    gather_dp_wait(ph, 0, do)
    ph = dact(0)
    seq_wait(ph_r0, lambda frm: ret.at[0, frm])
    seq_wait(ph_r1, lambda frm: ret.at[1, frm])
    widen(0, prev_sel, 0, prev_w)
    widen(1, dm2_sel, 1, None)
    slot_sh, slot_se1 = rows_pass_1(
        slot_h, slot_e, lambda at: sc[:, at].astype(F32), slot_mask, lambda at: ad[0, :, at], lambda at: ad[1, :, at]
    )

    def early(at, acc):
        collect(0, at, dmx[:, at] * (slot_h(at) * slot_sh), slot_mask)
        collect(1, at, dmx[:, at] * (slot_e(0, at) * slot_se1), slot_mask)
        return acc

    sweep(early, 0)

    def early_store(at, value):
        sls[1, :, at] = value[8:].astype(BF16)

    back_early = hop(sls.at[1], slr.at[1], 2 * NC + 3, before_me)
    back_rows = hop(sls.at[0], slr.at[0], 2 * NC, before_me)
    d_act = dact_wait(ph, 0)
    pre_grads(0, d_act)
    spread(dg.at[0])
    for b in range(S):
        gsrc[b] = jnp.sum(gacc[:, :, dslice(b)], axis=1)
    ph_g = seq_start(lambda to: gsrc.at[to], gland.at[me])
    gland[me] = gsrc[me]
    ph = reduce_dp(2, drows(0))
    rows_pass_2(slot_h, slot_e, None, slot_sh, slot_se1, None, early_store)
    back_early.start()
    spread_wait(ph_a2, act.at[1])
    down_grad(1)
    down_grad(0)
    in_grads(0)
    back = reduce_dp_wait(ph, 2)
    od[2 * RW:3 * RW, :] = back.astype(BF16)
    ph_r2 = send_back(2)

    seq_wait(ph_b2, lambda frm: landb.at[2, frm])
    unpack(1, landb.at[2], 8, 0)
    late_h = jnp.zeros((S, DS), F32)
    late_e = jnp.zeros((S, DS), F32)
    for i in range(C):
        part = back[i * S:(i + 1) * S]
        late_h = late_h + part * (rows_at(1, i) * fact(52 + i))
        late_e = late_e + part * (rows_at(2, i) * fact(58 + i))
    seq_wait(ph_g, lambda frm: gland.at[frm])
    value = add_up(gland)
    late = jnp.concatenate(
        [jnp.sum(late_h, axis=0, keepdims=True), jnp.sum(late_e, axis=0, keepdims=True), jnp.zeros((2, DS), F32)], 0
    )
    value = value + late
    QS = DS // Q
    for q in range(Q):
        gown[q] = value[:, q * QS:(q + 1) * QS]
    ph_q = dp_start(lambda to: gown.at[to], gland2.at[d])
    gland2[d] = gown[d]

    seq_wait(ph_r2, lambda frm: ret.at[2, frm])
    widen(2, prev_sel, 2, None)

    def slot_store(at, value):
        sls[0, :, at] = value[:8].astype(BF16)

    rows_pass_2(slot_h, slot_e, None, slot_sh, slot_se1, lambda at: ad[2, :, at], slot_store)
    back_rows.start()
    dp_wait(ph_q, lambda frm: gland2.at[frm])
    gains[...] = add_up(gland2)

    def finish(c):
        hid_copy(c).wait_send()
        hg_copy(c).wait_send()
        hg_copy(c).wait_recv()

    each_chunk(finish)
    ask_hop.wait_send()
    row_hop.wait_send()
    back_rows.wait()
    back_early.wait()
    wires.drain()


def chain(slots, w, mh, own, ahead, cot, ng, C):
    S, Q, X = lax.axis_size("seq"), lax.axis_size("dp"), lax.axis_size("section")
    DS, HS = w.shape[2], w.shape[3]
    T, D = mh.shape
    RW = C * S
    NR = Q * RW
    CG = S // Q
    PC = HS // CG
    NC = T // PK
    vm = pltpu.VMEM
    phases = 32
    return pl.pallas_call(
        functools.partial(chain_kernel, S, Q, X, C, D),
        out_shape=(
            jax.ShapeDtypeStruct(w.shape, BF16),
            jax.ShapeDtypeStruct((T, D), BF16),
            jax.ShapeDtypeStruct((2, 8, D), BF16),
            jax.ShapeDtypeStruct((4, DS // Q), F32),
            jax.ShapeDtypeStruct((8, 128), F32),
        ),
        in_specs=[pl.BlockSpec(memory_space=vm)] * 7,
        out_specs=(pl.BlockSpec(memory_space=vm),) * 5,
        scratch_shapes=[
            vm((T + PK, D), BF16),
            vm((PK, D), BF16),
            vm((PK, D), BF16),
            vm((2, PK, D), BF16),
            vm((PK, D), BF16),
            vm((2, S, PK, DS), BF16),
            vm((3, S, 8, DS), BF16),
            vm((2, S, PK, DS), BF16),
            vm((3, S, 8, DS), BF16),
            vm((8, 128), F32),
            vm((S, 8, 128), F32),
            vm((3, S * PK, DS), F32),
            vm((3, S, 8, DS), BF16),
            vm((3, S, 8, DS), BF16),
            vm((2, NR, DS), BF16),
            vm((2, NR, DS), BF16),
            vm((2, CG, 2, NR, PC), BF16),
            vm((2, S // 2, 2, RW, PC), BF16),
            vm((2, S // 2, 2, RW, PC), BF16),
            vm((2, S // 2, 2, RW, PC), BF16),
            vm((CG, 2, NR, PC), F32),
            vm((2, CG, 1, NR, PC), BF16),
            vm((2, S, 1, RW, PC), BF16),
            vm((2, CG, 1, NR, PC), BF16),
            vm((2, CG, 2, NR, PC), BF16),
            vm((3, NR, DS), BF16),
            vm((3, Q, RW, DS), BF16),
            vm((2 * RW, DS), F32),
            vm((2, 2, 128), F32),
            vm((2, S, 2, 128), F32),
            vm((4 * RW, DS), BF16),
            vm((2, 2, RW, PC), F32),
            vm((T, D), BF16),
            vm((T, D), BF16),
            vm((2 * PK, D), BF16),
            vm((PK, D), F32),
            vm((PK, D), F32),
            vm((PK, D), F32),
            vm((3, PK, D), F32),
            vm((2, 8, D), BF16),
            vm((4, 8, D), F32),
            vm((S, 4, DS), F32),
            vm((S, 4, DS), F32),
            vm((Q, 4, DS // Q), F32),
            vm((Q, 4, DS // Q), F32),
            pltpu.SemaphoreType.DMA((phases, S)),
            pltpu.SemaphoreType.DMA((phases, S)),
            pltpu.SemaphoreType.DMA((2 * NC + 4,)),
            pltpu.SemaphoreType.DMA((2 * NC + 4,)),
        ],
        compiler_params=pltpu.CompilerParams(
            collective_id=0, has_side_effects=True, vmem_limit_bytes=60 * 1024 * 1024
        ),
        name="expert_chain",
    )(slots, w, mh, own, ahead, cot, ng)


def pick(index, count):
    return (index[:, None] == jnp.arange(count, dtype=jnp.int32)[None, :]).astype(BF16)


def local(main_hidden, embedded, cotangent, slot_token, slot_count, route_gate, norm_gain, w):
    S = lax.axis_size("seq")
    me = lax.axis_index("seq")
    tokens_here, D = main_hidden.shape[2:]
    C = slot_token.shape[3]
    DS = D // S
    tok = slot_token[0, 0]
    live = (jnp.arange(C, dtype=jnp.int32)[None, :] < slot_count[0, 0]).astype(F32)
    weight = route_gate[0, 0] * live
    own, cot, mh = embedded[0, 0], cotangent[0, 0], main_hidden[0, 0]
    ahead = from_ahead(own[:2], "seq", 1)
    same = (tok[1][:, None] == tok[0][None, :]).astype(F32) * live[1][:, None] * live[0][None, :]
    fresh = jnp.stack([live[0], live[1] * (1.0 - jnp.max(same, axis=1))]).reshape(-1)
    flat = tok.reshape(-1)

    def lanes(*parts):
        row = jnp.concatenate(parts)
        return jnp.pad(row, (0, 128 - row.shape[0]))

    slots = jnp.stack([
        lanes(flat.astype(F32)),
        lanes(live.reshape(-1)),
        lanes(weight.reshape(-1)),
        lanes(fresh),
        lanes(weight[0], jnp.zeros((16 - C,), F32), same.reshape(-1)),
        lanes(tok[1].astype(F32)),
        lanes(live[1]),
        lanes(flat[:1].astype(F32) * 0.0),
    ])

    expert_grad, grads, slot_grads, total, asks = chain(slots, w, mh, own, ahead, cot, norm_gain, C)
    back_to = jnp.where(asks[3, :2 * C] > 0.5, asks[0, :2 * C], -1.0).astype(jnp.int32)
    put = pick(back_to, tokens_here)
    hit = jnp.sum(put.astype(F32), axis=0)
    placed = lax.dot_general(
        put, slot_grads.reshape(PK, D)[:2 * C], (((0,), (0,)), ((), ())), preferred_element_type=F32
    )
    hidden_grad = jnp.where(hit[:, None] > 0.5, placed.astype(BF16), grads)
    return (hidden_grad[None, None], expert_grad[None], total.reshape(1, 2, 2, -1))


def solution(mesh):
    return jax.shard_map(
        local,
        mesh=mesh,
        in_specs=(
            P("section", "dp", "seq", None),
            P("section", "dp", "seq", None),
            P("section", "dp", "seq", None),
            P("section", "dp", None, "seq"),
            P("section", "dp", None, "seq"),
            P("section", "dp", None, "seq"),
            P(),
            P(None, None, "seq", "dp"),
        ),
        out_specs=(
            P("section", "dp", "seq", None),
            P("section", None, None, "seq", "dp"),
            P("section", None, None, ("seq", "dp")),
        ),
        check_vma=False,
    )
```
